32 devices in a mesh: dp: 16 (over z, y, x), tensor: 2 (over core).
Axes of the slice: x: 2, y: 2, z: 4, core: 2. Of those that a mesh axis runs over, the one named last changes fastest.
Arguments:
- tokens: bfloat16 [16, 512, 384], P('dp'), may hold values from -6 to 6
- lengths: int32 [16], replicated, may hold values from 1 to 512, 5120 in all
- dealing: int32 [16], replicated, may hold values from 0 to 15, each once
- bucket_table: int32 [1023], replicated, may hold values from 0 to 511, as said below
- relative: bfloat16 [512, 384], replicated, may hold values from -6 to 6
- w_query: bfloat16 [384, 384], P(None, 'tensor'), may hold values from -0.3125 to 0.3125
- b_query: bfloat16 [384], P('tensor'), may hold values from -3 to 3
- w_key: bfloat16 [384, 384], P(None, 'tensor'), may hold values from -0.3125 to 0.3125
- b_key: bfloat16 [384], P('tensor'), may hold values from -3 to 3
- w_value: bfloat16 [384, 384], P(None, 'tensor'), may hold values from -0.3125 to 0.3125
- b_value: bfloat16 [384], P('tensor'), may hold values from -3 to 3
- w_out: bfloat16 [384, 384], P('tensor'), may hold values from -3 to 3
- b_out: bfloat16 [384], replicated, may hold values from -3 to 3
- attn_gain: bfloat16 [384], replicated, may hold values from 0.25 to 1.75
- attn_shift: bfloat16 [384], replicated, may hold values from -3 to 3
- w_up: bfloat16 [384, 1536], P(None, 'tensor'), may hold values from -0.3125 to 0.3125
- b_up: bfloat16 [1536], P('tensor'), may hold values from -3 to 3
- w_down: bfloat16 [1536, 384], P('tensor'), may hold values from -0.21875 to 0.21875
- b_down: bfloat16 [384], replicated, may hold values from -3 to 3
- ffn_gain: bfloat16 [384], replicated, may hold values from 0.25 to 1.75
- ffn_shift: bfloat16 [384], replicated, may hold values from -3 to 3
- cotangent: bfloat16 [16, 512, 384], P('dp'), may hold values from -6 to 6
Outputs:
- y_out: bfloat16 [16, 512, 384], P('dp')
- grad_tokens: bfloat16 [16, 512, 384], P('dp')
- grad_relative_embedding: float32 [512, 384], replicated
- grad_w_query: float32 [384, 384], P(None, 'tensor')
- grad_b_query: float32 [384], P('tensor')
- grad_w_key: float32 [384, 384], P(None, 'tensor')
- grad_b_key: float32 [384], P('tensor')
- grad_w_value: float32 [384, 384], P(None, 'tensor')
- grad_b_value: float32 [384], P('tensor')
- grad_w_out: float32 [384, 384], P('tensor')
- grad_b_out: float32 [384], replicated
- grad_attn_gain: float32 [384], replicated
- grad_attn_shift: float32 [384], replicated
- grad_w_up: float32 [384, 1536], P(None, 'tensor')
- grad_b_up: float32 [1536], P('tensor')
- grad_w_down: float32 [1536, 384], P('tensor')
- grad_b_down: float32 [384], replicated
- grad_ffn_gain: float32 [384], replicated
- grad_ffn_shift: float32 [384], replicated
The draws below stay inside these ranges and needn't reach their ends.
Inputs may be any that keep to these rules, and one draw needn't show every extreme that they name: Each of 0 to 15 appears once; slot k of the dealt order holds initial sequence dealing[k], and dp index g holds slots g * 1 to (g + 1) - 1. `bucket_table`: nondecreasing along its entries; entry a - b + 511 is the bucket of position a relative to position b.
All inputs are finite; a program needn't handle non-finite values.
Results may differ from the reference program's by a relative error of at most 0.024.
Values may be sent and summed in bfloat16 or wider, within the bound.
No kernel may reach another device: no remote copies, remote signals or barrier semaphores. Data moves between devices by JAX's collectives and lax.ppermute only.
A program may use at most 128 MiB of HBM per device.

```python
import math
import jax
import jax.numpy as jnp
import numpy as np
from jax import lax

D = 384
H = 6
FF = 1536
SPAN = 256
HEAD_DIM = 64
BUCKETS = 512
MAXLEN = 512
SEQS = 16


def draw_bucket_table(key, part):
    entries = 2 * MAXLEN - 1
    drawn = jax.random.randint(key, (entries,), 0, 2 * SPAN, dtype=jnp.int32)
    places = jnp.arange(entries, dtype=jnp.int32)
    drawn = jnp.where(places == 0, 0, drawn)
    drawn = jnp.where(places == entries - 1, 2 * SPAN - 1, drawn)
    return jnp.sort(drawn).astype(jnp.int32)


def levels(stream_key, extent, cuts, low, top_value):
    level = 1.0
    for dim, parts in cuts:
        steps = jax.random.uniform(jax.random.fold_in(jax.random.fold_in(stream_key, 6), dim), (parts,), jnp.float32, low / len(cuts), top_value / len(cuts))
        level = level * jnp.repeat(jnp.exp(steps), extent[dim] // parts).reshape((-1,) + (1,) * (len(extent) - 1 - dim))
    return level


def profile(number_of, total, limit, lean):
    weights = [(1 << 20) // math.isqrt(rank ** lean) + 1 for rank in range(2, number_of + 1)]
    rest, holding = total - limit - (number_of - 1), [1] * (number_of - 1)
    while rest > 0:
        free = [i for i in range(number_of - 1) if holding[i] < limit]
        mass, left = sum([weights[i] for i in free]), rest
        for i in free:
            addition = min(limit - holding[i], max(1, left * weights[i] // mass), rest)
            holding[i] = holding[i] + addition
            rest = rest - addition
    return np.array([limit] + holding)


def uneven_parts(stream_key, number_of, total, reach, skew):
    if number_of == 2:
        one = jax.random.randint(stream_key, (), max(1, total - reach), min(reach, total - 1) + 1)
        return jnp.stack([one, total - one])
    tallies = jnp.asarray(profile(number_of, total, reach, skew), jnp.int32)
    couples = (number_of - 1) // 2
    giver, receiver = tallies[1:1 + 2 * couples:2], tallies[2:2 + 2 * couples:2]
    room = jnp.minimum(giver - 1, reach - receiver)
    moved = jax.random.randint(jax.random.fold_in(stream_key, 1), (couples,), 0, 1 << 20) % (room + 1)
    tallies = tallies.at[1:1 + 2 * couples:2].set(giver - moved).at[2:2 + 2 * couples:2].set(receiver + moved)
    return tallies[jax.random.permutation(jax.random.fold_in(stream_key, 2), number_of)]


def scatter_about(stream_key, extent, width, limit, pieces=(), kind=jnp.bfloat16):
    array = jax.random.normal(stream_key, extent, jnp.float32) * width
    if len(pieces) > 0:
        array = levels(stream_key, extent, pieces, -0.22, 0.18) * array
    return jnp.clip(array, min=-limit, max=limit).astype(kind)


def setup_inputs(seed: int = 0) -> dict:
    key_list = jax.random.split(jax.random.key(seed), 23)
    return {
        "tokens": scatter_about(key_list[0], (SEQS, MAXLEN, D), 1.0, 6.0, ((0, 16),)),
        "lengths": uneven_parts(key_list[1], SEQS, SEQS * MAXLEN * 5 // 8, MAXLEN, 2).astype(jnp.int32),
        "dealing": jax.random.permutation(key_list[2], SEQS).astype(jnp.int32),
        "bucket_table": draw_bucket_table(jax.random.fold_in(key_list[22], 71), 0),
        "relative": scatter_about(key_list[4], (BUCKETS, D), 1.0, 6.0),
        "w_query": scatter_about(key_list[5], (D, D), D ** -0.5, 0.3125, ((1, 2),)),
        "b_query": scatter_about(key_list[6], (D,), 0.5, 3.0, ((0, 2),)),
        "w_key": scatter_about(key_list[7], (D, D), D ** -0.5, 0.3125, ((1, 2),)),
        "b_key": scatter_about(key_list[8], (D,), 0.5, 3.0, ((0, 2),)),
        "w_value": scatter_about(key_list[9], (D, D), D ** -0.5, 0.3125, ((1, 2),)),
        "b_value": scatter_about(key_list[10], (D,), 0.5, 3.0, ((0, 2),)),
        "w_out": scatter_about(key_list[11], (D, D), (max(1, 16 * D // (3 * MAXLEN))) ** -0.5, 3.0, ((0, 2),)),
        "b_out": scatter_about(key_list[12], (D,), 0.5, 3.0),
        "attn_gain": jnp.clip(1.0 + 0.15 * jax.random.normal(key_list[13], (D,), jnp.float32), 0.25, 1.75).astype(jnp.bfloat16),
        "attn_shift": scatter_about(key_list[14], (D,), 0.5, 3.0),
        "w_up": scatter_about(key_list[15], (D, FF), D ** -0.5, 0.3125, ((1, 2),)),
        "b_up": scatter_about(key_list[16], (FF,), 0.5, 3.0, ((0, 2),)),
        "w_down": scatter_about(key_list[17], (FF, D), (FF // 2) ** -0.5, 0.21875, ((0, 2),)),
        "b_down": scatter_about(key_list[18], (D,), 0.5, 3.0),
        "ffn_gain": jnp.clip(1.0 + 0.15 * jax.random.normal(key_list[19], (D,), jnp.float32), 0.25, 1.75).astype(jnp.bfloat16),
        "ffn_shift": scatter_about(key_list[20], (D,), 0.5, 3.0),
        "cotangent": scatter_about(key_list[21], (SEQS, MAXLEN, D), 1.0, 6.0, ((0, 16),)),
    }


EPSILON = 1e-07
PRECISION_FULL = lax.Precision.HIGHEST

@jax.custom_vjp
def low(v):
    return lax.optimization_barrier(v.astype(jnp.bfloat16)).astype(jnp.float32)

@jax.custom_vjp
def lowered_backward(v):
    return v

def low_keep(v):
    return (low(v), None)

def low_pass(kept, grad):
    return (grad,)

def back_keep(v):
    return (v, None)

def back_low(kept, grad):
    return (low(grad),)
low.defvjp(low_keep, low_pass)
lowered_backward.defvjp(back_keep, back_low)

def matmul(left, right):
    return jnp.dot(left, right, preferred_element_type=jnp.float32, precision=PRECISION_FULL)

def norm_rows(values, norm_gain, norm_shift):
    center = values - lax.optimization_barrier(jnp.mean(values, axis=-1, keepdims=True))
    spread = lax.optimization_barrier(jnp.mean(center * center, axis=-1, keepdims=True))
    return center * lax.rsqrt(spread + EPSILON) * norm_gain + norm_shift

def attend(queries, key_rows, value_rows, length_now, pos_query, position_key, bucket_table):
    seq_rows, head_count, head_dim = queries.shape
    block_rows = min(512, seq_rows)
    score_scale = 1.0 / math.sqrt(3.0 * head_dim)
    key_ids = jnp.arange(seq_rows, dtype=jnp.int32)
    key_valid = key_ids < length_now
    key_table = lowered_backward(jnp.einsum('jhd,bhd->hjb', key_rows, pos_query, precision=PRECISION_FULL))

    def one_block(first_row):
        query_tile_block = lax.dynamic_slice_in_dim(queries, first_row, block_rows, 0)
        row_ids = first_row + jnp.arange(block_rows, dtype=jnp.int32)
        bucket_ids = jnp.take(bucket_table, row_ids[:, None] - key_ids[None, :] + (seq_rows - 1))
        reverse_ids = jnp.take(bucket_table, key_ids[None, :] - row_ids[:, None] + (seq_rows - 1))
        query_lookup = lowered_backward(jnp.einsum('xrs,ers->rxe', query_tile_block, position_key, precision=PRECISION_FULL))
        wide_ids = jnp.broadcast_to(bucket_ids[None], (head_count, block_rows, seq_rows))
        to_pos = jnp.take_along_axis(query_lookup, wide_ids, axis=2)
        turned_ids = jnp.broadcast_to(jnp.transpose(reverse_ids)[None], (head_count, seq_rows, block_rows))
        from_pos = jnp.transpose(jnp.take_along_axis(key_table, turned_ids, axis=2), (0, 2, 1))
        content = jnp.einsum('ihd,jhd->hij', query_tile_block, key_rows, precision=PRECISION_FULL)
        scores = jnp.where(key_valid[None, None, :], lowered_backward((content + to_pos + from_pos) * score_scale), -1e+30)
        row_max = lax.optimization_barrier(jnp.max(scores, axis=2, keepdims=True))
        weights = jnp.exp(scores - row_max)
        probs = weights / lax.optimization_barrier(jnp.sum(weights, axis=2, keepdims=True))
        row_valid = row_ids < length_now
        probs = low(jnp.where(row_valid[None, :, None], probs, 0.0))
        return jnp.einsum('hij,jhd->ihd', probs, value_rows, precision=PRECISION_FULL)
    first_rows = jnp.arange(0, seq_rows, block_rows, dtype=jnp.int32)
    blocks = lax.map(jax.checkpoint(one_block), first_rows)
    return blocks.reshape(seq_rows, head_count, head_dim)

def layer(params, block_tokens, block_lengths, bucket_table):
    relative, w_query, b_query, w_key, b_key, w_value, b_value, w_out, b_out, attn_gain, attn_shift, w_up, b_up, w_down, b_down, ffn_gain, ffn_shift = params
    count, seq_rows, width_now = block_tokens.shape
    flat_rows = block_tokens.reshape(count * seq_rows, width_now)

    def project(weight, bias):
        return low(lowered_backward(matmul(flat_rows, weight) + bias)).reshape(count, seq_rows, H, HEAD_DIM)
    queries = project(w_query, b_query)
    key_rows = project(w_key, b_key)
    value_rows = project(w_value, b_value)
    pos_query = low(matmul(relative, w_query) + b_query).reshape(BUCKETS, H, HEAD_DIM)
    position_key = low(matmul(relative, w_key) + b_key).reshape(BUCKETS, H, HEAD_DIM)

    def one_sequence(seq_item):
        return attend(seq_item[0], seq_item[1], seq_item[2], seq_item[3], pos_query, position_key, bucket_table)
    contexts = lax.map(one_sequence, (queries, key_rows, value_rows, block_lengths))
    context = low(lowered_backward(contexts.reshape(count * seq_rows, width_now)))
    attn = lowered_backward(matmul(context, w_out) + b_out)
    hidden = norm_rows(flat_rows + attn, attn_gain, attn_shift)
    up_sum = lowered_backward(matmul(low(hidden), w_up) + b_up)
    activated = low(jax.nn.gelu(up_sum, approximate=False))
    down_sum = lowered_backward(matmul(activated, w_down) + b_down)
    return norm_rows(hidden + down_sum, ffn_gain, ffn_shift).reshape(count, seq_rows, width_now)

def reference(tokens, lengths, dealing, bucket_table, relative, w_query, b_query, w_key, b_key, w_value, b_value, w_out, b_out, attn_gain, attn_shift, w_up, b_up, w_down, b_down, ffn_gain, ffn_shift, cotangent):
    params = tuple((item.astype(jnp.float32) for item in (relative, w_query, b_query, w_key, b_key, w_value, b_value, w_out, b_out, attn_gain, attn_shift, w_up, b_up, w_down, b_down, ffn_gain, ffn_shift)))
    group_size = math.gcd(SEQS, max(1, 4096 // MAXLEN))
    count = SEQS // group_size
    dealt = tokens[dealing].astype(jnp.float32).reshape(count, group_size, MAXLEN, D)
    dealt_lengths = lengths[dealing]
    row_valid = (jnp.arange(MAXLEN, dtype=jnp.int32)[None, :] < dealt_lengths[:, None]).astype(jnp.float32)
    upstream = (cotangent.astype(jnp.float32) * row_valid[:, :, None]).reshape(count, group_size, MAXLEN, D)

    def step(totals, seq_item):
        block_tokens, block_lengths, block_upstream = seq_item

        def forward(weights, inputs):
            return layer(weights, inputs, block_lengths, bucket_table)
        result, pull = jax.vjp(forward, params, block_tokens)
        grad_params, grad_inputs = pull(block_upstream)
        totals = jax.tree.map(jnp.add, totals, grad_params)
        return (totals, (result.astype(jnp.bfloat16), grad_inputs.astype(jnp.bfloat16)))
    zeros = jax.tree.map(jnp.zeros_like, params)
    totals, (results, grads) = lax.scan(step, zeros, (dealt, dealt_lengths.reshape(count, group_size), upstream))
    y_out = results.reshape(SEQS, MAXLEN, D)
    inverse = jnp.zeros((SEQS,), jnp.int32).at[dealing].set(jnp.arange(SEQS, dtype=jnp.int32))
    grad_tokens = grads.reshape(SEQS, MAXLEN, D)[inverse]
    return (y_out, grad_tokens, totals[0], totals[1], totals[2], totals[3], totals[4], totals[5], totals[6], totals[7], totals[8], totals[9], totals[10], totals[11], totals[12], totals[13], totals[14], totals[15], totals[16])
```

```python
import math

import jax
import jax.numpy as jnp
from jax import lax
from jax.experimental import pallas as pl
from jax.experimental.pallas import tpu as pltpu
from jax.sharding import PartitionSpec as P

HEAD_DIM = 64
EPSILON = 1e-07
ROOT_HALF = 0.7071067811865476
INV_ROOT_TAU = 0.3989422804014327
BLOCK = 128
LOW = jnp.bfloat16
WIDE = jnp.float32

NN = (((1,), (0,)), ((), ()))
NT = (((1,), (1,)), ((), ()))
TN = (((0,), (0,)), ((), ()))
TT = (((0,), (1,)), ((), ()))


def mm(left, right, dims=NN):
    return lax.dot_general(left, right, dims, preferred_element_type=WIDE)


def pieces(first, count, chunk):
    out = []
    done = 0
    while done < count:
        place, offset = divmod(first + done, chunk)
        take = min(chunk - offset, count - done)
        out.append((place, offset, done, take))
        done += take
    return out


def chunk_rows(rows, parts, unit):
    return -(-(-(-rows // parts)) // unit) * unit


def call(body, out_shapes, args, scratch=(), smem=0, flops=10**9, moved=4 * 10**6, aliases=None):
    specs = [
        pl.BlockSpec(memory_space=pltpu.SMEM if i < smem else pltpu.VMEM) for i in range(len(args))
    ]
    return pl.pallas_call(
        body,
        out_shape=[jax.ShapeDtypeStruct(shape, kind) for shape, kind in out_shapes],
        in_specs=specs,
        out_specs=[pl.BlockSpec(memory_space=pltpu.VMEM) for _ in out_shapes],
        scratch_shapes=list(scratch),
        input_output_aliases=aliases or {},
        compiler_params=pltpu.CompilerParams(vmem_limit_bytes=40 * 1024 * 1024),
        cost_estimate=pl.CostEstimate(flops=flops, bytes_accessed=moved, transcendentals=0),
    )(*args)


def permute_body(scatter, dealing, source, target):
    total, rows, _ = source.shape

    def step(k, carry):
        if scatter:
            target[dealing[k]] = source[k]
        else:
            target[k] = source[dealing[k]]
        return carry

    lax.fori_loop(0, total, step, 0, unroll=True)


def attention_forward(
    lengths, x, relative, table, wq, bq, wk, bk, wv, bv, wout,
    q_out, k_out, v_out, tab_out, prob_out, ctx_out, attn_out, far_scratch,
):
    length = lengths[lax.axis_index("dp")]
    heads, rows, _ = q_out.shape
    span = tab_out.shape[3]
    buckets = relative.shape[0]
    window = rows + BLOCK
    scale = 1.0 / math.sqrt(3.0 * HEAD_DIM)
    xv = x[...]
    for weight, bias, out in ((wq, bq, q_out), (wk, bk, k_out), (wv, bv, v_out)):
        full = (mm(xv, weight[...]) + bias[...].astype(WIDE)).astype(LOW)
        for h in range(heads):
            out[h] = full[:, h * HEAD_DIM : (h + 1) * HEAD_DIM]
    rel = relative[...]
    hot = jnp.where(
        lax.broadcasted_iota(jnp.int32, (buckets, span), 0) == table[...], 1.0, 0.0
    ).astype(LOW)
    for slot, (weight, bias) in enumerate(((wq, bq), (wk, bk))):
        low = (mm(rel, weight[...]) + bias[...].astype(WIDE)).astype(LOW)
        spread = mm(low, hot, TN).astype(LOW)
        for h in range(heads):
            tab_out[slot, h] = spread[h * HEAD_DIM : (h + 1) * HEAD_DIM]
    key_ok = lax.broadcasted_iota(jnp.int32, (1, rows), 1) < length
    attn_out_acc = attn_out

    def head(h, carry):
        keys = k_out[h]
        values = v_out[h]
        for b in range(rows // BLOCK):
            j0 = b * BLOCK
            w0 = rows - BLOCK - j0
            far = mm(k_out[h, j0 : j0 + BLOCK, :], tab_out[0, h, :, w0 : w0 + window])
            far = pltpu.roll(far, window - BLOCK + 1, 1, stride=1, stride_axis=0)[:, :rows]
            far_scratch[:, j0 : j0 + BLOCK] = far.T
        for a in range(rows // BLOCK):
            i0 = a * BLOCK
            w0 = rows - BLOCK - i0
            block_q = q_out[h, i0 : i0 + BLOCK, :]
            near = mm(block_q, tab_out[1, h, :, w0 : w0 + window])
            near = pltpu.roll(near, window - BLOCK + 1, 1, stride=1, stride_axis=0)[:, :rows]
            score = (mm(block_q, keys, NT) + near + far_scratch[i0 : i0 + BLOCK, :]) * scale
            score = jnp.where(key_ok, score, -1e30)
            top = jnp.max(score, axis=1, keepdims=True)
            weights = jnp.exp(score - top)
            row_ok = i0 + lax.broadcasted_iota(jnp.int32, (BLOCK, 1), 0) < length
            norm = jnp.where(row_ok, 1.0 / jnp.sum(weights, axis=1, keepdims=True), 0.0)
            prob = (weights * norm).astype(LOW)
            prob_out[h, i0 : i0 + BLOCK, :] = prob
            ctx_out[h, i0 : i0 + BLOCK, :] = mm(prob, values).astype(LOW)
        return carry

    lax.fori_loop(0, heads, head, 0)
    total = mm(ctx_out[0], wout[0:HEAD_DIM, :])
    for h in range(1, heads):
        total += mm(ctx_out[h], wout[h * HEAD_DIM : (h + 1) * HEAD_DIM, :])
    attn_out_acc[...] = total.astype(LOW)


def row_norm(values):
    center = values - jnp.mean(values, axis=-1, keepdims=True)
    inverse = lax.rsqrt(jnp.mean(center * center, axis=-1, keepdims=True) + EPSILON)
    return center * inverse, inverse


def norm_back(scaled, normed, inverse):
    one = jnp.mean(scaled, axis=-1, keepdims=True)
    two = jnp.mean(scaled * normed, axis=-1, keepdims=True)
    return inverse * (scaled - one - normed * two)


def ffn_forward(
    x, mine, theirs, bout, gain, shift, wup, bup, wdown,
    normed_out, inverse_out, hidden_out, act_out, slope_out, down_out,
):
    rows = x.shape[0]

    def block(i, carry):
        here = pl.ds(pl.multiple_of(i * BLOCK, BLOCK), BLOCK)
        attn = mine[here, :].astype(WIDE) + theirs[here, :].astype(WIDE) + bout[...].astype(WIDE)
        normed, inverse = row_norm(x[here, :].astype(WIDE) + attn)
        normed_out[here, :] = normed
        inverse_out[here, :] = inverse
        low = (normed * gain[...].astype(WIDE) + shift[...].astype(WIDE)).astype(LOW)
        hidden_out[here, :] = low
        u = mm(low, wup[...]) + bup[...].astype(WIDE)
        cdf = 0.5 * (1.0 + lax.erf(u * ROOT_HALF))
        density = jnp.exp(-0.5 * u * u) * INV_ROOT_TAU
        act = (u * cdf).astype(LOW)
        act_out[here, :] = act
        slope_out[here, :] = (cdf + u * density).astype(LOW)
        down_out[here, :] = mm(act, wdown[...]).astype(LOW)
        return carry

    lax.fori_loop(0, rows // BLOCK, block, 0)


def ffn_backward(
    chunk, piece, lengths,
    mine, theirs, bdown, normed, gain, shift, fgain, fshift, cot_mine, cot_theirs,
    hidden, act, slope, wup, wdown,
    buffer_out, part_out, gf_out, small_out, low_scratch, gu_scratch,
):
    length = lengths[lax.axis_index("dp")]
    side = lax.axis_index("tensor")
    rows, width = normed.shape
    half = rows // 2
    total = buffer_out.shape[0]
    units = act.shape[1]
    sums = [jnp.zeros((1, width), WIDE) for _ in range(3)]
    for i in range(rows // BLOCK):
        here = slice(i * BLOCK, (i + 1) * BLOCK)
        source = (i * BLOCK) // half
        local = slice(i * BLOCK - source * half, (i + 1) * BLOCK - source * half)
        cot = jnp.where(side == source, cot_mine[local, :], cot_theirs[local, :]).astype(WIDE)
        f = mine[here, :].astype(WIDE) + theirs[here, :].astype(WIDE) + bdown[...].astype(WIDE)
        h = normed[here, :] * gain[...].astype(WIDE) + shift[...].astype(WIDE)
        n2, r2 = row_norm(h + f)
        y = (n2 * fgain[...].astype(WIDE) + fshift[...].astype(WIDE)).astype(LOW)

        @pl.when(side == source)
        def _():
            for p in range(BLOCK // piece):
                place = local.start // piece + p
                buffer_out[place, chunk : chunk + piece, :] = y[p * piece : (p + 1) * piece]

        row_ok = i * BLOCK + lax.broadcasted_iota(jnp.int32, (BLOCK, 1), 0) < length
        gy = jnp.where(row_ok, cot, 0.0)
        gf = norm_back(gy * fgain[...].astype(WIDE), n2, r2)
        gf_out[here, :] = gf
        low = gf.astype(LOW)
        low_scratch[here, :] = low
        sums[0] += jnp.sum(low.astype(WIDE), axis=0, keepdims=True)
        sums[1] += jnp.sum(gy * n2, axis=0, keepdims=True)
        sums[2] += jnp.sum(gy, axis=0, keepdims=True)
    gu_sum = jnp.zeros((1, units), WIDE)
    for i in range(rows // BLOCK):
        here = slice(i * BLOCK, (i + 1) * BLOCK)
        gu = (mm(low_scratch[here, :], wdown[...], NT) * slope[here, :].astype(WIDE)).astype(LOW)
        gu_scratch[here, :] = gu
        gu_sum += jnp.sum(gu.astype(WIDE), axis=0, keepdims=True)
        part_out[here, :] = mm(gu, wup[...], NT).astype(LOW)
    small_out[...] = jnp.zeros_like(small_out)
    for k in range(units // width):
        small_out[k : k + 1, :] = gu_sum[:, k * width : (k + 1) * width]
    for k in range(3):
        small_out[units // width + k : units // width + k + 1, :] = sums[k]

    def put(first, value):
        for place, offset, start, take in pieces(first, value.shape[0], chunk):
            buffer_out[place, offset : offset + take, :] = value[start : start + take]

    put(units, mm(act[...], low_scratch[...], TN).astype(LOW))
    for k in range(units // width):
        columns = slice(k * width, (k + 1) * width)
        put(k * width, mm(hidden[...], gu_scratch[:, columns], TN).astype(LOW))
    for place in range(-(-2 * units // chunk), total):
        buffer_out[place, :chunk, :] = jnp.zeros((chunk, width), LOW)
    for place in range(half // piece, total):
        buffer_out[place, chunk:, :] = jnp.zeros((piece, width), LOW)


def attention_backward(
    x, relative, table, wq, wk, wv, wout,
    mine, theirs, gf, normed, inverse, gain,
    q, k, v, tab, prob, ctx,
    send_out, keep_out, gp_out, weights_out, small_out,
    gpb_scratch, gs_scratch, gpk_scratch, gpq_scratch, g_scratch, rel_scratch, gctx_scratch,
):
    side = lax.axis_index("tensor")
    heads, rows, _ = q.shape
    width = x.shape[1]
    half = rows // 2
    span = tab.shape[3]
    buckets = relative.shape[0]
    window = rows + BLOCK
    scale = 1.0 / math.sqrt(3.0 * HEAD_DIM)
    blocks = rows // BLOCK
    part = heads * HEAD_DIM
    sums = [jnp.zeros((1, width), WIDE) for _ in range(3)]
    for i in range(blocks):
        here = slice(i * BLOCK, (i + 1) * BLOCK)
        gh = gf[here, :] + (mine[here, :].astype(WIDE) + theirs[here, :].astype(WIDE))
        n1 = normed[here, :]
        gp = norm_back(gh * gain[...].astype(WIDE), n1, inverse[here, :])
        gp_out[here, :] = gp
        low = gp.astype(LOW)
        gpb_scratch[here, :] = low
        sums[0] += jnp.sum(low.astype(WIDE), axis=0, keepdims=True)
        sums[1] += jnp.sum(gh * n1, axis=0, keepdims=True)
        sums[2] += jnp.sum(gh, axis=0, keepdims=True)
        grad = mm(low, wout[...], NT).astype(LOW)
        for h in range(heads):
            gctx_scratch[h, here, :] = grad[:, h * HEAD_DIM : (h + 1) * HEAD_DIM]
    small_out[...] = jnp.zeros_like(small_out)
    for n in range(3):
        small_out[2 + n : 3 + n, :] = sums[n]
    for h in range(heads):
        weights_out[width + part + h * HEAD_DIM : width + part + (h + 1) * HEAD_DIM, :] = mm(
            ctx[h], gpb_scratch[...], TN
        ).astype(LOW)
    anti = jnp.where(
        lax.broadcasted_iota(jnp.int32, (BLOCK, BLOCK), 0)
        + lax.broadcasted_iota(jnp.int32, (BLOCK, BLOCK), 1)
        == BLOCK - 1,
        1.0,
        0.0,
    ).astype(LOW)
    pad = jnp.zeros((BLOCK, BLOCK), WIDE)

    def head(h, carry):
        keys = k[h]
        queries = q[h]
        gpk_scratch[h] = jnp.zeros((HEAD_DIM, span), WIDE)
        gpq_scratch[h] = jnp.zeros((HEAD_DIM, span), WIDE)
        for i in range(blocks):
            i0 = i * BLOCK
            w0 = rows - BLOCK - i0
            weights = prob[h, i0 : i0 + BLOCK, :].astype(WIDE)
            gprob = mm(gctx_scratch[h, i0 : i0 + BLOCK, :], v[h], NT)
            dots = jnp.sum(weights * gprob, axis=1, keepdims=True)
            gs = (weights * (gprob - dots)).astype(LOW)
            gs_scratch[i0 : i0 + BLOCK, :] = gs
            turned = mm(anti, gs)
            moved = pltpu.roll(
                jnp.concatenate([turned, pad], axis=1), 0, 1, stride=1, stride_axis=0
            ).astype(LOW)
            table_here = tab[1, h, :, w0 : w0 + window]
            gq = (mm(turned.astype(LOW), keys) + mm(moved, table_here, NT)) * scale
            g_scratch[0, h, i0 : i0 + BLOCK, :] = mm(anti, gq.astype(LOW)).astype(LOW)
            turned_q = mm(anti, q[h, i0 : i0 + BLOCK, :]).astype(LOW)
            gpk_scratch[h, :, w0 : w0 + window] += mm(turned_q, moved, TN)
        for b in range(blocks):
            j0 = b * BLOCK
            w0 = rows - BLOCK - j0
            turned = mm(anti, gs_scratch[:, j0 : j0 + BLOCK], NT)
            moved = pltpu.roll(
                jnp.concatenate([turned, pad], axis=1), 0, 1, stride=1, stride_axis=0
            ).astype(LOW)
            table_here = tab[0, h, :, w0 : w0 + window]
            gk = (mm(turned.astype(LOW), queries) + mm(moved, table_here, NT)) * scale
            g_scratch[1, h, j0 : j0 + BLOCK, :] = mm(anti, gk.astype(LOW)).astype(LOW)
            turned_k = mm(anti, k[h, j0 : j0 + BLOCK, :]).astype(LOW)
            gpq_scratch[h, :, w0 : w0 + window] += mm(turned_k, moved, TN)
        g_scratch[2, h] = mm(prob[h], gctx_scratch[h], TN).astype(LOW)
        return carry

    lax.fori_loop(0, heads, head, 0)
    hot = jnp.where(
        lax.broadcasted_iota(jnp.int32, (buckets, span), 0) == table[...], 1.0, 0.0
    ).astype(LOW)
    gpq = jnp.concatenate(
        [mm(hot, gpq_scratch[h].astype(LOW), NT) * scale for h in range(heads)], axis=1
    )
    gpk = jnp.concatenate(
        [mm(hot, gpk_scratch[h].astype(LOW), NT) * scale for h in range(heads)], axis=1
    )
    gpq_low, gpk_low = gpq.astype(LOW), gpk.astype(LOW)
    rel_scratch[...] = mm(gpq_low, wq[...], NT) + mm(gpk_low, wk[...], NT)
    send_out[rows : rows + half, :] = rel_scratch[
        pl.ds(pl.multiple_of((1 - side) * half, half), half), :
    ].astype(LOW)
    keep_out[...] = rel_scratch[pl.ds(pl.multiple_of(side * half, half), half), :].astype(LOW)
    gq = jnp.concatenate([g_scratch[0, h] for h in range(heads)], axis=1)
    gk = jnp.concatenate([g_scratch[1, h] for h in range(heads)], axis=1)
    gv = jnp.concatenate([g_scratch[2, h] for h in range(heads)], axis=1)
    send_out[:rows, :] = (
        mm(gq, wq[...], NT) + mm(gk, wk[...], NT) + mm(gv, wv[...], NT)
    ).astype(LOW)
    xv = x[...]
    rel = relative[...]
    weights_out[:width, 0:part] = (mm(xv, gq, TN) + mm(rel, gpq_low, TN)).astype(LOW)
    weights_out[:width, part : 2 * part] = (mm(xv, gk, TN) + mm(rel, gpk_low, TN)).astype(LOW)
    grad_v = mm(xv, gv, TN).astype(LOW)
    weights_out[width : width + part, 0:part] = grad_v[:part]
    weights_out[width : width + part, part : 2 * part] = grad_v[part:]
    small_out[0:1, 0:part] = jnp.sum(gq.astype(WIDE), axis=0, keepdims=True) + jnp.sum(
        gpq, axis=0, keepdims=True
    )
    small_out[0:1, part : 2 * part] = jnp.sum(gk.astype(WIDE), axis=0, keepdims=True) + jnp.sum(
        gpk, axis=0, keepdims=True
    )
    small_out[1:2, 0:part] = jnp.sum(gv.astype(WIDE), axis=0, keepdims=True)


def tail_pack(
    chunk, send, got, keep, gp, weights, small_ffn, small_attn, y_moved, buffer_out, grad_out
):
    total, piece, width = y_moved.shape
    rows = gp.shape[0]

    def put(first, value):
        for place, offset, start, take in pieces(first, value.shape[0], chunk):
            buffer_out[place, offset : offset + take, :] = value[start : start + take]

    count = weights.shape[0]
    put(0, weights)
    put(count, (keep[...].astype(WIDE) + got[rows:, :].astype(WIDE)).astype(LOW))
    count += keep.shape[0]
    small = jnp.concatenate([small_ffn[...], small_attn[...]], axis=0).astype(LOW)
    put(count, small)
    count += small.shape[0]
    place, offset = divmod(count, chunk)
    if offset:
        buffer_out[place, offset:chunk, :] = jnp.zeros((chunk - offset, width), LOW)
        place += 1
    for rest in range(place, total):
        buffer_out[rest, :chunk, :] = jnp.zeros((chunk, width), LOW)
    buffer_out[:, chunk:, :] = y_moved[...]
    for i in range(rows // BLOCK):
        here = slice(i * BLOCK, (i + 1) * BLOCK)
        both = send[here, :].astype(WIDE) + got[here, :].astype(WIDE)
        grad_out[here, :] = (gp[here, :] + both).astype(LOW)


def reduce_first(chunk, dealing, got, sum_out, y_out):
    total = got.shape[0]
    acc = got[0, :chunk, :].astype(WIDE)
    for k in range(1, total):
        acc += got[k, :chunk, :].astype(WIDE)
    sum_out[...] = acc.astype(LOW)
    for k in range(total):
        y_out[k] = got[dealing[k], chunk:, :]


def reduce_second(chunk, got, first, spread_out, y_out):
    total = got.shape[0]
    piece = got.shape[1] - chunk
    acc = got[0, :chunk, :].astype(WIDE)
    for k in range(1, total):
        acc += got[k, :chunk, :].astype(WIDE)
    low = acc.astype(LOW)
    ahead = first.shape[0]
    for k in range(spread_out.shape[0]):
        spread_out[k, :ahead, :] = first[...]
        spread_out[k, ahead:, :] = low
    for k in range(y_out.shape[0] // piece):
        y_out[k * piece : (k + 1) * piece, :] = got[k, chunk:, :]


def unpack(
    chunk_one, chunk_two, gathered,
    wup_out, wdown_out, bup_out, wq_out, wk_out, wv_out, wout_out, rel_out,
    bq_out, bk_out, bv_out, bout_out, again_out, ashift_out, bdown_out, fgain_out, fshift_out,
):
    inner = gathered.shape[0]
    width = gathered.shape[3]
    units = wup_out.shape[1]
    part = wq_out.shape[1]

    def rows(first, count, chunk, base):
        for place, offset, start, take in pieces(first, count, chunk):
            yield start, take, gathered[
                place % inner, place // inner, base + offset : base + offset + take, :
            ].astype(WIDE)

    for k in range(units // width):
        for start, take, value in rows(k * width, width, chunk_one, 0):
            wup_out[start : start + take, k * width : (k + 1) * width] = value
    for start, take, value in rows(units, units, chunk_one, 0):
        wdown_out[start : start + take, :] = value
    for start, take, value in rows(0, width, chunk_two, chunk_one):
        wq_out[start : start + take, :] = value[:, :part]
        wk_out[start : start + take, :] = value[:, part:]
    for start, take, value in rows(width, part, chunk_two, chunk_one):
        wv_out[start : start + take, :] = value[:, :part]
        wv_out[part + start : part + start + take, :] = value[:, part:]
    for start, take, value in rows(width + part, part, chunk_two, chunk_one):
        wout_out[start : start + take, :] = value
    first = width + 2 * part
    for start, take, value in rows(first, rel_out.shape[0], chunk_two, chunk_one):
        rel_out[start : start + take, :] = value.astype(LOW)
    first += rel_out.shape[0]
    small = jnp.concatenate([value for _, _, value in rows(first, 16, chunk_two, chunk_one)], axis=0)
    ups = units // width
    for k in range(ups):
        bup_out[:, k * width : (k + 1) * width] = small[k : k + 1]
    bdown_out[...] = small[ups : ups + 1]
    fgain_out[...] = small[ups + 1 : ups + 2]
    fshift_out[...] = small[ups + 2 : ups + 3]
    bq_out[...] = small[8:9, :part]
    bk_out[...] = small[8:9, part:]
    bv_out[...] = small[9:10, :part]
    bout_out[...] = small[10:11]
    again_out[...] = small[11:12]
    ashift_out[...] = small[12:13]


def with_statics(body, *statics):
    def wrapped(*refs):
        body(*statics, *refs)

    wrapped.__name__ = body.__name__
    return wrapped


def swap(array):
    return lax.ppermute(array, "tensor", [(0, 1), (1, 0)])


def exchange(array, groups=None):
    return lax.all_to_all(
        array, "dp", split_axis=0, concat_axis=0, tiled=True, axis_index_groups=groups
    )


def on_device(
    tokens, lengths, dealing, bucket_table, relative,
    w_query, b_query, w_key, b_key, w_value, b_value, w_out, b_out,
    attn_gain, attn_shift, w_up, b_up, w_down, b_down, ffn_gain, ffn_shift, cotangent,
):
    _, rows, width = tokens.shape
    total = dealing.shape[0]
    part = w_query.shape[1]
    heads = part // HEAD_DIM
    units = w_up.shape[1]
    half = rows // 2
    span = 2 * rows
    piece = max(16, half // total)
    spots = half // piece
    side = lax.axis_index("tensor")
    chunk_one = chunk_rows(2 * units, total, 8)
    chunk_two = chunk_rows(width + 2 * part + half + 16, total, 8)

    def row(vector):
        return vector.reshape(1, -1)

    def padded(array):
        if spots == total:
            return array
        return jnp.pad(array, ((0, total - spots), (0, 0), (0, 0)))

    cot_half = lax.dynamic_slice_in_dim(cotangent[0], side * half, half, 0)
    cot_got = exchange(padded(cot_half.reshape(spots, piece, width)))
    (cot_turned,) = call(
        with_statics(permute_body, True), [(cot_got.shape, LOW)], (dealing, cot_got), smem=1
    )
    cot_back = exchange(cot_turned)
    cot_mine = cot_back[:spots].reshape(half, width)
    cot_theirs = swap(cot_mine)

    x = tokens[0]
    table = jnp.pad(jnp.flip(bucket_table), (0, span - bucket_table.shape[0]), constant_values=-1)
    table = table.reshape(1, span)
    q, k, v, tab, prob, ctx, attn_part = call(
        attention_forward,
        [((heads, rows, HEAD_DIM), LOW)] * 3
        + [((2, heads, HEAD_DIM, span), LOW), ((heads, rows, rows), LOW)]
        + [((heads, rows, HEAD_DIM), LOW), ((rows, width), LOW)],
        (lengths, x, relative, table, w_query, row(b_query), w_key, row(b_key), w_value,
         row(b_value), w_out),
        scratch=[pltpu.VMEM((rows, rows), WIDE)],
        smem=1,
        flops=10**10,
    )
    attn_got = swap(attn_part)
    normed, inverse, hidden, act, slope, down_part = call(
        ffn_forward,
        [((rows, width), WIDE), ((rows, 1), WIDE), ((rows, width), LOW), ((rows, units), LOW),
         ((rows, units), LOW), ((rows, width), LOW)],
        (x, attn_part, attn_got, row(b_out), row(attn_gain), row(attn_shift), w_up, row(b_up),
         w_down),
        flops=4 * 10**9,
    )
    down_got = swap(down_part)
    buffer_one, hidden_part, gf, small_ffn = call(
        with_statics(ffn_backward, chunk_one, piece),
        [((total, chunk_one + piece, width), LOW), ((rows, width), LOW), ((rows, width), WIDE),
         ((8, width), WIDE)],
        (lengths, down_part, down_got, row(b_down), normed, row(attn_gain), row(attn_shift),
         row(ffn_gain), row(ffn_shift), cot_mine, cot_theirs, hidden, act, slope, w_up, w_down),
        scratch=[pltpu.VMEM((rows, width), LOW), pltpu.VMEM((rows, units), LOW)],
        smem=1,
        flops=4 * 10**9,
    )
    hidden_got = swap(hidden_part)
    got_one = exchange(buffer_one)
    send, keep, gp, weights, small_attn = call(
        attention_backward,
        [((rows + half, width), LOW), ((half, width), LOW), ((rows, width), WIDE),
         ((width + 2 * part, width), LOW), ((8, width), WIDE)],
        (x, relative, table, w_query, w_key, w_value, w_out, hidden_part, hidden_got, gf, normed,
         inverse, row(attn_gain), q, k, v, tab, prob, ctx),
        scratch=[
            pltpu.VMEM((rows, width), LOW),
            pltpu.VMEM((rows, rows), LOW),
            pltpu.VMEM((heads, HEAD_DIM, span), WIDE),
            pltpu.VMEM((heads, HEAD_DIM, span), WIDE),
            pltpu.VMEM((3, heads, rows, HEAD_DIM), LOW),
            pltpu.VMEM((rows, width), WIDE),
            pltpu.VMEM((heads, rows, HEAD_DIM), LOW),
        ],
        flops=2 * 10**10,
    )
    sent = swap(send)
    sum_one, y_moved = call(
        with_statics(reduce_first, chunk_one),
        [((chunk_one, width), LOW), ((total, piece, width), LOW)],
        (dealing, got_one),
        smem=1,
    )
    buffer_two, grad_tokens = call(
        with_statics(tail_pack, chunk_two),
        [((total, chunk_two + piece, width), LOW), ((rows, width), LOW)],
        (send, sent, keep, gp, weights, small_ffn, small_attn, y_moved),
    )
    got_two = exchange(buffer_two)
    inner = 1 << ((total.bit_length()) // 2)
    outer = total // inner
    ring_far = [[o * inner + i for o in range(outer)] for i in range(inner)]
    ring_near = [[o * inner + i for i in range(inner)] for o in range(outer)]
    chunk = chunk_one + chunk_two
    spread, y_half = call(
        with_statics(reduce_second, chunk_two),
        [((outer, chunk, width), LOW), ((half, width), LOW)],
        (got_two, sum_one),
    )
    lines = exchange(spread, ring_far)
    y_other = swap(y_half)
    wide = jnp.broadcast_to(lines[None], (inner, outer, chunk, width)).reshape(
        inner * outer, chunk, width
    )
    gathered = exchange(wide, ring_near).reshape(inner, outer, chunk, width)
    out = call(
        with_statics(unpack, chunk_one, chunk_two),
        [((width, units), WIDE), ((units, width), WIDE), ((1, units), WIDE)]
        + [((width, part), WIDE)] * 3
        + [((part, width), WIDE), ((half, width), LOW)]
        + [((1, part), WIDE)] * 3
        + [((1, width), WIDE)] * 6,
        (gathered,),
    )
    (g_up, g_down, g_bup, g_wq, g_wk, g_wv, g_wout, rel_half, g_bq, g_bk, g_bv, g_bout, g_again,
     g_ashift, g_bdown, g_fgain, g_fshift) = out
    rel_other = swap(rel_half)

    def join(own, other):
        first = jnp.where(side == 0, own, other)
        second = jnp.where(side == 0, other, own)
        return jnp.concatenate([first, second], axis=0)

    y = join(y_half, y_other)[None]
    g_rel = join(rel_half, rel_other).astype(WIDE)
    return (
        y, grad_tokens[None], g_rel, g_wq, g_bq[0], g_wk, g_bk[0], g_wv, g_bv[0], g_wout,
        g_bout[0], g_again[0], g_ashift[0], g_up, g_bup[0], g_down, g_bdown[0], g_fgain[0],
        g_fshift[0],
    )


def solution(mesh):
    return jax.shard_map(
        on_device,
        mesh=mesh,
        in_specs=(
            P("dp", None, None), P(), P(), P(), P(),
            P(None, "tensor"), P("tensor"), P(None, "tensor"), P("tensor"),
            P(None, "tensor"), P("tensor"), P("tensor", None), P(), P(), P(),
            P(None, "tensor"), P("tensor"), P("tensor", None), P(), P(), P(),
            P("dp", None, None),
        ),
        out_specs=(
            P("dp", None, None), P("dp", None, None), P(),
            P(None, "tensor"), P("tensor"), P(None, "tensor"), P("tensor"),
            P(None, "tensor"), P("tensor"), P("tensor", None), P(), P(), P(),
            P(None, "tensor"), P("tensor"), P("tensor", None), P(), P(), P(),
        ),
        check_vma=False,
    )
```

```python
import math

import jax
import jax.numpy as jnp
from jax import lax
from jax.experimental import pallas as pl
from jax.experimental.pallas import tpu as pltpu
from jax.sharding import PartitionSpec as P

HEAD_DIM = 64
EPSILON = 1e-07
ROOT_HALF = 0.7071067811865476
INV_ROOT_TAU = 0.3989422804014327
BLOCK = 128
LOW = jnp.bfloat16
WIDE = jnp.float32

NN = (((1,), (0,)), ((), ()))
NT = (((1,), (1,)), ((), ()))
TN = (((0,), (0,)), ((), ()))
TT = (((0,), (1,)), ((), ()))


def mm(left, right, dims=NN):
    return lax.dot_general(left, right, dims, preferred_element_type=WIDE)


def pieces(first, count, chunk):
    out = []
    done = 0
    while done < count:
        place, offset = divmod(first + done, chunk)
        take = min(chunk - offset, count - done)
        out.append((place, offset, done, take))
        done += take
    return out


def chunk_rows(rows, parts, unit):
    return -(-(-(-rows // parts)) // unit) * unit


def call(body, out_shapes, args, scratch=(), smem=0, flops=10**9, moved=4 * 10**6, aliases=None):
    specs = [
        pl.BlockSpec(memory_space=pltpu.SMEM if i < smem else pltpu.VMEM) for i in range(len(args))
    ]
    return pl.pallas_call(
        body,
        out_shape=[jax.ShapeDtypeStruct(shape, kind) for shape, kind in out_shapes],
        in_specs=specs,
        out_specs=[pl.BlockSpec(memory_space=pltpu.VMEM) for _ in out_shapes],
        scratch_shapes=list(scratch),
        input_output_aliases=aliases or {},
        compiler_params=pltpu.CompilerParams(vmem_limit_bytes=16 * 1024 * 1024),
        cost_estimate=pl.CostEstimate(flops=flops, bytes_accessed=moved, transcendentals=0),
    )(*args)


def permute_body(piece, dealing, source, target):
    for k in range(source.shape[0]):
        there = dealing[k]
        target[there, :piece, :] = source[k, :piece, :]
        target[k, piece:, :] = source[there, piece:, :]


def assemble(mine, theirs, spots, first, piece, target):
    side = lax.axis_index("tensor")
    half = spots * piece
    for source, base in ((mine, side * half), (theirs, (1 - side) * half)):
        for p in range(spots):
            target[pl.ds(pl.multiple_of(base + p * piece, piece), piece), :] = source[
                p, first : first + piece, :
            ]


def project(x, weights, biases, outs):
    for weight, bias, out in zip(weights, biases, outs):
        full = (mm(x, weight[...], NT) + bias[...].astype(WIDE)[None, :]).astype(LOW)
        for h in range(out.shape[0]):
            out[h] = full[:, h * HEAD_DIM : (h + 1) * HEAD_DIM]


def anti_diagonal():
    return jnp.where(
        lax.broadcasted_iota(jnp.int32, (BLOCK, BLOCK), 0)
        + lax.broadcasted_iota(jnp.int32, (BLOCK, BLOCK), 1)
        == BLOCK - 1,
        1.0,
        0.0,
    ).astype(LOW)


def one_hot(table, buckets):
    anti = anti_diagonal()
    entries = table[...]
    high = entries // 256
    turned = mm(high.astype(WIDE).astype(LOW), anti) * 256.0 + mm(
        (entries - high * 256).astype(WIDE).astype(LOW), anti
    )
    turned = turned.astype(jnp.int32)
    count = table.shape[0]
    rows = lax.broadcasted_iota(jnp.int32, (buckets, BLOCK), 0)
    return jnp.concatenate(
        [
            jnp.where(rows == turned[count - 1 - b : count - b, :], 1.0, 0.0).astype(LOW)
            for b in range(count)
        ],
        axis=1,
    )


def attend(length, q, k, v, tab, wout, ctx, attn_out, far_scratch, prob_out):
    heads, rows, _ = q.shape
    window = rows + BLOCK
    scale = 1.0 / math.sqrt(3.0 * HEAD_DIM)
    key_ok = lax.broadcasted_iota(jnp.int32, (1, rows), 1) < length

    def head(h, carry):
        keys = k[h]
        values = v[h]
        for b in range(rows // BLOCK):
            j0 = b * BLOCK
            w0 = rows - BLOCK - j0
            far = mm(k[h, j0 : j0 + BLOCK, :], tab[0, h, :, w0 : w0 + window])
            far = pltpu.roll(far, window - BLOCK, 1, stride=1, stride_axis=0)[:, :rows]
            far_scratch[:, j0 : j0 + BLOCK] = far.T
        for a in range(rows // BLOCK):
            i0 = a * BLOCK
            w0 = rows - BLOCK - i0
            block_q = q[h, i0 : i0 + BLOCK, :]
            near = mm(block_q, tab[1, h, :, w0 : w0 + window])
            near = pltpu.roll(near, window - BLOCK, 1, stride=1, stride_axis=0)[:, :rows]
            score = (mm(block_q, keys, NT) + near + far_scratch[i0 : i0 + BLOCK, :]) * scale
            score = jnp.where(key_ok, score, -1e30)
            top = jnp.max(score, axis=1, keepdims=True)
            weights = jnp.exp(score - top)
            row_ok = i0 + lax.broadcasted_iota(jnp.int32, (BLOCK, 1), 0) < length
            norm = jnp.where(row_ok, 1.0 / jnp.sum(weights, axis=1, keepdims=True), 0.0)
            prob = (weights * norm).astype(LOW)
            if prob_out is not None:
                prob_out[h, i0 : i0 + BLOCK, :] = prob
            ctx[h, i0 : i0 + BLOCK, :] = mm(prob, values).astype(LOW)
        return carry

    lax.fori_loop(0, heads, head, 0)
    total = mm(ctx[0], wout[0:HEAD_DIM, :])
    for h in range(1, heads):
        total += mm(ctx[h], wout[h * HEAD_DIM : (h + 1) * HEAD_DIM, :])
    attn_out[...] = total.astype(LOW)


def attention_forward(
    lengths, x, relative, table, wq, bq, wk, bk, wv, bv, wout,
    q_out, k_out, v_out, tab_out, prob_out, ctx_out, attn_out, far_scratch,
):
    length = lengths[lax.axis_index("dp")]
    project(x[...], (wq, wk, wv), (bq, bk, bv), (q_out, k_out, v_out))
    rel = relative[...]
    hot = one_hot(table, relative.shape[0])
    for slot, (weight, bias) in enumerate(((wq, bq), (wk, bk))):
        low = (mm(rel, weight[...], NT) + bias[...].astype(WIDE)[None, :]).astype(LOW)
        spread = mm(low, hot, TN).astype(LOW)
        for h in range(q_out.shape[0]):
            tab_out[slot, h] = spread[h * HEAD_DIM : (h + 1) * HEAD_DIM]
    attend(length, q_out, k_out, v_out, tab_out, wout, ctx_out, attn_out, far_scratch, prob_out)


def attention_dealt(
    spots, piece, lengths, dealing, mine, theirs, tab, wq, bq, wk, bk, wv, bv, wout,
    x_out, attn_out, q, k, v, ctx, far_scratch,
):
    length = lengths[dealing[lax.axis_index("dp")]]
    assemble(mine, theirs, spots, piece, piece, x_out)
    project(x_out[...], (wq, wk, wv), (bq, bk, bv), (q, k, v))
    attend(length, q, k, v, tab, wout, ctx, attn_out, far_scratch, None)


def row_norm(values):
    center = values - jnp.mean(values, axis=-1, keepdims=True)
    inverse = lax.rsqrt(jnp.mean(center * center, axis=-1, keepdims=True) + EPSILON)
    return center * inverse, inverse


def norm_back(scaled, normed, inverse):
    one = jnp.mean(scaled, axis=-1, keepdims=True)
    two = jnp.mean(scaled * normed, axis=-1, keepdims=True)
    return inverse * (scaled - one - normed * two)


def ffn_forward(
    keep, x, mine, theirs, bout, gain, shift, wup, bup, wdown, normed_out, down_out,
    inverse_out=None, hidden_out=None, act_out=None, slope_out=None,
):
    rows = x.shape[0]

    def block(i, carry):
        here = pl.ds(pl.multiple_of(i * BLOCK, BLOCK), BLOCK)
        attn = mine[here, :].astype(WIDE) + theirs[here, :].astype(WIDE) + wide_row(bout)
        normed, inverse = row_norm(x[here, :].astype(WIDE) + attn)
        normed_out[here, :] = normed
        low = (normed * wide_row(gain) + wide_row(shift)).astype(LOW)
        u = mm(low, wup[...]) + wide_row(bup)
        cdf = 0.5 * (1.0 + lax.erf(u * ROOT_HALF))
        act = (u * cdf).astype(LOW)
        if keep:
            inverse_out[here, :] = inverse
            hidden_out[here, :] = low
            act_out[here, :] = act
            density = jnp.exp(-0.5 * u * u) * INV_ROOT_TAU
            slope_out[here, :] = (cdf + u * density).astype(LOW)
        down_out[here, :] = mm(act, wdown[...]).astype(LOW)
        return carry

    lax.fori_loop(0, rows // BLOCK, block, 0)


def wide_row(vector):
    return vector[...].astype(WIDE)[None, :]


def second_norm(here, mine, theirs, bdown, normed, gain, shift):
    f = mine[here, :].astype(WIDE) + theirs[here, :].astype(WIDE) + wide_row(bdown)
    return row_norm(normed[here, :] * wide_row(gain) + wide_row(shift) + f)


def finish_dealt(mine, theirs, bdown, normed, gain, shift, fgain, fshift, y_out):
    for i in range(normed.shape[0] // BLOCK):
        here = slice(i * BLOCK, (i + 1) * BLOCK)
        n2, _ = second_norm(here, mine, theirs, bdown, normed, gain, shift)
        y_out[here, :] = (n2 * wide_row(fgain) + wide_row(fshift)).astype(LOW)


def put(buffer, chunk, base, first, value):
    inner = buffer.shape[0]
    for place, offset, start, take in pieces(first, value.shape[0], chunk):
        buffer[place % inner, place // inner, base + offset : base + offset + take, :] = value[
            start : start + take
        ]


def put_zeros(buffer, chunk, first):
    inner, outer, _, width = buffer.shape
    left = inner * outer * chunk - first
    if left > 0:
        put(buffer, chunk, 0, first, jnp.zeros((left, width), buffer.dtype))


def ffn_backward(
    chunk, spots, piece, lengths,
    mine, theirs, bdown, normed, gain, shift, fgain, cot_mine, cot_theirs,
    hidden, act, slope, wup, wdown,
    buffer_out, part_out, gf_out, small_out, low_scratch, gu_scratch, cot_scratch,
):
    length = lengths[lax.axis_index("dp")]
    rows, width = normed.shape
    units = act.shape[1]
    assemble(cot_mine, cot_theirs, spots, 0, piece, cot_scratch)
    sums = [jnp.zeros((1, width), WIDE) for _ in range(3)]
    for i in range(rows // BLOCK):
        here = slice(i * BLOCK, (i + 1) * BLOCK)
        n2, r2 = second_norm(here, mine, theirs, bdown, normed, gain, shift)
        row_ok = i * BLOCK + lax.broadcasted_iota(jnp.int32, (BLOCK, 1), 0) < length
        gy = jnp.where(row_ok, cot_scratch[here, :].astype(WIDE), 0.0)
        gf = norm_back(gy * wide_row(fgain), n2, r2)
        gf_out[here, :] = gf
        low = gf.astype(LOW)
        low_scratch[here, :] = low
        sums[0] += jnp.sum(low.astype(WIDE), axis=0, keepdims=True)
        sums[1] += jnp.sum(gy * n2, axis=0, keepdims=True)
        sums[2] += jnp.sum(gy, axis=0, keepdims=True)
    gu_sum = jnp.zeros((1, units), WIDE)
    for i in range(rows // BLOCK):
        here = slice(i * BLOCK, (i + 1) * BLOCK)
        gu = (mm(low_scratch[here, :], wdown[...], NT) * slope[here, :].astype(WIDE)).astype(LOW)
        gu_scratch[here, :] = gu
        gu_sum += jnp.sum(gu.astype(WIDE), axis=0, keepdims=True)
        part_out[here, :] = mm(gu, wup[...], NT).astype(LOW)
    small_out[...] = jnp.zeros_like(small_out)
    for k in range(units // width):
        small_out[k : k + 1, :] = gu_sum[:, k * width : (k + 1) * width]
    for k in range(3):
        small_out[units // width + k : units // width + k + 1, :] = sums[k]
    put(buffer_out, chunk, 0, units, mm(act[...], low_scratch[...], TN).astype(LOW))
    for k in range(units // width):
        columns = slice(k * width, (k + 1) * width)
        put(
            buffer_out, chunk, 0, k * width,
            mm(hidden[...], gu_scratch[:, columns], TN).astype(LOW),
        )
    put_zeros(buffer_out, chunk, 2 * units)


def attention_backward(
    x, relative, table, wq, wk, wv, wout,
    mine, theirs, gf, normed, inverse, gain,
    q, k, v, tab, prob, ctx,
    send_out, keep_out, gp_out, weights_out, small_out,
    gpb_scratch, gs_scratch, gpk_scratch, gpq_scratch, g_scratch, rel_scratch, gctx_scratch,
):
    side = lax.axis_index("tensor")
    heads, rows, _ = q.shape
    width = x.shape[1]
    half = rows // 2
    span = tab.shape[3]
    buckets = relative.shape[0]
    window = rows + BLOCK
    scale = 1.0 / math.sqrt(3.0 * HEAD_DIM)
    blocks = rows // BLOCK
    part = heads * HEAD_DIM
    sums = [jnp.zeros((1, width), WIDE) for _ in range(3)]
    for i in range(blocks):
        here = slice(i * BLOCK, (i + 1) * BLOCK)
        gh = gf[here, :] + (mine[here, :].astype(WIDE) + theirs[here, :].astype(WIDE))
        n1 = normed[here, :]
        gp = norm_back(gh * wide_row(gain), n1, inverse[here, :])
        gp_out[here, :] = gp
        low = gp.astype(LOW)
        gpb_scratch[here, :] = low
        sums[0] += jnp.sum(low.astype(WIDE), axis=0, keepdims=True)
        sums[1] += jnp.sum(gh * n1, axis=0, keepdims=True)
        sums[2] += jnp.sum(gh, axis=0, keepdims=True)
        grad = mm(low, wout[...], NT).astype(LOW)
        for h in range(heads):
            gctx_scratch[h, here, :] = grad[:, h * HEAD_DIM : (h + 1) * HEAD_DIM]
    small_out[...] = jnp.zeros_like(small_out)
    for n in range(3):
        small_out[2 + n : 3 + n, :] = sums[n]
    for h in range(heads):
        first = 3 * part + h * HEAD_DIM
        weights_out[first : first + HEAD_DIM, :] = mm(ctx[h], gpb_scratch[...], TN).astype(LOW)
    anti = anti_diagonal()
    pad = jnp.zeros((BLOCK, BLOCK), WIDE)

    def head(h, carry):
        keys = k[h]
        queries = q[h]
        gpk_scratch[h] = jnp.zeros((HEAD_DIM, span), WIDE)
        gpq_scratch[h] = jnp.zeros((HEAD_DIM, span), WIDE)
        for i in range(blocks):
            i0 = i * BLOCK
            w0 = rows - BLOCK - i0
            weights = prob[h, i0 : i0 + BLOCK, :].astype(WIDE)
            gprob = mm(gctx_scratch[h, i0 : i0 + BLOCK, :], v[h], NT)
            dots = jnp.sum(weights * gprob, axis=1, keepdims=True)
            gs = (weights * (gprob - dots)).astype(LOW)
            gs_scratch[i0 : i0 + BLOCK, :] = gs
            turned = mm(anti, gs)
            moved = pltpu.roll(
                jnp.concatenate([turned, pad], axis=1), 1, 1, stride=1, stride_axis=0
            ).astype(LOW)
            table_here = tab[1, h, :, w0 : w0 + window]
            gq = (mm(turned.astype(LOW), keys) + mm(moved, table_here, NT)) * scale
            g_scratch[0, h, i0 : i0 + BLOCK, :] = mm(anti, gq.astype(LOW)).astype(LOW)
            turned_q = mm(anti, q[h, i0 : i0 + BLOCK, :]).astype(LOW)
            gpk_scratch[h, :, w0 : w0 + window] += mm(turned_q, moved, TN)
        for b in range(blocks):
            j0 = b * BLOCK
            w0 = rows - BLOCK - j0
            turned = mm(anti, gs_scratch[:, j0 : j0 + BLOCK], NT)
            moved = pltpu.roll(
                jnp.concatenate([turned, pad], axis=1), 1, 1, stride=1, stride_axis=0
            ).astype(LOW)
            table_here = tab[0, h, :, w0 : w0 + window]
            gk = (mm(turned.astype(LOW), queries) + mm(moved, table_here, NT)) * scale
            g_scratch[1, h, j0 : j0 + BLOCK, :] = mm(anti, gk.astype(LOW)).astype(LOW)
            turned_k = mm(anti, k[h, j0 : j0 + BLOCK, :]).astype(LOW)
            gpq_scratch[h, :, w0 : w0 + window] += mm(turned_k, moved, TN)
        g_scratch[2, h] = mm(prob[h], gctx_scratch[h], TN).astype(LOW)
        return carry

    lax.fori_loop(0, heads, head, 0)
    hot = one_hot(table, buckets)
    gpq = jnp.concatenate(
        [mm(hot, gpq_scratch[h].astype(LOW), NT) * scale for h in range(heads)], axis=1
    )
    gpk = jnp.concatenate(
        [mm(hot, gpk_scratch[h].astype(LOW), NT) * scale for h in range(heads)], axis=1
    )
    gpq_low, gpk_low = gpq.astype(LOW), gpk.astype(LOW)
    rel_scratch[...] = mm(gpq_low, wq[...]) + mm(gpk_low, wk[...])
    send_out[rows : rows + half, :] = rel_scratch[
        pl.ds(pl.multiple_of((1 - side) * half, half), half), :
    ].astype(LOW)
    keep_out[...] = rel_scratch[pl.ds(pl.multiple_of(side * half, half), half), :].astype(LOW)
    gq = jnp.concatenate([g_scratch[0, h] for h in range(heads)], axis=1)
    gk = jnp.concatenate([g_scratch[1, h] for h in range(heads)], axis=1)
    gv = jnp.concatenate([g_scratch[2, h] for h in range(heads)], axis=1)
    send_out[:rows, :] = (
        mm(gq, wq[...]) + mm(gk, wk[...]) + mm(gv, wv[...])
    ).astype(LOW)
    xv = x[...]
    rel = relative[...]
    weights_out[:part, :] = (mm(gq, xv, TN) + mm(gpq_low, rel, TN)).astype(LOW)
    weights_out[part : 2 * part, :] = (mm(gk, xv, TN) + mm(gpk_low, rel, TN)).astype(LOW)
    weights_out[2 * part : 3 * part, :] = mm(gv, xv, TN).astype(LOW)
    small_out[0:1, 0:part] = jnp.sum(gq.astype(WIDE), axis=0, keepdims=True) + jnp.sum(
        gpq, axis=0, keepdims=True
    )
    small_out[0:1, part : 2 * part] = jnp.sum(gk.astype(WIDE), axis=0, keepdims=True) + jnp.sum(
        gpk, axis=0, keepdims=True
    )
    small_out[1:2, 0:part] = jnp.sum(gv.astype(WIDE), axis=0, keepdims=True)


def tail_pack(
    chunk, send, got, keep, gp, weights, small_ffn, small_attn, buffer_out, grad_out
):
    rows = gp.shape[0]
    count = weights.shape[0]
    put(buffer_out, chunk, 0, 0, weights)
    both = (keep[...].astype(WIDE) + got[rows:, :].astype(WIDE)).astype(LOW)
    put(buffer_out, chunk, 0, count, both)
    count += keep.shape[0]
    small = jnp.concatenate([small_ffn[...], small_attn[...]], axis=0).astype(LOW)
    put(buffer_out, chunk, 0, count, small)
    put_zeros(buffer_out, chunk, count + small.shape[0])
    for i in range(rows // BLOCK):
        here = slice(i * BLOCK, (i + 1) * BLOCK)
        both = send[here, :].astype(WIDE) + got[here, :].astype(WIDE)
        grad_out[here, :] = (gp[here, :] + both).astype(LOW)


def add_up(got):
    acc = got[0].astype(WIDE)
    for k in range(1, got.shape[0]):
        acc += got[k].astype(WIDE)
    return acc.astype(LOW)


def reduce_near(got, sum_out):
    sum_out[...] = add_up(got)


def reduce_near_both(first, got, sum_out):
    ahead = first.shape[1]
    sum_out[:, :ahead, :] = first[...]
    sum_out[:, ahead:, :] = add_up(got)


def reduce_far(got, spread_out):
    low = add_up(got)
    for k in range(spread_out.shape[0]):
        spread_out[k] = low


def spread_near(lines, spread_out):
    for k in range(spread_out.shape[0]):
        spread_out[k] = lines[...]


def unpack(
    chunk_one, chunk_two, gathered,
    wup_out, wdown_out, bup_out, wq_out, wk_out, wv_out, wout_out, rel_out,
    bq_out, bk_out, bv_out, bout_out, again_out, ashift_out, bdown_out, fgain_out, fshift_out,
):
    inner = gathered.shape[0]
    width = gathered.shape[3]
    units = wup_out.shape[1]
    part = wq_out.shape[0]

    def rows(first, count, chunk, base):
        for place, offset, start, take in pieces(first, count, chunk):
            yield start, take, gathered[
                place % inner, place // inner, base + offset : base + offset + take, :
            ].astype(WIDE)

    for k in range(units // width):
        for start, take, value in rows(k * width, width, chunk_one, 0):
            wup_out[start : start + take, k * width : (k + 1) * width] = value
    for start, take, value in rows(units, units, chunk_one, 0):
        wdown_out[start : start + take, :] = value
    for k, out in enumerate((wq_out, wk_out, wv_out, wout_out)):
        for start, take, value in rows(k * part, part, chunk_two, chunk_one):
            out[start : start + take, :] = value
    first = 4 * part
    for start, take, value in rows(first, rel_out.shape[0], chunk_two, chunk_one):
        rel_out[start : start + take, :] = value.astype(LOW)
    first += rel_out.shape[0]
    small = jnp.concatenate([value for _, _, value in rows(first, 16, chunk_two, chunk_one)], axis=0)
    ups = units // width
    for k in range(ups):
        bup_out[k * width : (k + 1) * width] = small[k]
    bdown_out[...] = small[ups]
    fgain_out[...] = small[ups + 1]
    fshift_out[...] = small[ups + 2]
    bq_out[...] = small[8, :part]
    bk_out[...] = small[8, part:]
    bv_out[...] = small[9, :part]
    bout_out[...] = small[10]
    again_out[...] = small[11]
    ashift_out[...] = small[12]


def join_relative(mine, theirs, out):
    side = lax.axis_index("tensor")
    half = mine.shape[0]
    out[pl.ds(pl.multiple_of(side * half, half), half), :] = mine[...].astype(WIDE)
    out[pl.ds(pl.multiple_of((1 - side) * half, half), half), :] = theirs[...].astype(WIDE)


def with_statics(body, *statics):
    def wrapped(*refs):
        body(*statics, *refs)

    wrapped.__name__ = body.__name__
    return wrapped


def swap(array):
    return lax.ppermute(array, "tensor", [(0, 1), (1, 0)])


def exchange(array, groups=None):
    return lax.all_to_all(
        array, "dp", split_axis=0, concat_axis=0, tiled=True, axis_index_groups=groups
    )


def on_device(
    tokens, lengths, dealing, bucket_table, relative,
    w_query, b_query, w_key, b_key, w_value, b_value, w_out, b_out,
    attn_gain, attn_shift, w_up, b_up, w_down, b_down, ffn_gain, ffn_shift, cotangent,
):
    _, rows, width = tokens.shape
    total = dealing.shape[0]
    part = w_query.shape[1]
    heads = part // HEAD_DIM
    units = w_up.shape[1]
    half = rows // 2
    span = 2 * rows
    piece = max(16, half // total)
    spots = half // piece
    side = lax.axis_index("tensor")
    inner = 1 << ((total.bit_length()) // 2)
    outer = total // inner
    far_groups = [[o * inner + i for o in range(outer)] for i in range(inner)]
    near_groups = [[o * inner + i for i in range(inner)] for o in range(outer)]
    chunk_one = chunk_rows(2 * units, total, 8)
    chunk_two = chunk_rows(4 * part + half + 16, total, 8)
    chunk = chunk_one + chunk_two

    def cut(array):
        mine = lax.dynamic_slice_in_dim(array[0], side * half, half, 0)
        return mine.reshape(spots, piece, width)

    moving = jnp.concatenate([cut(cotangent), cut(tokens)], axis=1)
    if spots < total:
        moving = jnp.pad(moving, ((0, total - spots), (0, 0), (0, 0)))
    arrived = exchange(moving)
    (turned,) = call(
        with_statics(permute_body, piece), [(arrived.shape, LOW)], (dealing, arrived), smem=1
    )
    dealt_mine = exchange(turned)
    dealt_theirs = swap(dealt_mine)

    x = tokens[0]
    table = jnp.pad(bucket_table, (0, span - bucket_table.shape[0]), constant_values=-1)
    table = table.reshape(span // BLOCK, BLOCK)
    projections = (w_query.T, b_query, w_key.T, b_key, w_value.T, b_value, w_out)
    head_shape = (heads, rows, HEAD_DIM)
    q, k, v, tab, prob, ctx, attn_part = call(
        attention_forward,
        [(head_shape, LOW)] * 3
        + [((2, heads, HEAD_DIM, span), LOW), ((heads, rows, rows), LOW)]
        + [(head_shape, LOW), ((rows, width), LOW)],
        (lengths, x, relative, table) + projections,
        scratch=[pltpu.VMEM((rows, rows), WIDE)],
        smem=1,
        flops=10**10,
    )
    attn_got = swap(attn_part)
    ffn_weights = (b_out, attn_gain, attn_shift, w_up, b_up, w_down)
    normed, down_part, inverse, hidden, act, slope = call(
        with_statics(ffn_forward, True),
        [((rows, width), WIDE), ((rows, width), LOW), ((rows, 1), WIDE), ((rows, width), LOW),
         ((rows, units), LOW), ((rows, units), LOW)],
        (x, attn_part, attn_got) + ffn_weights,
        flops=4 * 10**9,
    )
    down_got = swap(down_part)
    buffer_one, hidden_part, gf, small_ffn = call(
        with_statics(ffn_backward, chunk_one, spots, piece),
        [((inner, outer, chunk_one, width), LOW), ((rows, width), LOW), ((rows, width), WIDE),
         ((8, width), WIDE)],
        (lengths, down_part, down_got, b_down, normed, attn_gain, attn_shift,
         ffn_gain, dealt_mine, dealt_theirs, hidden, act, slope, w_up, w_down),
        scratch=[
            pltpu.VMEM((rows, width), LOW),
            pltpu.VMEM((rows, units), LOW),
            pltpu.VMEM((rows, width), LOW),
        ],
        smem=1,
        flops=4 * 10**9,
    )
    hidden_got = swap(hidden_part)
    near_one = exchange(buffer_one, near_groups)
    send, keep, gp, weights, small_attn = call(
        attention_backward,
        [((rows + half, width), LOW), ((half, width), LOW), ((rows, width), WIDE),
         ((4 * part, width), LOW), ((8, width), WIDE)],
        (x, relative, table, w_query.T, w_key.T, w_value.T, w_out, hidden_part, hidden_got, gf,
         normed, inverse, attn_gain, q, k, v, tab, prob, ctx),
        scratch=[
            pltpu.VMEM((rows, width), LOW),
            pltpu.VMEM((rows, rows), LOW),
            pltpu.VMEM((heads, HEAD_DIM, span), WIDE),
            pltpu.VMEM((heads, HEAD_DIM, span), WIDE),
            pltpu.VMEM((3, heads, rows, HEAD_DIM), LOW),
            pltpu.VMEM((rows, width), WIDE),
            pltpu.VMEM((heads, rows, HEAD_DIM), LOW),
        ],
        flops=2 * 10**10,
    )
    sent = swap(send)
    buffer_two, grad_tokens = call(
        with_statics(tail_pack, chunk_two),
        [((inner, outer, chunk_two, width), LOW), ((rows, width), LOW)],
        (send, sent, keep, gp, weights, small_ffn, small_attn),
    )
    near_two = exchange(buffer_two, near_groups)
    (sum_one,) = call(reduce_near, [((outer, chunk_one, width), LOW)], (near_one,))
    (sums,) = call(reduce_near_both, [((outer, chunk, width), LOW)], (sum_one, near_two))
    (spread,) = call(reduce_far, [((outer, chunk, width), LOW)], (exchange(sums, far_groups),))
    lines = exchange(spread, far_groups)
    (wide,) = call(spread_near, [((inner, outer, chunk, width), LOW)], (lines,))
    gathered = exchange(wide, near_groups)

    dealt_mine, dealt_theirs, tab, _ = lax.optimization_barrier(
        (dealt_mine, dealt_theirs, tab, buffer_two)
    )
    x_dealt, attn_dealt = call(
        with_statics(attention_dealt, spots, piece),
        [((rows, width), LOW), ((rows, width), LOW)],
        (lengths, dealing, dealt_mine, dealt_theirs, tab) + projections,
        scratch=[pltpu.VMEM(head_shape, LOW) for _ in range(4)] + [pltpu.VMEM((rows, rows), WIDE)],
        smem=2,
        flops=10**10,
    )
    normed_dealt, down_dealt = call(
        with_statics(ffn_forward, False),
        [((rows, width), WIDE), ((rows, width), LOW)],
        (x_dealt, attn_dealt, swap(attn_dealt)) + ffn_weights,
        flops=4 * 10**9,
    )
    (y,) = call(
        finish_dealt,
        [((rows, width), LOW)],
        (down_dealt, swap(down_dealt), b_down, normed_dealt, attn_gain, attn_shift, ffn_gain,
         ffn_shift),
    )
    out = call(
        with_statics(unpack, chunk_one, chunk_two),
        [((width, units), WIDE), ((units, width), WIDE), ((units,), WIDE)]
        + [((part, width), WIDE)] * 4
        + [((half, width), LOW)]
        + [((part,), WIDE)] * 3
        + [((width,), WIDE)] * 6,
        (gathered,),
    )
    (g_up, g_down, g_bup, g_wq, g_wk, g_wv, g_wout, rel_half, g_bq, g_bk, g_bv, g_bout, g_again,
     g_ashift, g_bdown, g_fgain, g_fshift) = out
    (g_rel,) = call(join_relative, [((rows, width), WIDE)], (rel_half, swap(rel_half)))
    return (
        y[None], grad_tokens[None], g_rel, g_wq.T, g_bq, g_wk.T, g_bk, g_wv.T, g_bv, g_wout,
        g_bout, g_again, g_ashift, g_up, g_bup, g_down, g_bdown, g_fgain, g_fshift,
    )


def solution(mesh):
    return jax.shard_map(
        on_device,
        mesh=mesh,
        in_specs=(
            P("dp", None, None), P(), P(), P(), P(),
            P(None, "tensor"), P("tensor"), P(None, "tensor"), P("tensor"),
            P(None, "tensor"), P("tensor"), P("tensor", None), P(), P(), P(),
            P(None, "tensor"), P("tensor"), P("tensor", None), P(), P(), P(),
            P("dp", None, None),
        ),
        out_specs=(
            P("dp", None, None), P("dp", None, None), P(),
            P(None, "tensor"), P("tensor"), P(None, "tensor"), P("tensor"),
            P(None, "tensor"), P("tensor"), P("tensor", None), P(), P(), P(),
            P(None, "tensor"), P("tensor"), P("tensor", None), P(), P(), P(),
        ),
        check_vma=False,
    )
```

```python
import math

import jax
import jax.numpy as jnp
from jax import lax
from jax.experimental import pallas as pl
from jax.experimental.pallas import tpu as pltpu
from jax.sharding import PartitionSpec as P

HEAD_DIM = 64
EPSILON = 1e-07
ROOT_HALF = 0.7071067811865476
INV_ROOT_TAU = 0.3989422804014327
BLOCK = 128
LOW = jnp.bfloat16
WIDE = jnp.float32

NN = (((1,), (0,)), ((), ()))
NT = (((1,), (1,)), ((), ()))
TN = (((0,), (0,)), ((), ()))
TT = (((0,), (1,)), ((), ()))


def mm(left, right, dims=NN):
    return lax.dot_general(left, right, dims, preferred_element_type=WIDE)


def pieces(first, count, chunk):
    out = []
    done = 0
    while done < count:
        place, offset = divmod(first + done, chunk)
        take = min(chunk - offset, count - done)
        out.append((place, offset, done, take))
        done += take
    return out


def chunk_rows(rows, parts, unit):
    return -(-(-(-rows // parts)) // unit) * unit


class Part:
    def __init__(self, array, axis, start, count):
        self.array, self.axis, self.start, self.count = array, axis, start, count


class Stack:
    def __init__(self, arrays):
        self.arrays = tuple(arrays)


class Here:
    def __init__(self, *what):
        self.what = what


class Pieces:
    def __init__(self, count, shape, kind):
        self.count, self.shape, self.kind = count, shape, kind


class Fetched:
    def __init__(self, buffer, copies):
        self.buffer, self.copies = buffer, copies
        self.shape, self.dtype = buffer.shape, buffer.dtype
        for copy in copies:
            copy.start()

    def ready(self):
        for copy in self.copies:
            copy.wait()
        self.copies = ()

    def __getitem__(self, index):
        self.ready()
        return self.buffer[index]


class Shipped:
    def __init__(self, buffer, copies):
        self.buffer, self.copies, self.sent = buffer, copies, False
        self.shape, self.dtype = buffer.shape, buffer.dtype

    def send(self):
        if not self.sent:
            for copy in self.copies:
                copy.start()
        self.sent = True

    def wait(self):
        for copy in self.copies:
            copy.wait()

    def __getitem__(self, index):
        return self.buffer[index]

    def __setitem__(self, index, value):
        self.buffer[index] = value


def ready(*refs):
    for ref in refs:
        ref.ready()


def send(*refs):
    for ref in refs:
        ref.send()


def position(inner):
    index = lax.axis_index("dp")
    return index % inner


def call(body, outs, args, scratch=(), smem=0, flops=1):
    arrays, buffers, copies_in, here_in, here_out, loose = [], [], 0, set(), set(), set()
    for arg in args[smem:]:
        if isinstance(arg, Part):
            shape = list(arg.array.shape)
            shape[arg.axis] = arg.count
            arrays.append(arg.array)
            buffers.append(pltpu.VMEM(tuple(shape), arg.array.dtype))
            copies_in += 1
        elif isinstance(arg, Here):
            arrays.append(arg.what[0])
            here_in.add(len(arrays) - 1)
        elif isinstance(arg, Stack):
            first = arg.arrays[0]
            here_in.update(range(len(arrays), len(arrays) + len(arg.arrays)))
            loose.update(range(len(arrays), len(arrays) + len(arg.arrays)))
            arrays.extend(arg.arrays)
            buffers.append(pltpu.VMEM((len(arg.arrays),) + first.shape, first.dtype))
            copies_in += len(arg.arrays)
        else:
            arrays.append(arg)
            buffers.append(pltpu.VMEM(arg.shape, arg.dtype))
            copies_in += 1
    results, out_buffers, copies_out = [], [], 0
    for out in outs:
        if isinstance(out, Pieces):
            results += [pltpu.HBM(out.shape, out.kind)] * out.count
            out_buffers.append(pltpu.VMEM((out.count,) + out.shape, out.kind))
            copies_out += out.count
        elif isinstance(out, Here):
            here_out.add(len(results))
            results.append(jax.ShapeDtypeStruct(*out.what))
        else:
            results.append(pltpu.HBM(*out))
            out_buffers.append(pltpu.VMEM(*out))
            copies_out += 1

    def kernel(*refs):
        refs = list(refs)
        scalars = [refs.pop(0) for _ in range(smem)]
        sources = [refs.pop(0) for _ in arrays]
        targets = [refs.pop(0) for _ in results]
        in_sems, out_sems = refs.pop(0), refs.pop(0)
        fetched, shipped = [], []
        count = 0
        for arg in args[smem:]:
            if isinstance(arg, Here):
                fetched.append(Fetched(sources.pop(0), ()))
                continue
            buffer = refs.pop(0)
            if isinstance(arg, Stack):
                copies = []
                near = position(len(arg.arrays))
                for k in range(len(arg.arrays)):
                    copies.append(
                        pltpu.make_async_copy(
                            sources.pop(0), buffer.at[k ^ near], in_sems.at[count]
                        )
                    )
                    count += 1
            else:
                source = sources.pop(0)
                if isinstance(arg, Part):
                    window = (slice(None),) * arg.axis + (pl.ds(arg.start, arg.count),)
                    source = source.at[window]
                copies = [pltpu.make_async_copy(source, buffer, in_sems.at[count])]
                count += 1
            fetched.append(Fetched(buffer, copies))
        count = 0
        for out in outs:
            if isinstance(out, Here):
                shipped.append(Shipped(targets.pop(0), ()))
                continue
            buffer = refs.pop(0)
            if isinstance(out, Pieces):
                ends = [(buffer.at[k], targets.pop(0)) for k in range(out.count)]
            else:
                ends = [(buffer, targets.pop(0))]
            copies = []
            for source, target in ends:
                copies.append(pltpu.make_async_copy(source, target, out_sems.at[count]))
                count += 1
            shipped.append(Shipped(buffer, copies))
        body(*scalars, *fetched, *shipped, *refs)
        ready(*fetched)
        send(*shipped)
        for ship in shipped:
            ship.wait()

    kernel.__name__ = body.__name__
    space = pltpu.MemorySpace.HBM
    got = pl.pallas_call(
        kernel,
        out_shape=results,
        in_specs=[pl.BlockSpec(memory_space=pltpu.SMEM) for _ in range(smem)]
        + [
            pl.BlockSpec(memory_space=pltpu.VMEM if i in here_in - loose else pl.ANY if i in loose else space)
            for i in range(len(arrays))
        ],
        out_specs=[
            pl.BlockSpec(memory_space=pltpu.VMEM if i in here_out else space)
            for i in range(len(results))
        ],
        scratch_shapes=[
            pltpu.SemaphoreType.DMA((max(copies_in, 1),)),
            pltpu.SemaphoreType.DMA((max(copies_out, 1),)),
        ]
        + buffers
        + out_buffers
        + list(scratch),
        compiler_params=pltpu.CompilerParams(vmem_limit_bytes=40 * 1024 * 1024),
        cost_estimate=pl.CostEstimate(flops=flops, bytes_accessed=1, transcendentals=0),
    )(
        *args[:smem],
        *(
            array if i in here_in else pltpu.with_memory_space_constraint(array, space)
            for i, array in enumerate(arrays)
        ),
    )
    final = []
    for out in outs:
        if isinstance(out, Pieces):
            final.append(list(got[: out.count]))
            got = got[out.count :]
        else:
            final.append(got[0])
            got = got[1:]
    return final


def call_here(body, outs, args, smem=0):
    return pl.pallas_call(
        body,
        out_shape=[jax.ShapeDtypeStruct(shape, kind) for shape, kind in outs],
        in_specs=[
            pl.BlockSpec(memory_space=pltpu.SMEM if i < smem else pltpu.VMEM) for i in range(len(args))
        ],
        out_specs=[pl.BlockSpec(memory_space=pltpu.VMEM) for _ in outs],
    )(*args)


def permute_body(piece, dealing, source, target):
    for k in range(source.shape[0]):
        there = dealing[k]
        target[there, :piece, :] = source[k, :piece, :]
        target[k, piece:, :] = source[there, piece:, :]


def assemble(mine, theirs, spots, first, piece, target):
    side = lax.axis_index("tensor")
    half = spots * piece
    for source, base in ((mine, side * half), (theirs, (1 - side) * half)):
        for p in range(spots):
            target[pl.ds(pl.multiple_of(base + p * piece, piece), piece), :] = source[
                p, first : first + piece, :
            ]


def project(x, weights, biases, outs):
    for weight, bias, out in zip(weights, biases, outs):
        full = (mm(x, weight[...], NT) + bias[...].astype(WIDE)[None, :]).astype(LOW)
        for h in range(out.shape[0]):
            out[h] = full[:, h * HEAD_DIM : (h + 1) * HEAD_DIM]


def anti_diagonal():
    return jnp.where(
        lax.broadcasted_iota(jnp.int32, (BLOCK, BLOCK), 0)
        + lax.broadcasted_iota(jnp.int32, (BLOCK, BLOCK), 1)
        == BLOCK - 1,
        1.0,
        0.0,
    ).astype(LOW)


def one_hot(table, buckets):
    anti = anti_diagonal()
    entries = table[...]
    high = entries // 256
    turned = mm(high.astype(WIDE).astype(LOW), anti) * 256.0 + mm(
        (entries - high * 256).astype(WIDE).astype(LOW), anti
    )
    turned = turned.astype(jnp.int32)
    count = table.shape[0]
    rows = lax.broadcasted_iota(jnp.int32, (buckets, BLOCK), 0)
    return jnp.concatenate(
        [
            jnp.where(rows == turned[count - 1 - b : count - b, :], 1.0, 0.0).astype(LOW)
            for b in range(count)
        ],
        axis=1,
    )


def attend(length, q, k, v, tab, wout, ctx, attn_out, far_scratch, prob_out):
    heads, rows, _ = q.shape
    window = rows + BLOCK
    scale = 1.0 / math.sqrt(3.0 * HEAD_DIM)
    key_ok = lax.broadcasted_iota(jnp.int32, (1, rows), 1) < length

    def head(h, carry):
        keys = k[h]
        values = v[h]
        for b in range(rows // BLOCK):
            j0 = b * BLOCK
            w0 = rows - BLOCK - j0
            far = mm(k[h, j0 : j0 + BLOCK, :], tab[0, h, :, w0 : w0 + window])
            far = pltpu.roll(far, window - BLOCK, 1, stride=1, stride_axis=0)[:, :rows]
            far_scratch[:, j0 : j0 + BLOCK] = far.T
        for a in range(rows // BLOCK):
            i0 = a * BLOCK
            w0 = rows - BLOCK - i0
            block_q = q[h, i0 : i0 + BLOCK, :]
            near = mm(block_q, tab[1, h, :, w0 : w0 + window])
            near = pltpu.roll(near, window - BLOCK, 1, stride=1, stride_axis=0)[:, :rows]
            score = (mm(block_q, keys, NT) + near + far_scratch[i0 : i0 + BLOCK, :]) * scale
            score = jnp.where(key_ok, score, -1e30)
            top = jnp.max(score, axis=1, keepdims=True)
            weights = jnp.exp(score - top)
            row_ok = i0 + lax.broadcasted_iota(jnp.int32, (BLOCK, 1), 0) < length
            norm = jnp.where(row_ok, 1.0 / jnp.sum(weights, axis=1, keepdims=True), 0.0)
            prob = (weights * norm).astype(LOW)
            if prob_out is not None:
                prob_out[h, i0 : i0 + BLOCK, :] = prob
            ctx[h, i0 : i0 + BLOCK, :] = mm(prob, values).astype(LOW)
        return carry

    lax.fori_loop(0, heads, head, 0)
    total = mm(ctx[0], wout[0:HEAD_DIM, :])
    for h in range(1, heads):
        total += mm(ctx[h], wout[h * HEAD_DIM : (h + 1) * HEAD_DIM, :])
    attn_out[...] = total.astype(LOW)


def attention_forward(
    lengths, x, relative, table, wq, bq, wk, bk, wv, bv, wout,
    q_out, k_out, v_out, tab_out, prob_out, ctx_out, attn_out, far_scratch,
):
    length = lengths[lax.axis_index("dp")]
    project(x[...], (wq, wk, wv), (bq, bk, bv), (q_out, k_out, v_out))
    send(q_out, k_out, v_out)
    rel = relative[...]
    hot = one_hot(table, relative.shape[0])
    for slot, (weight, bias) in enumerate(((wq, bq), (wk, bk))):
        low = (mm(rel, weight[...], NT) + bias[...].astype(WIDE)[None, :]).astype(LOW)
        spread = mm(low, hot, TN).astype(LOW)
        for h in range(q_out.shape[0]):
            tab_out[slot, h] = spread[h * HEAD_DIM : (h + 1) * HEAD_DIM]
    send(tab_out)
    attend(length, q_out, k_out, v_out, tab_out, wout, ctx_out, attn_out, far_scratch, prob_out)


def attention_dealt(
    spots, piece, lengths, dealing, mine, theirs, tab, wq, bq, wk, bk, wv, bv, wout,
    x_out, attn_out, q, k, v, ctx, far_scratch,
):
    length = lengths[dealing[lax.axis_index("dp")]]
    assemble(mine, theirs, spots, piece, piece, x_out)
    send(x_out)
    project(x_out[...], (wq, wk, wv), (bq, bk, bv), (q, k, v))
    ready(tab)
    attend(length, q, k, v, tab, wout, ctx, attn_out, far_scratch, None)


def row_norm(values):
    center = values - jnp.mean(values, axis=-1, keepdims=True)
    inverse = lax.rsqrt(jnp.mean(center * center, axis=-1, keepdims=True) + EPSILON)
    return center * inverse, inverse


def norm_back(scaled, normed, inverse):
    one = jnp.mean(scaled, axis=-1, keepdims=True)
    two = jnp.mean(scaled * normed, axis=-1, keepdims=True)
    return inverse * (scaled - one - normed * two)


def ffn_forward(
    keep, x, mine, theirs, bout, gain, shift, wup, bup, wdown, normed_out, down_out,
    inverse_out=None, hidden_out=None, act_out=None, slope_out=None,
):
    rows = x.shape[0]
    ready(x, mine, theirs, bout, gain, shift, wup, bup, wdown)

    def block(i, carry):
        here = pl.ds(pl.multiple_of(i * BLOCK, BLOCK), BLOCK)
        attn = mine[here, :].astype(WIDE) + theirs[here, :].astype(WIDE) + wide_row(bout)
        normed, inverse = row_norm(x[here, :].astype(WIDE) + attn)
        normed_out[here, :] = normed
        low = (normed * wide_row(gain) + wide_row(shift)).astype(LOW)
        u = mm(low, wup[...]) + wide_row(bup)
        cdf = 0.5 * (1.0 + lax.erf(u * ROOT_HALF))
        act = (u * cdf).astype(LOW)
        if keep:
            inverse_out[here, :] = inverse
            hidden_out[here, :] = low
            act_out[here, :] = act
            density = jnp.exp(-0.5 * u * u) * INV_ROOT_TAU
            slope_out[here, :] = (cdf + u * density).astype(LOW)
        down_out[here, :] = mm(act, wdown[...]).astype(LOW)
        return carry

    lax.fori_loop(0, rows // BLOCK, block, 0)


def wide_row(vector):
    return vector[...].astype(WIDE)[None, :]


def second_norm(here, mine, theirs, bdown, normed, gain, shift):
    f = mine[here, :].astype(WIDE) + theirs[here, :].astype(WIDE) + wide_row(bdown)
    return row_norm(normed[here, :] * wide_row(gain) + wide_row(shift) + f)


def finish_dealt(mine, theirs, bdown, normed, gain, shift, fgain, fshift, y_out):
    for i in range(normed.shape[0] // BLOCK):
        here = slice(i * BLOCK, (i + 1) * BLOCK)
        n2, _ = second_norm(here, mine, theirs, bdown, normed, gain, shift)
        y_out[here, :] = (n2 * wide_row(fgain) + wide_row(fshift)).astype(LOW)


def put(buffer, chunk, first, value):
    near = position(buffer.shape[0])
    for place, offset, start, take in pieces(first, value.shape[0], chunk):
        buffer[place ^ near, offset : offset + take, :] = value[start : start + take]


def put_zeros(buffer, chunk, first):
    inner, _, width = buffer.shape
    left = inner * chunk - first
    if left > 0:
        put(buffer, chunk, first, jnp.zeros((left, width), buffer.dtype))


def ffn_backward(
    chunk, spots, piece, lengths,
    mine, theirs, bdown, normed, gain, shift, fgain, cot_mine, cot_theirs,
    hidden, act, slope, wup, wdown,
    part_out, gf_out, small_out, buffer_out, low_scratch, gu_scratch, cot_scratch,
):
    length = lengths[lax.axis_index("dp")]
    rows, width = normed.shape
    units = act.shape[1]
    assemble(cot_mine, cot_theirs, spots, 0, piece, cot_scratch)
    sums = [jnp.zeros((1, width), WIDE) for _ in range(3)]
    for i in range(rows // BLOCK):
        here = slice(i * BLOCK, (i + 1) * BLOCK)
        n2, r2 = second_norm(here, mine, theirs, bdown, normed, gain, shift)
        row_ok = i * BLOCK + lax.broadcasted_iota(jnp.int32, (BLOCK, 1), 0) < length
        gy = jnp.where(row_ok, cot_scratch[here, :].astype(WIDE), 0.0)
        gf = norm_back(gy * wide_row(fgain), n2, r2)
        gf_out[here, :] = gf
        low = gf.astype(LOW)
        low_scratch[here, :] = low
        sums[0] += jnp.sum(low.astype(WIDE), axis=0, keepdims=True)
        sums[1] += jnp.sum(gy * n2, axis=0, keepdims=True)
        sums[2] += jnp.sum(gy, axis=0, keepdims=True)
    send(gf_out)
    gu_sum = jnp.zeros((1, units), WIDE)
    for i in range(rows // BLOCK):
        here = slice(i * BLOCK, (i + 1) * BLOCK)
        gu = (mm(low_scratch[here, :], wdown[...], NT) * slope[here, :].astype(WIDE)).astype(LOW)
        gu_scratch[here, :] = gu
        gu_sum += jnp.sum(gu.astype(WIDE), axis=0, keepdims=True)
        part_out[here, :] = mm(gu, wup[...], NT).astype(LOW)
    send(part_out)
    small_out[...] = jnp.zeros(small_out.shape, WIDE)
    for k in range(units // width):
        small_out[k : k + 1, :] = gu_sum[:, k * width : (k + 1) * width]
    for k in range(3):
        small_out[units // width + k : units // width + k + 1, :] = sums[k]
    put(buffer_out, chunk, units, mm(act[...], low_scratch[...], TN).astype(LOW))
    for k in range(units // width):
        columns = slice(k * width, (k + 1) * width)
        put(
            buffer_out, chunk, k * width,
            mm(hidden[...], gu_scratch[:, columns], TN).astype(LOW),
        )
    put_zeros(buffer_out, chunk, 2 * units)


def head_backward(h, q, k, v, tab, prob, gctx, anti, g_out, gpq_out, gpk_out, gs_scratch, gp_scratch):
    rows = q.shape[1]
    span = tab.shape[3]
    window = rows + BLOCK
    scale = 1.0 / math.sqrt(3.0 * HEAD_DIM)
    blocks = rows // BLOCK
    pad = jnp.zeros((BLOCK, BLOCK), WIDE)
    keys = k[h]
    queries = q[h]
    gp_scratch[...] = jnp.zeros((2, HEAD_DIM, span), WIDE)
    for i in range(blocks):
        i0 = i * BLOCK
        w0 = rows - BLOCK - i0
        weights = prob[h, i0 : i0 + BLOCK, :].astype(WIDE)
        gprob = mm(gctx[h, i0 : i0 + BLOCK, :], v[h], NT)
        dots = jnp.sum(weights * gprob, axis=1, keepdims=True)
        gs = (weights * (gprob - dots)).astype(LOW)
        gs_scratch[i0 : i0 + BLOCK, :] = gs
        turned = mm(anti, gs)
        moved = pltpu.roll(
            jnp.concatenate([turned, pad], axis=1), 1, 1, stride=1, stride_axis=0
        ).astype(LOW)
        table_here = tab[1, h, :, w0 : w0 + window]
        gq = (mm(turned.astype(LOW), keys) + mm(moved, table_here, NT)) * scale
        g_out[0, h, i0 : i0 + BLOCK, :] = mm(anti, gq.astype(LOW)).astype(LOW)
        turned_q = mm(anti, q[h, i0 : i0 + BLOCK, :]).astype(LOW)
        gp_scratch[1, :, w0 : w0 + window] += mm(turned_q, moved, TN)
    for b in range(blocks):
        j0 = b * BLOCK
        w0 = rows - BLOCK - j0
        turned = mm(anti, gs_scratch[:, j0 : j0 + BLOCK], NT)
        moved = pltpu.roll(
            jnp.concatenate([turned, pad], axis=1), 1, 1, stride=1, stride_axis=0
        ).astype(LOW)
        table_here = tab[0, h, :, w0 : w0 + window]
        gk = (mm(turned.astype(LOW), queries) + mm(moved, table_here, NT)) * scale
        g_out[1, h, j0 : j0 + BLOCK, :] = mm(anti, gk.astype(LOW)).astype(LOW)
        turned_k = mm(anti, k[h, j0 : j0 + BLOCK, :]).astype(LOW)
        gp_scratch[0, :, w0 : w0 + window] += mm(turned_k, moved, TN)
    g_out[2, h] = mm(prob[h], gctx[h], TN).astype(LOW)
    gpq_out[h] = gp_scratch[0].astype(LOW)
    gpk_out[h] = gp_scratch[1].astype(LOW)


def attention_backward(
    wout, mine, theirs, gf, normed, inverse, gain, ctx, q, k, v, tab, prob,
    gp_out, wout_out, small_out, gctx_out, g_out, gpq_out, gpk_out,
    gpb_scratch, gs_scratch, gp_scratch, gctx_scratch,
):
    heads, rows, _ = ctx.shape
    width = gp_out.shape[1]
    first = q.shape[0]
    blocks = rows // BLOCK
    sums = [jnp.zeros((1, width), WIDE) for _ in range(3)]
    for i in range(blocks):
        here = slice(i * BLOCK, (i + 1) * BLOCK)
        gh = gf[here, :] + (mine[here, :].astype(WIDE) + theirs[here, :].astype(WIDE))
        n1 = normed[here, :]
        gp = norm_back(gh * wide_row(gain), n1, inverse[here, :])
        gp_out[here, :] = gp
        low = gp.astype(LOW)
        gpb_scratch[here, :] = low
        sums[0] += jnp.sum(low.astype(WIDE), axis=0, keepdims=True)
        sums[1] += jnp.sum(gh * n1, axis=0, keepdims=True)
        sums[2] += jnp.sum(gh, axis=0, keepdims=True)
        grad = mm(low, wout[...], NT).astype(LOW)
        for h in range(heads):
            part = grad[:, h * HEAD_DIM : (h + 1) * HEAD_DIM]
            if h < first:
                gctx_scratch[h, here, :] = part
            else:
                gctx_out[h - first, here, :] = part
    small_out[...] = jnp.zeros(small_out.shape, WIDE)
    for n in range(3):
        small_out[2 + n : 3 + n, :] = sums[n]
    for h in range(heads):
        wout_out[h * HEAD_DIM : (h + 1) * HEAD_DIM, :] = mm(ctx[h], gpb_scratch[...], TN).astype(LOW)
    send(gp_out, small_out, wout_out, gctx_out)
    anti = anti_diagonal()
    ready(q, k, v, tab, prob)

    def head(h, carry):
        head_backward(
            h, q, k, v, tab, prob, gctx_scratch, anti, g_out, gpq_out, gpk_out, gs_scratch, gp_scratch
        )
        return carry

    lax.fori_loop(0, first, head, 0)


def attention_backward_last(
    table, wq, wk, wv, gctx, q, k, v, tab, prob, before, gpq_before, gpk_before,
    g_out, gpq_out, gpk_out, send_out, keep_out,
    gs_scratch, gp_scratch, gpq_scratch, gpk_scratch, rel_scratch,
):
    side = lax.axis_index("tensor")
    buckets = rel_scratch.shape[0]
    half = buckets // 2
    scale = 1.0 / math.sqrt(3.0 * HEAD_DIM)
    anti = anti_diagonal()
    head_backward(
        0, q, k, v, tab, prob, gctx, anti, g_out, gpq_scratch, gpk_scratch, gs_scratch, gp_scratch
    )
    send(g_out)
    hot = one_hot(table, buckets)
    for first, here, out in (
        (gpq_before, gpq_scratch, gpq_out), (gpk_before, gpk_scratch, gpk_out)
    ):
        parts = [first[h] for h in range(first.shape[0])] + [here[0]]
        out[...] = mm(hot, jnp.concatenate(parts, axis=0), NT) * scale
    rel_scratch[...] = mm(gpq_out[...].astype(LOW), wq[...]) + mm(gpk_out[...].astype(LOW), wk[...])
    send(gpq_out, gpk_out)
    rows = buckets
    send_out[rows:, :] = rel_scratch[
        pl.ds(pl.multiple_of((1 - side) * half, half), half), :
    ].astype(LOW)
    keep_out[...] = rel_scratch[pl.ds(pl.multiple_of(side * half, half), half), :].astype(LOW)
    send_out[:rows, :] = (
        mm(together(0, before, g_out), wq[...])
        + mm(together(1, before, g_out), wk[...])
        + mm(together(2, before, g_out), wv[...])
    ).astype(LOW)


def together(slot, before, last):
    parts = [before[slot, h] for h in range(before.shape[1])] + [last[slot, 0]]
    return jnp.concatenate(parts, axis=1)


def weight_gradients(
    chunk, x, relative, before, last, gpq, gpk, wout_grad, small_ffn, small_attn, keep, got,
    buffer_out,
):
    part = gpq.shape[1]
    xv = x[...]
    rel = relative[...]
    gq, gk, gv = (together(slot, before, last) for slot in range(3))
    put(
        buffer_out, chunk, 0,
        (mm(gq, xv, TN) + mm(gpq[...].astype(LOW), rel, TN)).astype(LOW),
    )
    put(
        buffer_out, chunk, part,
        (mm(gk, xv, TN) + mm(gpk[...].astype(LOW), rel, TN)).astype(LOW),
    )
    put(buffer_out, chunk, 2 * part, mm(gv, xv, TN).astype(LOW))
    put(buffer_out, chunk, 3 * part, wout_grad[...])
    half = keep.shape[0]
    both = (keep[...].astype(WIDE) + got[got.shape[0] - half :, :].astype(WIDE)).astype(LOW)
    put(buffer_out, chunk, 4 * part, both)
    count = 4 * part + keep.shape[0]
    bias = [
        jnp.sum(gq.astype(WIDE), axis=0, keepdims=True) + jnp.sum(gpq[...], axis=0, keepdims=True),
        jnp.sum(gk.astype(WIDE), axis=0, keepdims=True) + jnp.sum(gpk[...], axis=0, keepdims=True),
        jnp.sum(gv.astype(WIDE), axis=0, keepdims=True),
    ]
    second = jnp.concatenate([bias[2], jnp.zeros_like(bias[2])], axis=1)
    small = jnp.concatenate(
        [small_ffn[...], jnp.concatenate(bias[:2], axis=1), second, small_attn[2:, :]], axis=0
    ).astype(LOW)
    put(buffer_out, chunk, count, small)
    put_zeros(buffer_out, chunk, count + small.shape[0])


def finish_tokens(gp, mine, theirs, grad_out):
    for i in range(gp.shape[0] // BLOCK):
        here = slice(i * BLOCK, (i + 1) * BLOCK)
        both = mine[here, :].astype(WIDE) + theirs[here, :].astype(WIDE)
        grad_out[here, :] = (gp[here, :] + both).astype(LOW)


def add_up(*refs):
    parts, sum_out = refs[:-1], refs[-1]
    acc = parts[0][...].astype(WIDE)
    for other in parts[1:]:
        acc += other[...].astype(WIDE)
    sum_out[...] = acc.astype(LOW)


def chunks(gathered, first, count):
    for place, offset, start, take in pieces(first, count, gathered.shape[1]):
        yield start, take, gathered[place, offset : offset + take, :].astype(WIDE)


def unpack_ffn(gathered, wup_out, wdown_out):
    width, units = wup_out.shape
    for start, take, value in chunks(gathered, units, units):
        wdown_out[start : start + take, :] = value
    send(wdown_out)
    for k in range(units // width):
        for start, take, value in chunks(gathered, k * width, width):
            wup_out[start : start + take, k * width : (k + 1) * width] = value


def unpack_relative(first, gathered, rel_out):
    for start, take, value in chunks(gathered, first, rel_out.shape[0]):
        rel_out[start : start + take, :] = value.astype(LOW)


def unpack_attention(
    first, gathered, wq_out, wk_out, wv_out, wout_out, bup_out,
    bq_out, bk_out, bv_out, bout_out, again_out, ashift_out, bdown_out, fgain_out, fshift_out,
):
    part, width = wq_out.shape
    units = bup_out.shape[0]
    for k, out in enumerate((wq_out, wk_out, wv_out, wout_out)):
        for start, take, value in chunks(gathered, k * part, part):
            out[start : start + take, :] = value
        send(out)
    small = jnp.concatenate([value for _, _, value in chunks(gathered, first, 16)], axis=0)
    ups = units // width
    for k in range(ups):
        bup_out[k * width : (k + 1) * width] = small[k]
    bdown_out[...] = small[ups]
    fgain_out[...] = small[ups + 1]
    fshift_out[...] = small[ups + 2]
    bq_out[...] = small[8, :part]
    bk_out[...] = small[8, part:]
    bv_out[...] = small[9, :part]
    bout_out[...] = small[10]
    again_out[...] = small[11]
    ashift_out[...] = small[12]


def join_relative(mine, theirs, out):
    side = lax.axis_index("tensor")
    half = mine.shape[0]
    out[pl.ds(pl.multiple_of(side * half, half), half), :] = mine[...].astype(WIDE)
    out[pl.ds(pl.multiple_of((1 - side) * half, half), half), :] = theirs[...].astype(WIDE)


def with_statics(body, *statics):
    def wrapped(*refs):
        body(*statics, *refs)

    wrapped.__name__ = body.__name__
    return wrapped


def swap(array):
    return lax.ppermute(array, "tensor", [(0, 1), (1, 0)])


def exchange(array):
    return lax.all_to_all(array, "dp", split_axis=0, concat_axis=0, tiled=True)


def trade(arrays, groups):
    got = []
    for k, array in enumerate(arrays, 1):
        pairs = [(group[p], group[p ^ k]) for group in groups for p in range(len(group))]
        got.append(lax.ppermute(array, "dp", pairs))
    return got


def after(value, *others):
    return lax.optimization_barrier((value,) + others)[0]


class Sequence:
    def __init__(self):
        self.last = None

    def run(self, body, outs, args, scratch=(), smem=0, flops=1):
        args = list(args)
        if self.last is not None:
            free = [i for i in range(smem, len(args)) if not isinstance(args[i], (Here, Stack))]
            if free:
                arg = args[free[0]]
                if isinstance(arg, Part):
                    args[free[0]] = Part(after(arg.array, self.last), arg.axis, arg.start, arg.count)
                else:
                    args[free[0]] = after(arg, self.last)
            elif isinstance(args[smem], Stack):
                first = args[smem].arrays
                args[smem] = Stack((after(first[0], self.last),) + first[1:])
            else:
                args[smem] = Here(after(args[smem].what[0], self.last))
        got = call(body, outs, args, scratch, smem, flops)
        self.last = got[0][0] if isinstance(got[0], list) else got[0]
        return got


def on_device(
    tokens, lengths, dealing, bucket_table, relative,
    w_query, b_query, w_key, b_key, w_value, b_value, w_out, b_out,
    attn_gain, attn_shift, w_up, b_up, w_down, b_down, ffn_gain, ffn_shift, cotangent,
):
    _, rows, width = tokens.shape
    total = dealing.shape[0]
    part = w_query.shape[1]
    heads = part // HEAD_DIM
    units = w_up.shape[1]
    half = rows // 2
    span = 2 * rows
    piece = max(16, half // total)
    spots = half // piece
    side = lax.axis_index("tensor")
    inner = 1 << ((total.bit_length()) // 2)
    outer = total // inner
    near_groups = [[o * inner + i for i in range(inner)] for o in range(outer)]
    chunk_one = chunk_rows(2 * units, inner, 16)
    chunk_two = chunk_rows(4 * part + half + 16, inner, 16)

    sequence = Sequence()
    run = sequence.run

    def cut(array):
        mine = lax.dynamic_slice_in_dim(array[0], side * half, half, 0)
        return mine.reshape(spots, piece, width)

    moving = jnp.concatenate([cut(cotangent), cut(tokens)], axis=1)
    if spots < total:
        moving = jnp.pad(moving, ((0, total - spots), (0, 0), (0, 0)))
    arrived = exchange(moving)
    x = tokens[0]
    table = jnp.pad(bucket_table, (0, span - bucket_table.shape[0]), constant_values=-1)
    table = table.reshape(span // BLOCK, BLOCK)
    projections = (w_query.T, b_query, w_key.T, b_key, w_value.T, b_value, w_out)
    head_shape = (heads, rows, HEAD_DIM)
    q, k, v, tab, prob, ctx, attn_part = run(
        attention_forward,
        [(head_shape, LOW)] * 3
        + [((2, heads, HEAD_DIM, span), LOW), ((heads, rows, rows), LOW)]
        + [(head_shape, LOW), Here((rows, width), LOW)],
        (lengths, x, relative, table) + projections,
        scratch=[pltpu.VMEM((rows, rows), WIDE)],
        smem=1,
    )
    arrived = after(arrived, sequence.last)
    (turned,) = call_here(
        with_statics(permute_body, piece), [(arrived.shape, LOW)], (dealing, arrived), smem=1
    )
    sequence.last = turned
    dealt_mine = exchange(turned)
    dealt_theirs = swap(dealt_mine)
    attn_got = swap(attn_part)
    ffn_weights = (b_out, attn_gain, attn_shift, w_up, b_up, w_down)
    normed, down_part, inverse, hidden, act, slope = run(
        with_statics(ffn_forward, True),
        [((rows, width), WIDE), Here((rows, width), LOW), ((rows, 1), WIDE), ((rows, width), LOW),
         ((rows, units), LOW), ((rows, units), LOW)],
        (x, Here(attn_part), Here(attn_got)) + ffn_weights,
    )
    down_got = swap(down_part)
    hidden_part, gf, small_ffn, near_one = run(
        with_statics(ffn_backward, chunk_one, spots, piece),
        [Here((rows, width), LOW), ((rows, width), WIDE), ((8, width), WIDE),
         Pieces(inner, (chunk_one, width), LOW)],
        (lengths, Here(down_part), Here(down_got), b_down, normed, attn_gain, attn_shift,
         ffn_gain, Here(dealt_mine), Here(dealt_theirs), hidden, act, slope, w_up, w_down),
        scratch=[
            pltpu.VMEM((rows, width), LOW),
            pltpu.VMEM((rows, units), LOW),
            pltpu.VMEM((rows, width), LOW),
        ],
        smem=1,
    )
    hidden_got = swap(hidden_part)
    near_one[1:] = trade(near_one[1:], near_groups)

    def total_of(own, got):
        (out,) = run(add_up, [(own.shape, LOW)], (own,) + tuple(Here(array) for array in got))
        return out

    def far_step(array, step):
        reach = inner << step
        return lax.ppermute(array, "dp", [(p, p ^ reach) for p in range(total)])

    steps = outer.bit_length() - 1

    def gather_near(line):
        return Stack([line] + trade([line] * (inner - 1), near_groups))

    before = heads - 1
    gp, wout_grad, small_attn, gctx, g_before, gpq_before, gpk_before = run(
        attention_backward,
        [((rows, width), WIDE), ((part, width), LOW), ((8, width), WIDE),
         ((1, rows, HEAD_DIM), LOW), ((3, before, rows, HEAD_DIM), LOW),
         ((before, HEAD_DIM, span), LOW), ((before, HEAD_DIM, span), LOW)],
        (w_out, Here(hidden_part), Here(hidden_got), gf, normed, inverse, attn_gain, ctx)
        + tuple(Part(array, 0, 0, before) for array in (q, k, v))
        + (Part(tab, 1, 0, before), Part(prob, 0, 0, before)),
        scratch=[
            pltpu.VMEM((rows, width), LOW),
            pltpu.VMEM((rows, rows), LOW),
            pltpu.VMEM((2, HEAD_DIM, span), WIDE),
            pltpu.VMEM((before, rows, HEAD_DIM), LOW),
        ],
    )
    line_one = total_of(near_one[0], near_one[1:])
    got_one = far_step(line_one, 0)
    g_last, gpq, gpk, send_part, rel_keep = run(
        attention_backward_last,
        [((3, 1, rows, HEAD_DIM), LOW), ((rows, part), WIDE), ((rows, part), WIDE),
         ((rows + half, width), LOW), ((half, width), LOW)],
        (table, w_query.T, w_key.T, w_value.T, gctx)
        + tuple(Part(array, 0, before, 1) for array in (q, k, v))
        + (Part(tab, 1, before, 1), Part(prob, 0, before, 1), g_before, gpq_before, gpk_before),
        scratch=[
            pltpu.VMEM((rows, rows), LOW),
            pltpu.VMEM((2, HEAD_DIM, span), WIDE),
            pltpu.VMEM((1, HEAD_DIM, span), LOW),
            pltpu.VMEM((1, HEAD_DIM, span), LOW),
            pltpu.VMEM((rows, width), WIDE),
        ],
    )
    for step in range(1, steps):
        line_one = total_of(line_one, [got_one])
        got_one = far_step(line_one, step)
    send_got = swap(after(send_part, line_one))
    (near_two,) = run(
        with_statics(weight_gradients, chunk_two),
        [Pieces(inner, (chunk_two, width), LOW)],
        (x, relative, g_before, g_last, gpq, gpk, wout_grad, small_ffn, small_attn, rel_keep,
         Here(send_got)),
    )
    near_two[1:] = trade(near_two[1:], near_groups)

    x_dealt, attn_dealt = run(
        with_statics(attention_dealt, spots, piece),
        [((rows, width), LOW), Here((rows, width), LOW)],
        (lengths, dealing, dealt_mine, dealt_theirs, tab) + projections,
        scratch=[pltpu.VMEM(head_shape, LOW) for _ in range(4)] + [pltpu.VMEM((rows, rows), WIDE)],
        smem=2,
    )
    line_two = total_of(near_two[0], near_two[1:])
    got_two = far_step(line_two, 0)
    line_one = total_of(line_one, [got_one])
    all_one = gather_near(line_one)
    attn_dealt_got = swap(after(attn_dealt, line_one))
    normed_dealt, down_dealt = run(
        with_statics(ffn_forward, False),
        [((rows, width), WIDE), Here((rows, width), LOW)],
        (x_dealt, Here(attn_dealt), Here(attn_dealt_got)) + ffn_weights,
    )
    for step in range(1, steps):
        line_two = total_of(line_two, [got_two])
        got_two = far_step(line_two, step)
    g_up, g_down = run(
        unpack_ffn, [((width, units), WIDE), ((units, width), WIDE)], (all_one,),
        flops=10**11,
    )
    down_dealt_got = swap(after(down_dealt, line_two))
    (grad_tokens,) = run(
        finish_tokens,
        [((rows, width), LOW)],
        (gp, Part(send_part, 0, 0, rows), Part(send_got, 0, 0, rows)),
    )
    (y,) = run(
        finish_dealt,
        [((rows, width), LOW)],
        (Here(down_dealt), Here(down_dealt_got), b_down, normed_dealt, attn_gain, attn_shift,
         ffn_gain, ffn_shift),
    )
    line_two = total_of(line_two, [got_two])
    all_two = gather_near(line_two)
    first = 4 * part
    (rel_half,) = run(with_statics(unpack_relative, first), [Here((half, width), LOW)], (all_two,))
    rel_other = swap(rel_half)
    g_wq, g_wk, g_wv, g_wout, g_bup, g_bq, g_bk, g_bv, g_bout, g_again, g_ashift, g_bdown, g_fgain, g_fshift = run(
        with_statics(unpack_attention, first + half),
        [((part, width), WIDE)] * 4
        + [((units,), WIDE)]
        + [((part,), WIDE)] * 3
        + [((width,), WIDE)] * 6,
        (all_two,),
    )
    (g_rel,) = run(join_relative, [((rows, width), WIDE)], (Here(rel_half), Here(rel_other)))
    return (
        y[None], grad_tokens[None], g_rel, g_wq.T, g_bq, g_wk.T, g_bk, g_wv.T, g_bv, g_wout,
        g_bout, g_again, g_ashift, g_up, g_bup, g_down, g_bdown, g_fgain, g_fshift,
    )


def solution(mesh):
    return jax.shard_map(
        on_device,
        mesh=mesh,
        in_specs=(
            P("dp", None, None), P(), P(), P(), P(),
            P(None, "tensor"), P("tensor"), P(None, "tensor"), P("tensor"),
            P(None, "tensor"), P("tensor"), P("tensor", None), P(), P(), P(),
            P(None, "tensor"), P("tensor"), P("tensor", None), P(), P(), P(),
            P("dp", None, None),
        ),
        out_specs=(
            P("dp", None, None), P("dp", None, None), P(),
            P(None, "tensor"), P("tensor"), P(None, "tensor"), P("tensor"),
            P(None, "tensor"), P("tensor"), P("tensor", None), P(), P(), P(),
            P(None, "tensor"), P("tensor"), P("tensor", None), P(), P(), P(),
        ),
        check_vma=False,
    )
```

```python
import math

import jax
import jax.numpy as jnp
from jax import lax
from jax.experimental import pallas as pl
from jax.experimental.pallas import tpu as pltpu
from jax.sharding import PartitionSpec as P

HEAD_DIM = 64
EPSILON = 1e-07
ROOT_HALF = 0.7071067811865476
INV_ROOT_TAU = 0.3989422804014327
BLOCK = 128
LOW = jnp.bfloat16
WIDE = jnp.float32

NN = (((1,), (0,)), ((), ()))
NT = (((1,), (1,)), ((), ()))
TN = (((0,), (0,)), ((), ()))
TT = (((0,), (1,)), ((), ()))


def mm(left, right, dims=NN):
    return lax.dot_general(left, right, dims, preferred_element_type=WIDE)


def pieces(first, count, chunk):
    out = []
    done = 0
    while done < count:
        place, offset = divmod(first + done, chunk)
        take = min(chunk - offset, count - done)
        out.append((place, offset, done, take))
        done += take
    return out


def chunk_rows(rows, parts, unit):
    return -(-(-(-rows // parts)) // unit) * unit


class Part:
    def __init__(self, array, axis, start, count):
        self.array, self.axis, self.start, self.count = array, axis, start, count


class Stack:
    def __init__(self, arrays):
        self.arrays = tuple(arrays)


class Here:
    def __init__(self, *what):
        self.what = what


class Pieces:
    def __init__(self, count, shape, kind):
        self.count, self.shape, self.kind = count, shape, kind


class Fetched:
    def __init__(self, buffer, copies):
        self.buffer, self.copies = buffer, copies
        self.shape, self.dtype = buffer.shape, buffer.dtype
        for copy in copies:
            copy.start()

    def ready(self):
        for copy in self.copies:
            copy.wait()
        self.copies = ()

    def __getitem__(self, index):
        self.ready()
        return self.buffer[index]


class Shipped:
    def __init__(self, buffer, copies):
        self.buffer, self.copies, self.sent = buffer, copies, False
        self.shape, self.dtype = buffer.shape, buffer.dtype

    def send(self):
        if not self.sent:
            for copy in self.copies:
                copy.start()
        self.sent = True

    def wait(self):
        for copy in self.copies:
            copy.wait()

    def __getitem__(self, index):
        return self.buffer[index]

    def __setitem__(self, index, value):
        self.buffer[index] = value


def ready(*refs):
    for ref in refs:
        ref.ready()


def send(*refs):
    for ref in refs:
        ref.send()


def position(inner):
    index = lax.axis_index("dp")
    return index % inner


def call(body, outs, args, scratch=(), smem=0, flops=1):
    arrays, buffers, copies_in, here_in, here_out, loose = [], [], 0, set(), set(), set()
    for arg in args[smem:]:
        if isinstance(arg, Part):
            shape = list(arg.array.shape)
            shape[arg.axis] = arg.count
            arrays.append(arg.array)
            buffers.append(pltpu.VMEM(tuple(shape), arg.array.dtype))
            copies_in += 1
        elif isinstance(arg, Here):
            arrays.append(arg.what[0])
            here_in.add(len(arrays) - 1)
        elif isinstance(arg, Stack):
            first = arg.arrays[0]
            here_in.update(range(len(arrays), len(arrays) + len(arg.arrays)))
            loose.update(range(len(arrays), len(arrays) + len(arg.arrays)))
            arrays.extend(arg.arrays)
            buffers.append(pltpu.VMEM((len(arg.arrays),) + first.shape, first.dtype))
            copies_in += len(arg.arrays)
        else:
            arrays.append(arg)
            buffers.append(pltpu.VMEM(arg.shape, arg.dtype))
            copies_in += 1
    results, out_buffers, copies_out = [], [], 0
    for out in outs:
        if isinstance(out, Pieces):
            results += [pltpu.HBM(out.shape, out.kind)] * out.count
            out_buffers.append(pltpu.VMEM((out.count,) + out.shape, out.kind))
            copies_out += out.count
        elif isinstance(out, Here):
            here_out.add(len(results))
            results.append(jax.ShapeDtypeStruct(*out.what))
        else:
            results.append(pltpu.HBM(*out))
            out_buffers.append(pltpu.VMEM(*out))
            copies_out += 1

    def kernel(*refs):
        refs = list(refs)
        scalars = [refs.pop(0) for _ in range(smem)]
        sources = [refs.pop(0) for _ in arrays]
        targets = [refs.pop(0) for _ in results]
        in_sems, out_sems = refs.pop(0), refs.pop(0)
        fetched, shipped = [], []
        count = 0
        for arg in args[smem:]:
            if isinstance(arg, Here):
                fetched.append(Fetched(sources.pop(0), ()))
                continue
            buffer = refs.pop(0)
            if isinstance(arg, Stack):
                copies = []
                near = position(len(arg.arrays))
                for k in range(len(arg.arrays)):
                    copies.append(
                        pltpu.make_async_copy(
                            sources.pop(0), buffer.at[k ^ near], in_sems.at[count]
                        )
                    )
                    count += 1
            else:
                source = sources.pop(0)
                if isinstance(arg, Part):
                    window = (slice(None),) * arg.axis + (pl.ds(arg.start, arg.count),)
                    source = source.at[window]
                copies = [pltpu.make_async_copy(source, buffer, in_sems.at[count])]
                count += 1
            fetched.append(Fetched(buffer, copies))
        count = 0
        for out in outs:
            if isinstance(out, Here):
                shipped.append(Shipped(targets.pop(0), ()))
                continue
            buffer = refs.pop(0)
            if isinstance(out, Pieces):
                ends = [(buffer.at[k], targets.pop(0)) for k in range(out.count)]
            else:
                ends = [(buffer, targets.pop(0))]
            copies = []
            for source, target in ends:
                copies.append(pltpu.make_async_copy(source, target, out_sems.at[count]))
                count += 1
            shipped.append(Shipped(buffer, copies))
        body(*scalars, *fetched, *shipped, *refs)
        ready(*fetched)
        send(*shipped)
        for ship in shipped:
            ship.wait()

    kernel.__name__ = body.__name__
    space = pltpu.MemorySpace.HBM
    got = pl.pallas_call(
        kernel,
        out_shape=results,
        in_specs=[pl.BlockSpec(memory_space=pltpu.SMEM) for _ in range(smem)]
        + [
            pl.BlockSpec(memory_space=pltpu.VMEM if i in here_in - loose else pl.ANY if i in loose else space)
            for i in range(len(arrays))
        ],
        out_specs=[
            pl.BlockSpec(memory_space=pltpu.VMEM if i in here_out else space)
            for i in range(len(results))
        ],
        scratch_shapes=[
            pltpu.SemaphoreType.DMA((max(copies_in, 1),)),
            pltpu.SemaphoreType.DMA((max(copies_out, 1),)),
        ]
        + buffers
        + out_buffers
        + list(scratch),
        compiler_params=pltpu.CompilerParams(vmem_limit_bytes=40 * 1024 * 1024),
        cost_estimate=pl.CostEstimate(flops=flops, bytes_accessed=1, transcendentals=0),
    )(
        *args[:smem],
        *(
            array if i in here_in else pltpu.with_memory_space_constraint(array, space)
            for i, array in enumerate(arrays)
        ),
    )
    final = []
    for out in outs:
        if isinstance(out, Pieces):
            final.append(list(got[: out.count]))
            got = got[out.count :]
        else:
            final.append(got[0])
            got = got[1:]
    return final


def call_here(body, outs, args, smem=0):
    return pl.pallas_call(
        body,
        out_shape=[jax.ShapeDtypeStruct(shape, kind) for shape, kind in outs],
        in_specs=[
            pl.BlockSpec(memory_space=pltpu.SMEM if i < smem else pltpu.VMEM) for i in range(len(args))
        ],
        out_specs=[pl.BlockSpec(memory_space=pltpu.VMEM) for _ in outs],
    )(*args)


def permute_body(piece, dealing, source, target):
    for k in range(source.shape[0]):
        there = dealing[k]
        target[there, :piece, :] = source[k, :piece, :]
        target[k, piece:, :] = source[there, piece:, :]


def assemble(mine, theirs, spots, first, piece, target):
    side = lax.axis_index("tensor")
    half = spots * piece
    for source, base in ((mine, side * half), (theirs, (1 - side) * half)):
        for p in range(spots):
            target[pl.ds(pl.multiple_of(base + p * piece, piece), piece), :] = source[
                p, first : first + piece, :
            ]


def project(x, weights, biases, outs):
    for weight, bias, out in zip(weights, biases, outs):
        full = (mm(x, weight[...], NT) + bias[...].astype(WIDE)[None, :]).astype(LOW)
        for h in range(out.shape[0]):
            out[h] = full[:, h * HEAD_DIM : (h + 1) * HEAD_DIM]


def anti_diagonal():
    return jnp.where(
        lax.broadcasted_iota(jnp.int32, (BLOCK, BLOCK), 0)
        + lax.broadcasted_iota(jnp.int32, (BLOCK, BLOCK), 1)
        == BLOCK - 1,
        1.0,
        0.0,
    ).astype(LOW)


def one_hot(table, buckets):
    anti = anti_diagonal()
    entries = table[...]
    high = entries // 256
    turned = mm(high.astype(WIDE).astype(LOW), anti) * 256.0 + mm(
        (entries - high * 256).astype(WIDE).astype(LOW), anti
    )
    turned = turned.astype(jnp.int32)
    count = table.shape[0]
    rows = lax.broadcasted_iota(jnp.int32, (buckets, BLOCK), 0)
    return jnp.concatenate(
        [
            jnp.where(rows == turned[count - 1 - b : count - b, :], 1.0, 0.0).astype(LOW)
            for b in range(count)
        ],
        axis=1,
    )


def attend(length, count, q, k, v, tab, ctx, far_scratch, prob_out):
    rows = q.shape[1]
    window = rows + BLOCK
    scale = 1.0 / math.sqrt(3.0 * HEAD_DIM)
    key_ok = lax.broadcasted_iota(jnp.int32, (1, rows), 1) < length
    blocks = [slice(i * BLOCK, (i + 1) * BLOCK) for i in range(rows // BLOCK)]

    def head(h, carry):
        for here in blocks:
            w0 = rows - BLOCK - here.start
            far = mm(k[h, here, :], tab[0, h, :, w0 : w0 + window])
            far = pltpu.roll(far, window - BLOCK, 1, stride=1, stride_axis=0)[:, :rows]
            far_scratch[:, here] = far.T
        for here in blocks:
            w0 = rows - BLOCK - here.start
            near = mm(q[h, here, :], tab[1, h, :, w0 : w0 + window])
            near = pltpu.roll(near, window - BLOCK, 1, stride=1, stride_axis=0)[:, :rows]
            far_scratch[here, :] += near
        for here in blocks:
            score = (mm(q[h, here, :], k[h], NT) + far_scratch[here, :]) * scale
            score = jnp.where(key_ok, score, -1e30)
            top = jnp.max(score, axis=1, keepdims=True)
            weights = jnp.exp(score - top)
            row_ok = here.start + lax.broadcasted_iota(jnp.int32, (BLOCK, 1), 0) < length
            norm = jnp.where(row_ok, 1.0 / jnp.sum(weights, axis=1, keepdims=True), 0.0)
            prob = (weights * norm).astype(LOW)
            if prob_out is not None:
                prob_out[h, here, :] = prob
            ctx[h, here, :] = mm(prob, v[h]).astype(LOW)
        return carry

    lax.fori_loop(0, count, head, 0)


def attention_first(
    lengths, x, relative, table, wq, bq, wk, bk, wv, bv,
    q_out, k_out, v_out, tab_out, prob_out, ctx_out, far_scratch,
):
    length = lengths[lax.axis_index("dp")]
    project(x[...], (wq, wk, wv), (bq, bk, bv), (q_out, k_out, v_out))
    send(q_out, k_out, v_out)
    rel = relative[...]
    hot = one_hot(table, relative.shape[0])
    for slot, (weight, bias) in enumerate(((wq, bq), (wk, bk))):
        low = (mm(rel, weight[...], NT) + bias[...].astype(WIDE)[None, :]).astype(LOW)
        spread = mm(low, hot, TN).astype(LOW)
        for h in range(q_out.shape[0]):
            tab_out[slot, h] = spread[h * HEAD_DIM : (h + 1) * HEAD_DIM]
    send(tab_out)
    attend(length, ctx_out.shape[0], q_out, k_out, v_out, tab_out, ctx_out, far_scratch, prob_out)


def attention_rest(
    lengths, q, k, v, tab, wout, ctx_before, prob_out, ctx_out, attn_out, far_scratch
):
    length = lengths[lax.axis_index("dp")]
    ready(q, k, v, tab)
    attend(length, q.shape[0], q, k, v, tab, ctx_out, far_scratch, prob_out)
    send(prob_out)
    heads = [ctx_before[h] for h in range(ctx_before.shape[0])]
    heads += [ctx_out[h] for h in range(q.shape[0])]
    attn_out[...] = mm(jnp.concatenate(heads, axis=1), wout[...]).astype(LOW)


def attention_dealt(
    spots, piece, lengths, dealing, mine, theirs, tab, wq, bq, wk, bk, wv, bv, wout,
    x_out, attn_out, q, k, v, ctx, far_scratch,
):
    length = lengths[dealing[lax.axis_index("dp")]]
    assemble(mine, theirs, spots, piece, piece, x_out)
    send(x_out)
    project(x_out[...], (wq, wk, wv), (bq, bk, bv), (q, k, v))
    ready(tab)
    attend(length, q.shape[0], q, k, v, tab, ctx, far_scratch, None)
    heads = [ctx[h] for h in range(q.shape[0])]
    attn_out[...] = mm(jnp.concatenate(heads, axis=1), wout[...]).astype(LOW)


def row_norm(values):
    center = values - jnp.mean(values, axis=-1, keepdims=True)
    inverse = lax.rsqrt(jnp.mean(center * center, axis=-1, keepdims=True) + EPSILON)
    return center * inverse, inverse


def norm_back(scaled, normed, inverse):
    one = jnp.mean(scaled, axis=-1, keepdims=True)
    two = jnp.mean(scaled * normed, axis=-1, keepdims=True)
    return inverse * (scaled - one - normed * two)


def ffn_forward(
    keep, x, mine, theirs, bout, gain, shift, wup, bup, wdown, normed_out, down_out, *rest
):
    low_scratch, act_scratch = rest[-2:]
    if keep:
        inverse_out, hidden_out, act_out, slope_out = rest[:4]
    rows = x.shape[0]
    blocks = [slice(i * BLOCK, (i + 1) * BLOCK) for i in range(rows // BLOCK)]
    for here in blocks:
        attn = mine[here, :].astype(WIDE) + theirs[here, :].astype(WIDE) + wide_row(bout)
        normed, inverse = row_norm(x[here, :].astype(WIDE) + attn)
        normed_out[here, :] = normed
        low = (normed * wide_row(gain) + wide_row(shift)).astype(LOW)
        low_scratch[here, :] = low
        if keep:
            inverse_out[here, :] = inverse
            hidden_out[here, :] = low
    send(normed_out)
    for here in blocks:
        u = mm(low_scratch[here, :], wup[...]) + wide_row(bup)
        cdf = 0.5 * (1.0 + lax.erf(u * ROOT_HALF))
        act = (u * cdf).astype(LOW)
        act_scratch[here, :] = act
        if keep:
            act_out[here, :] = act
            density = jnp.exp(-0.5 * u * u) * INV_ROOT_TAU
            slope_out[here, :] = (cdf + u * density).astype(LOW)
    if keep:
        send(inverse_out, hidden_out, act_out, slope_out)
    for here in blocks:
        down_out[here, :] = mm(act_scratch[here, :], wdown[...]).astype(LOW)


def wide_row(vector):
    return vector[...].astype(WIDE)[None, :]


def second_norm(here, mine, theirs, bdown, normed, gain, shift):
    f = mine[here, :].astype(WIDE) + theirs[here, :].astype(WIDE) + wide_row(bdown)
    return row_norm(normed[here, :] * wide_row(gain) + wide_row(shift) + f)


def finish_dealt(mine, theirs, bdown, normed, gain, shift, fgain, fshift, y_out):
    for i in range(normed.shape[0] // BLOCK):
        here = slice(i * BLOCK, (i + 1) * BLOCK)
        n2, _ = second_norm(here, mine, theirs, bdown, normed, gain, shift)
        y_out[here, :] = (n2 * wide_row(fgain) + wide_row(fshift)).astype(LOW)


def put(buffer, chunk, first, value):
    near = position(buffer.shape[0])
    for place, offset, start, take in pieces(first, value.shape[0], chunk):
        buffer[place ^ near, offset : offset + take, :] = value[start : start + take]


def put_zeros(buffer, chunk, first):
    inner, _, width = buffer.shape
    left = inner * chunk - first
    if left > 0:
        put(buffer, chunk, first, jnp.zeros((left, width), buffer.dtype))


def ffn_backward(
    chunk, spots, piece, lengths,
    mine, theirs, bdown, normed, gain, shift, fgain, cot_mine, cot_theirs,
    hidden, act, slope, wup, wdown,
    part_out, gf_out, small_out, buffer_out, low_scratch, gu_scratch, cot_scratch,
):
    length = lengths[lax.axis_index("dp")]
    rows, width = normed.shape
    units = act.shape[1]
    assemble(cot_mine, cot_theirs, spots, 0, piece, cot_scratch)
    sums = [jnp.zeros((1, width), WIDE) for _ in range(3)]
    for i in range(rows // BLOCK):
        here = slice(i * BLOCK, (i + 1) * BLOCK)
        n2, r2 = second_norm(here, mine, theirs, bdown, normed, gain, shift)
        row_ok = i * BLOCK + lax.broadcasted_iota(jnp.int32, (BLOCK, 1), 0) < length
        gy = jnp.where(row_ok, cot_scratch[here, :].astype(WIDE), 0.0)
        gf = norm_back(gy * wide_row(fgain), n2, r2)
        gf_out[here, :] = gf
        low = gf.astype(LOW)
        low_scratch[here, :] = low
        sums[0] += jnp.sum(low.astype(WIDE), axis=0, keepdims=True)
        sums[1] += jnp.sum(gy * n2, axis=0, keepdims=True)
        sums[2] += jnp.sum(gy, axis=0, keepdims=True)
    send(gf_out)
    gu_sum = jnp.zeros((1, units), WIDE)
    for i in range(rows // BLOCK):
        here = slice(i * BLOCK, (i + 1) * BLOCK)
        gu = (mm(low_scratch[here, :], wdown[...], NT) * slope[here, :].astype(WIDE)).astype(LOW)
        gu_scratch[here, :] = gu
        gu_sum += jnp.sum(gu.astype(WIDE), axis=0, keepdims=True)
        part_out[here, :] = mm(gu, wup[...], NT).astype(LOW)
    send(part_out)
    small_out[...] = jnp.zeros(small_out.shape, WIDE)
    for k in range(units // width):
        small_out[k : k + 1, :] = gu_sum[:, k * width : (k + 1) * width]
    for k in range(3):
        small_out[units // width + k : units // width + k + 1, :] = sums[k]
    put(buffer_out, chunk, units, mm(act[...], low_scratch[...], TN).astype(LOW))
    for k in range(units // width):
        columns = slice(k * width, (k + 1) * width)
        put(
            buffer_out, chunk, k * width,
            mm(hidden[...], gu_scratch[:, columns], TN).astype(LOW),
        )
    put_zeros(buffer_out, chunk, 2 * units)


def head_backward(
    h, q, k, v, tab, prob, gctx, anti, g_out, gpq_out, gpk_out,
    gs_scratch, gp_scratch, turned_scratch, moved_scratch,
):
    rows = q.shape[1]
    span = tab.shape[3]
    window = rows + BLOCK
    scale = 1.0 / math.sqrt(3.0 * HEAD_DIM)
    blocks = [slice(i * BLOCK, (i + 1) * BLOCK) for i in range(rows // BLOCK)]
    pad = jnp.zeros((BLOCK, BLOCK), WIDE)
    for here in blocks:
        weights = prob[h, here, :].astype(WIDE)
        gprob = mm(gctx[h, here, :], v[h], NT)
        dots = jnp.sum(weights * gprob, axis=1, keepdims=True)
        gs_scratch[here, :] = (weights * (gprob - dots)).astype(LOW)
    g_out[2, h] = mm(prob[h], gctx[h], TN).astype(LOW)
    for slot, (source, other) in enumerate(((q, k), (k, q))):
        for here in blocks:
            if slot == 0:
                turned = mm(anti, gs_scratch[here, :])
            else:
                turned = mm(anti, gs_scratch[:, here], NT)
            turned_scratch[slot, here, :] = turned.astype(LOW)
            moved_scratch[slot, here, :] = pltpu.roll(
                jnp.concatenate([turned, pad], axis=1), 1, 1, stride=1, stride_axis=0
            ).astype(LOW)
    gp_scratch[...] = jnp.zeros((2, HEAD_DIM, span), WIDE)
    for slot, (source, other) in enumerate(((q, k), (k, q))):
        for here in blocks:
            w0 = rows - BLOCK - here.start
            moved = moved_scratch[slot, here, :]
            table_here = tab[1 - slot, h, :, w0 : w0 + window]
            grad = (mm(turned_scratch[slot, here, :], other[h]) + mm(moved, table_here, NT)) * scale
            g_out[slot, h, here, :] = mm(anti, grad.astype(LOW)).astype(LOW)
            turned = mm(anti, source[h, here, :]).astype(LOW)
            gp_scratch[1 - slot, :, w0 : w0 + window] += mm(turned, moved, TN)
    gpq_out[h] = gp_scratch[0].astype(LOW)
    gpk_out[h] = gp_scratch[1].astype(LOW)


def attention_backward(
    wout, mine, theirs, gf, normed, inverse, gain, ctx, ctx_last, q, k, v, tab, prob,
    gp_out, wout_out, small_out, gctx_out, g_out, gpq_out, gpk_out,
    gpb_scratch, gctx_scratch, *scratch,
):
    first, rows, _ = ctx.shape
    heads = first + 1
    width = gp_out.shape[1]
    blocks = rows // BLOCK
    sums = [jnp.zeros((1, width), WIDE) for _ in range(3)]
    for i in range(blocks):
        here = slice(i * BLOCK, (i + 1) * BLOCK)
        gh = gf[here, :] + (mine[here, :].astype(WIDE) + theirs[here, :].astype(WIDE))
        n1 = normed[here, :]
        gp = norm_back(gh * wide_row(gain), n1, inverse[here, :])
        gp_out[here, :] = gp
        low = gp.astype(LOW)
        gpb_scratch[here, :] = low
        sums[0] += jnp.sum(low.astype(WIDE), axis=0, keepdims=True)
        sums[1] += jnp.sum(gh * n1, axis=0, keepdims=True)
        sums[2] += jnp.sum(gh, axis=0, keepdims=True)
        grad = mm(low, wout[...], NT).astype(LOW)
        for h in range(heads):
            part = grad[:, h * HEAD_DIM : (h + 1) * HEAD_DIM]
            if h < first:
                gctx_scratch[h, here, :] = part
            else:
                gctx_out[0, here, :] = part
    small_out[...] = jnp.zeros(small_out.shape, WIDE)
    for n in range(3):
        small_out[2 + n : 3 + n, :] = sums[n]
    for h in range(heads):
        wout_out[h * HEAD_DIM : (h + 1) * HEAD_DIM, :] = mm(
            ctx[h] if h < first else ctx_last[0], gpb_scratch[...], TN
        ).astype(LOW)
    send(gp_out, small_out, wout_out, gctx_out)
    anti = anti_diagonal()
    ready(q, k, v, tab, prob)

    def head(h, carry):
        head_backward(
            h, q, k, v, tab, prob, gctx_scratch, anti, g_out, gpq_out, gpk_out, *scratch
        )
        return carry

    lax.fori_loop(0, first, head, 0)


def attention_backward_last(
    table, wq, wk, wv, gctx, q, k, v, tab, prob, before, gpq_before, gpk_before,
    g_out, gpq_out, gpk_out, send_out, keep_out,
    gpq_scratch, gpk_scratch, rel_scratch, *scratch,
):
    side = lax.axis_index("tensor")
    buckets = rel_scratch.shape[0]
    half = buckets // 2
    scale = 1.0 / math.sqrt(3.0 * HEAD_DIM)
    anti = anti_diagonal()
    head_backward(
        0, q, k, v, tab, prob, gctx, anti, g_out, gpq_scratch, gpk_scratch, *scratch
    )
    send(g_out)
    hot = one_hot(table, buckets)
    for first, here, out in (
        (gpq_before, gpq_scratch, gpq_out), (gpk_before, gpk_scratch, gpk_out)
    ):
        parts = [first[h] for h in range(first.shape[0])] + [here[0]]
        out[...] = mm(hot, jnp.concatenate(parts, axis=0), NT) * scale
    rel_scratch[...] = mm(gpq_out[...].astype(LOW), wq[...]) + mm(gpk_out[...].astype(LOW), wk[...])
    send(gpq_out, gpk_out)
    rows = buckets
    send_out[rows:, :] = rel_scratch[
        pl.ds(pl.multiple_of((1 - side) * half, half), half), :
    ].astype(LOW)
    keep_out[...] = rel_scratch[pl.ds(pl.multiple_of(side * half, half), half), :].astype(LOW)
    send_out[:rows, :] = (
        mm(together(0, before, g_out), wq[...])
        + mm(together(1, before, g_out), wk[...])
        + mm(together(2, before, g_out), wv[...])
    ).astype(LOW)


def together(slot, before, last):
    parts = [before[slot, h] for h in range(before.shape[1])] + [last[slot, 0]]
    return jnp.concatenate(parts, axis=1)


def weight_gradients(
    chunk, x, relative, before, last, gpq, gpk, wout_grad, small_ffn, small_attn, keep, got,
    buffer_out,
):
    part = gpq.shape[1]
    xv = x[...]
    rel = relative[...]
    gq, gk, gv = (together(slot, before, last) for slot in range(3))
    put(
        buffer_out, chunk, 0,
        (mm(gq, xv, TN) + mm(gpq[...].astype(LOW), rel, TN)).astype(LOW),
    )
    put(
        buffer_out, chunk, part,
        (mm(gk, xv, TN) + mm(gpk[...].astype(LOW), rel, TN)).astype(LOW),
    )
    put(buffer_out, chunk, 2 * part, mm(gv, xv, TN).astype(LOW))
    put(buffer_out, chunk, 3 * part, wout_grad[...])
    half = keep.shape[0]
    both = (keep[...].astype(WIDE) + got[got.shape[0] - half :, :].astype(WIDE)).astype(LOW)
    put(buffer_out, chunk, 4 * part, both)
    count = 4 * part + keep.shape[0]
    bias = [
        jnp.sum(gq.astype(WIDE), axis=0, keepdims=True) + jnp.sum(gpq[...], axis=0, keepdims=True),
        jnp.sum(gk.astype(WIDE), axis=0, keepdims=True) + jnp.sum(gpk[...], axis=0, keepdims=True),
        jnp.sum(gv.astype(WIDE), axis=0, keepdims=True),
    ]
    second = jnp.concatenate([bias[2], jnp.zeros_like(bias[2])], axis=1)
    small = jnp.concatenate(
        [small_ffn[...], jnp.concatenate(bias[:2], axis=1), second, small_attn[2:, :]], axis=0
    ).astype(LOW)
    put(buffer_out, chunk, count, small)
    put_zeros(buffer_out, chunk, count + small.shape[0])


def finish_tokens(gp, mine, theirs, grad_out):
    for i in range(gp.shape[0] // BLOCK):
        here = slice(i * BLOCK, (i + 1) * BLOCK)
        both = mine[here, :].astype(WIDE) + theirs[here, :].astype(WIDE)
        grad_out[here, :] = (gp[here, :] + both).astype(LOW)


def chunks(gathered, first, count):
    for place, offset, start, take in pieces(first, count, gathered.shape[1]):
        yield start, take, gathered[place, offset : offset + take, :].astype(WIDE)


def unpack_ffn(gathered, wup_out, wdown_out):
    width, units = wup_out.shape
    for start, take, value in chunks(gathered, units, units):
        wdown_out[start : start + take, :] = value
    send(wdown_out)
    for k in range(units // width):
        for start, take, value in chunks(gathered, k * width, width):
            wup_out[start : start + take, k * width : (k + 1) * width] = value


def unpack_relative(first, gathered, rel_out):
    for start, take, value in chunks(gathered, first, rel_out.shape[0]):
        rel_out[start : start + take, :] = value.astype(LOW)


def unpack_attention(
    first, gathered, wq_out, wk_out, wv_out, wout_out, bup_out,
    bq_out, bk_out, bv_out, bout_out, again_out, ashift_out, bdown_out, fgain_out, fshift_out,
):
    part, width = wq_out.shape
    units = bup_out.shape[0]
    for k, out in enumerate((wq_out, wk_out, wv_out, wout_out)):
        for start, take, value in chunks(gathered, k * part, part):
            out[start : start + take, :] = value
        send(out)
    small = jnp.concatenate([value for _, _, value in chunks(gathered, first, 16)], axis=0)
    ups = units // width
    for k in range(ups):
        bup_out[k * width : (k + 1) * width] = small[k]
    bdown_out[...] = small[ups]
    fgain_out[...] = small[ups + 1]
    fshift_out[...] = small[ups + 2]
    bq_out[...] = small[8, :part]
    bk_out[...] = small[8, part:]
    bv_out[...] = small[9, :part]
    bout_out[...] = small[10]
    again_out[...] = small[11]
    ashift_out[...] = small[12]


def join_relative(mine, theirs, out):
    side = lax.axis_index("tensor")
    half = mine.shape[0]
    out[pl.ds(pl.multiple_of(side * half, half), half), :] = mine[...].astype(WIDE)
    out[pl.ds(pl.multiple_of((1 - side) * half, half), half), :] = theirs[...].astype(WIDE)


def with_statics(body, *statics):
    def wrapped(*refs):
        body(*statics, *refs)

    wrapped.__name__ = body.__name__
    return wrapped


def swap(array):
    return lax.ppermute(array, "tensor", [(0, 1), (1, 0)])


def exchange(array):
    return lax.all_to_all(array, "dp", split_axis=0, concat_axis=0, tiled=True)


def trade(arrays, groups):
    got = []
    for k, array in enumerate(arrays, 1):
        pairs = [(group[p], group[p ^ k]) for group in groups for p in range(len(group))]
        got.append(lax.ppermute(array, "dp", pairs))
    return got


def after(value, *others):
    return lax.optimization_barrier((value,) + others)[0]


class Sequence:
    def __init__(self):
        self.last = None

    def run(self, body, outs, args, scratch=(), smem=0, flops=1):
        args = list(args)
        if self.last is not None:
            free = [i for i in range(smem, len(args)) if not isinstance(args[i], (Here, Stack))]
            if free:
                arg = args[free[0]]
                if isinstance(arg, Part):
                    args[free[0]] = Part(after(arg.array, self.last), arg.axis, arg.start, arg.count)
                else:
                    args[free[0]] = after(arg, self.last)
            elif isinstance(args[smem], Stack):
                first = args[smem].arrays
                args[smem] = Stack((after(first[0], self.last),) + first[1:])
            else:
                args[smem] = Here(after(args[smem].what[0], self.last))
        got = call(body, outs, args, scratch, smem, flops)
        self.last = got[0][0] if isinstance(got[0], list) else got[0]
        return got


def on_device(
    tokens, lengths, dealing, bucket_table, relative,
    w_query, b_query, w_key, b_key, w_value, b_value, w_out, b_out,
    attn_gain, attn_shift, w_up, b_up, w_down, b_down, ffn_gain, ffn_shift, cotangent,
):
    _, rows, width = tokens.shape
    total = dealing.shape[0]
    part = w_query.shape[1]
    heads = part // HEAD_DIM
    before = heads - 1
    units = w_up.shape[1]
    half = rows // 2
    span = 2 * rows
    piece = max(16, half // total)
    spots = half // piece
    side = lax.axis_index("tensor")
    inner = 1 << ((total.bit_length()) // 2)
    outer = total // inner
    near_groups = [[o * inner + i for i in range(inner)] for o in range(outer)]
    chunk_one = chunk_rows(2 * units, inner, 16)
    chunk_two = chunk_rows(4 * part + half + 16, inner, 16)

    sequence = Sequence()
    run = sequence.run

    def cut(array):
        mine = lax.dynamic_slice_in_dim(array[0], side * half, half, 0)
        return mine.reshape(spots, piece, width)

    moving = jnp.concatenate([cut(cotangent), cut(tokens)], axis=1)
    if spots < total:
        moving = jnp.pad(moving, ((0, total - spots), (0, 0), (0, 0)))
    arrived = exchange(moving)
    x = tokens[0]
    table = jnp.pad(bucket_table, (0, span - bucket_table.shape[0]), constant_values=-1)
    table = table.reshape(span // BLOCK, BLOCK)
    projections = (w_query.T, b_query, w_key.T, b_key, w_value.T, b_value, w_out)
    head_shape = (heads, rows, HEAD_DIM)
    q, k, v, tab, prob, ctx = run(
        attention_first,
        [(head_shape, LOW)] * 3
        + [((2, heads, HEAD_DIM, span), LOW), ((before, rows, rows), LOW),
           ((before, rows, HEAD_DIM), LOW)],
        (lengths, x, relative, table) + projections[:6],
        scratch=[pltpu.VMEM((rows, rows), WIDE)],
        smem=1,
    )
    arrived = after(arrived, sequence.last)
    (turned,) = call_here(
        with_statics(permute_body, piece), [(arrived.shape, LOW)], (dealing, arrived), smem=1
    )
    sequence.last = turned
    dealt_mine = exchange(turned)
    dealt_theirs = swap(dealt_mine)
    prob_last, ctx_last, attn_part = run(
        attention_rest,
        [((1, rows, rows), LOW), ((1, rows, HEAD_DIM), LOW), Here((rows, width), LOW)],
        (lengths,)
        + tuple(Part(array, 0, before, 1) for array in (q, k, v))
        + (Part(tab, 1, before, 1), w_out, ctx),
        scratch=[pltpu.VMEM((rows, rows), WIDE)],
        smem=1,
    )
    attn_got = swap(attn_part)
    ffn_weights = (b_out, attn_gain, attn_shift, w_up, b_up, w_down)
    normed, down_part, inverse, hidden, act, slope = run(
        with_statics(ffn_forward, True),
        [((rows, width), WIDE), Here((rows, width), LOW), ((rows, 1), WIDE), ((rows, width), LOW),
         ((rows, units), LOW), ((rows, units), LOW)],
        (x, Here(attn_part), Here(attn_got)) + ffn_weights,
        scratch=[pltpu.VMEM((rows, width), LOW), pltpu.VMEM((rows, units), LOW)],
    )
    down_got = swap(down_part)
    hidden_part, gf, small_ffn, near_one = run(
        with_statics(ffn_backward, chunk_one, spots, piece),
        [Here((rows, width), LOW), ((rows, width), WIDE), ((8, width), WIDE),
         Pieces(inner, (chunk_one, width), LOW)],
        (lengths, Here(down_part), Here(down_got), b_down, normed, attn_gain, attn_shift,
         ffn_gain, Here(dealt_mine), Here(dealt_theirs), hidden, act, slope, w_up, w_down),
        scratch=[
            pltpu.VMEM((rows, width), LOW),
            pltpu.VMEM((rows, units), LOW),
            pltpu.VMEM((rows, width), LOW),
        ],
        smem=1,
    )
    hidden_got = swap(hidden_part)
    near_one[1:] = trade(near_one[1:], near_groups)

    def total_of(own, got):
        acc = after(own, sequence.last).astype(WIDE)
        for other in got:
            acc += other.astype(WIDE)
        sequence.last = acc.astype(LOW)
        return sequence.last

    def far_step(array, step):
        reach = inner << step
        return lax.ppermute(array, "dp", [(p, p ^ reach) for p in range(total)])

    steps = outer.bit_length() - 1

    def gather_near(line):
        return Stack([line] + trade([line] * (inner - 1), near_groups))

    head_scratch = [
        pltpu.VMEM((rows, rows), LOW),
        pltpu.VMEM((2, HEAD_DIM, span), WIDE),
        pltpu.VMEM((2, rows, rows), LOW),
        pltpu.VMEM((2, rows, rows + BLOCK), LOW),
    ]
    gp, wout_grad, small_attn, gctx, g_before, gpq_before, gpk_before = run(
        attention_backward,
        [((rows, width), WIDE), ((part, width), LOW), ((8, width), WIDE),
         ((1, rows, HEAD_DIM), LOW), ((3, before, rows, HEAD_DIM), LOW),
         ((before, HEAD_DIM, span), LOW), ((before, HEAD_DIM, span), LOW)],
        (w_out, Here(hidden_part), Here(hidden_got), gf, normed, inverse, attn_gain, ctx, ctx_last)
        + tuple(Part(array, 0, 0, before) for array in (q, k, v))
        + (Part(tab, 1, 0, before), prob),
        scratch=[
            pltpu.VMEM((rows, width), LOW),
            pltpu.VMEM((before, rows, HEAD_DIM), LOW),
        ]
        + head_scratch,
    )
    line_one = total_of(near_one[0], near_one[1:])
    got_one = far_step(line_one, 0)
    g_last, gpq, gpk, send_part, rel_keep = run(
        attention_backward_last,
        [((3, 1, rows, HEAD_DIM), LOW), ((rows, part), WIDE), ((rows, part), WIDE),
         ((rows + half, width), LOW), ((half, width), LOW)],
        (table, w_query.T, w_key.T, w_value.T, gctx)
        + tuple(Part(array, 0, before, 1) for array in (q, k, v))
        + (Part(tab, 1, before, 1), prob_last, g_before, gpq_before, gpk_before),
        scratch=[
            pltpu.VMEM((1, HEAD_DIM, span), LOW),
            pltpu.VMEM((1, HEAD_DIM, span), LOW),
            pltpu.VMEM((rows, width), WIDE),
        ]
        + head_scratch,
    )
    for step in range(1, steps):
        line_one = total_of(line_one, [got_one])
        got_one = far_step(line_one, step)
    send_got = swap(after(send_part, line_one))
    (near_two,) = run(
        with_statics(weight_gradients, chunk_two),
        [Pieces(inner, (chunk_two, width), LOW)],
        (x, relative, g_before, g_last, gpq, gpk, wout_grad, small_ffn, small_attn, rel_keep,
         Here(send_got)),
    )
    near_two[1:] = trade(near_two[1:], near_groups)

    x_dealt, attn_dealt = run(
        with_statics(attention_dealt, spots, piece),
        [((rows, width), LOW), Here((rows, width), LOW)],
        (lengths, dealing, dealt_mine, dealt_theirs, tab) + projections,
        scratch=[pltpu.VMEM(head_shape, LOW) for _ in range(4)] + [pltpu.VMEM((rows, rows), WIDE)],
        smem=2,
    )
    line_two = total_of(near_two[0], near_two[1:])
    got_two = far_step(line_two, 0)
    line_one = total_of(line_one, [got_one])
    all_one = gather_near(line_one)
    attn_dealt_got = swap(after(attn_dealt, line_one))
    normed_dealt, down_dealt = run(
        with_statics(ffn_forward, False),
        [((rows, width), WIDE), Here((rows, width), LOW)],
        (x_dealt, Here(attn_dealt), Here(attn_dealt_got)) + ffn_weights,
        scratch=[pltpu.VMEM((rows, width), LOW), pltpu.VMEM((rows, units), LOW)],
    )
    for step in range(1, steps):
        line_two = total_of(line_two, [got_two])
        got_two = far_step(line_two, step)
    g_up, g_down = run(
        unpack_ffn, [((width, units), WIDE), ((units, width), WIDE)], (all_one,),
        flops=10**11,
    )
    down_dealt_got = swap(after(down_dealt, line_two))
    (grad_tokens,) = run(
        finish_tokens,
        [((rows, width), LOW)],
        (gp, Part(send_part, 0, 0, rows), Part(send_got, 0, 0, rows)),
    )
    (y,) = run(
        finish_dealt,
        [((rows, width), LOW)],
        (Here(down_dealt), Here(down_dealt_got), b_down, normed_dealt, attn_gain, attn_shift,
         ffn_gain, ffn_shift),
    )
    line_two = total_of(line_two, [got_two])
    all_two = gather_near(line_two)
    first = 4 * part
    (rel_half,) = run(with_statics(unpack_relative, first), [Here((half, width), LOW)], (all_two,))
    rel_other = swap(rel_half)
    g_wq, g_wk, g_wv, g_wout, g_bup, g_bq, g_bk, g_bv, g_bout, g_again, g_ashift, g_bdown, g_fgain, g_fshift = run(
        with_statics(unpack_attention, first + half),
        [((part, width), WIDE)] * 4
        + [((units,), WIDE)]
        + [((part,), WIDE)] * 3
        + [((width,), WIDE)] * 6,
        (all_two,),
    )
    (g_rel,) = run(join_relative, [((rows, width), WIDE)], (Here(rel_half), Here(rel_other)))
    return (
        y[None], grad_tokens[None], g_rel, g_wq.T, g_bq, g_wk.T, g_bk, g_wv.T, g_bv, g_wout,
        g_bout, g_again, g_ashift, g_up, g_bup, g_down, g_bdown, g_fgain, g_fshift,
    )


def solution(mesh):
    return jax.shard_map(
        on_device,
        mesh=mesh,
        in_specs=(
            P("dp", None, None), P(), P(), P(), P(),
            P(None, "tensor"), P("tensor"), P(None, "tensor"), P("tensor"),
            P(None, "tensor"), P("tensor"), P("tensor", None), P(), P(), P(),
            P(None, "tensor"), P("tensor"), P("tensor", None), P(), P(), P(),
            P("dp", None, None),
        ),
        out_specs=(
            P("dp", None, None), P("dp", None, None), P(),
            P(None, "tensor"), P("tensor"), P(None, "tensor"), P("tensor"),
            P(None, "tensor"), P("tensor"), P("tensor", None), P(), P(), P(),
            P(None, "tensor"), P("tensor"), P("tensor", None), P(), P(), P(),
        ),
        check_vma=False,
    )
```

```python
import math

import jax
import jax.numpy as jnp
from jax import lax
from jax.experimental import pallas as pl
from jax.experimental.pallas import tpu as pltpu
from jax.sharding import PartitionSpec as P

HEAD_DIM = 64
EPSILON = 1e-07
ROOT_HALF = 0.7071067811865476
INV_ROOT_TAU = 0.3989422804014327
BLOCK = 128
LOW = jnp.bfloat16
WIDE = jnp.float32

NN = (((1,), (0,)), ((), ()))
NT = (((1,), (1,)), ((), ()))
TN = (((0,), (0,)), ((), ()))
TT = (((0,), (1,)), ((), ()))


def mm(left, right, dims=NN):
    return lax.dot_general(left, right, dims, preferred_element_type=WIDE)


def pieces(first, count, chunk):
    out = []
    done = 0
    while done < count:
        place, offset = divmod(first + done, chunk)
        take = min(chunk - offset, count - done)
        out.append((place, offset, done, take))
        done += take
    return out


def chunk_rows(rows, parts, unit):
    return -(-(-(-rows // parts)) // unit) * unit


class Part:
    def __init__(self, array, axis, start, count):
        self.array, self.axis, self.start, self.count = array, axis, start, count


class Stack:
    def __init__(self, arrays):
        self.arrays = tuple(arrays)


class Here:
    def __init__(self, *what):
        self.what = what


class Pieces:
    def __init__(self, count, shape, kind):
        self.count, self.shape, self.kind = count, shape, kind


class Fetched:
    def __init__(self, buffer, copies):
        self.buffer, self.copies = buffer, copies
        self.shape, self.dtype = buffer.shape, buffer.dtype
        for copy in copies:
            copy.start()

    def ready(self):
        for copy in self.copies:
            copy.wait()
        self.copies = ()

    def __getitem__(self, index):
        self.ready()
        return self.buffer[index]


class Shipped:
    def __init__(self, buffer, copies):
        self.buffer, self.copies, self.sent = buffer, copies, False
        self.shape, self.dtype = buffer.shape, buffer.dtype

    def send(self):
        if not self.sent:
            for copy in self.copies:
                copy.start()
        self.sent = True

    def wait(self):
        for copy in self.copies:
            copy.wait()

    def __getitem__(self, index):
        return self.buffer[index]

    def __setitem__(self, index, value):
        self.buffer[index] = value


def ready(*refs):
    for ref in refs:
        ref.ready()


def send(*refs):
    for ref in refs:
        ref.send()


def position(inner):
    index = lax.axis_index("dp")
    return index % inner


def call(body, outs, args, scratch=(), smem=0, flops=1):
    arrays, buffers, copies_in, here_in, here_out, loose = [], [], 0, set(), set(), set()
    for arg in args[smem:]:
        if isinstance(arg, Part):
            shape = list(arg.array.shape)
            shape[arg.axis] = arg.count
            arrays.append(arg.array)
            buffers.append(pltpu.VMEM(tuple(shape), arg.array.dtype))
            copies_in += 1
        elif isinstance(arg, Here):
            arrays.append(arg.what[0])
            here_in.add(len(arrays) - 1)
        elif isinstance(arg, Stack):
            first = arg.arrays[0]
            here_in.update(range(len(arrays), len(arrays) + len(arg.arrays)))
            loose.update(range(len(arrays), len(arrays) + len(arg.arrays)))
            arrays.extend(arg.arrays)
            buffers.append(pltpu.VMEM((len(arg.arrays),) + first.shape, first.dtype))
            copies_in += len(arg.arrays)
        else:
            arrays.append(arg)
            buffers.append(pltpu.VMEM(arg.shape, arg.dtype))
            copies_in += 1
    results, out_buffers, copies_out = [], [], 0
    for out in outs:
        if isinstance(out, Pieces):
            results += [pltpu.HBM(out.shape, out.kind)] * out.count
            out_buffers.append(pltpu.VMEM((out.count,) + out.shape, out.kind))
            copies_out += out.count
        elif isinstance(out, Here):
            here_out.add(len(results))
            results.append(jax.ShapeDtypeStruct(*out.what))
        else:
            results.append(pltpu.HBM(*out))
            out_buffers.append(pltpu.VMEM(*out))
            copies_out += 1

    def kernel(*refs):
        refs = list(refs)
        scalars = [refs.pop(0) for _ in range(smem)]
        sources = [refs.pop(0) for _ in arrays]
        targets = [refs.pop(0) for _ in results]
        in_sems, out_sems = refs.pop(0), refs.pop(0)
        fetched, shipped = [], []
        count = 0
        for arg in args[smem:]:
            if isinstance(arg, Here):
                fetched.append(Fetched(sources.pop(0), ()))
                continue
            buffer = refs.pop(0)
            if isinstance(arg, Stack):
                copies = []
                near = position(len(arg.arrays))
                for k in range(len(arg.arrays)):
                    copies.append(
                        pltpu.make_async_copy(
                            sources.pop(0), buffer.at[k ^ near], in_sems.at[count]
                        )
                    )
                    count += 1
            else:
                source = sources.pop(0)
                if isinstance(arg, Part):
                    window = (slice(None),) * arg.axis + (pl.ds(arg.start, arg.count),)
                    source = source.at[window]
                copies = [pltpu.make_async_copy(source, buffer, in_sems.at[count])]
                count += 1
            fetched.append(Fetched(buffer, copies))
        count = 0
        for out in outs:
            if isinstance(out, Here):
                shipped.append(Shipped(targets.pop(0), ()))
                continue
            buffer = refs.pop(0)
            if isinstance(out, Pieces):
                ends = [(buffer.at[k], targets.pop(0)) for k in range(out.count)]
            else:
                ends = [(buffer, targets.pop(0))]
            copies = []
            for source, target in ends:
                copies.append(pltpu.make_async_copy(source, target, out_sems.at[count]))
                count += 1
            shipped.append(Shipped(buffer, copies))
        body(*scalars, *fetched, *shipped, *refs)
        ready(*fetched)
        send(*shipped)
        for ship in shipped:
            ship.wait()

    kernel.__name__ = body.__name__
    space = pltpu.MemorySpace.HBM
    got = pl.pallas_call(
        kernel,
        out_shape=results,
        in_specs=[pl.BlockSpec(memory_space=pltpu.SMEM) for _ in range(smem)]
        + [
            pl.BlockSpec(memory_space=pltpu.VMEM if i in here_in - loose else pl.ANY if i in loose else space)
            for i in range(len(arrays))
        ],
        out_specs=[
            pl.BlockSpec(memory_space=pltpu.VMEM if i in here_out else space)
            for i in range(len(results))
        ],
        scratch_shapes=[
            pltpu.SemaphoreType.DMA((max(copies_in, 1),)),
            pltpu.SemaphoreType.DMA((max(copies_out, 1),)),
        ]
        + buffers
        + out_buffers
        + list(scratch),
        compiler_params=pltpu.CompilerParams(vmem_limit_bytes=40 * 1024 * 1024),
        cost_estimate=pl.CostEstimate(flops=flops, bytes_accessed=1, transcendentals=0),
    )(
        *args[:smem],
        *(
            array if i in here_in else pltpu.with_memory_space_constraint(array, space)
            for i, array in enumerate(arrays)
        ),
    )
    final = []
    for out in outs:
        if isinstance(out, Pieces):
            final.append(list(got[: out.count]))
            got = got[out.count :]
        else:
            final.append(got[0])
            got = got[1:]
    return final


def call_here(body, outs, args, smem=0):
    return pl.pallas_call(
        body,
        out_shape=[jax.ShapeDtypeStruct(shape, kind) for shape, kind in outs],
        in_specs=[
            pl.BlockSpec(memory_space=pltpu.SMEM if i < smem else pltpu.VMEM) for i in range(len(args))
        ],
        out_specs=[pl.BlockSpec(memory_space=pltpu.VMEM) for _ in outs],
        compiler_params=pltpu.CompilerParams(vmem_limit_bytes=4 * 1024 * 1024),
    )(*args)


def permute_body(piece, dealing, source, target):
    for k in range(source.shape[0]):
        there = dealing[k]
        target[there, :piece, :] = source[k, :piece, :]
        target[k, piece:, :] = source[there, piece:, :]


def assemble(mine, theirs, spots, first, piece, target):
    side = lax.axis_index("tensor")
    half = spots * piece
    for source, base in ((mine, side * half), (theirs, (1 - side) * half)):
        for p in range(spots):
            target[pl.ds(pl.multiple_of(base + p * piece, piece), piece), :] = source[
                p, first : first + piece, :
            ]


def project(x, weights, biases, outs):
    for weight, bias, out in zip(weights, biases, outs):
        full = (mm(x, weight[...], NT) + bias[...].astype(WIDE)[None, :]).astype(LOW)
        for h in range(out.shape[0]):
            out[h] = full[:, h * HEAD_DIM : (h + 1) * HEAD_DIM]


def anti_diagonal():
    return jnp.where(
        lax.broadcasted_iota(jnp.int32, (BLOCK, BLOCK), 0)
        + lax.broadcasted_iota(jnp.int32, (BLOCK, BLOCK), 1)
        == BLOCK - 1,
        1.0,
        0.0,
    ).astype(LOW)


def one_hot(table, buckets):
    anti = anti_diagonal()
    entries = table[...]
    high = entries // 256
    turned = mm(high.astype(WIDE).astype(LOW), anti) * 256.0 + mm(
        (entries - high * 256).astype(WIDE).astype(LOW), anti
    )
    turned = turned.astype(jnp.int32)
    count = table.shape[0]
    rows = lax.broadcasted_iota(jnp.int32, (buckets, BLOCK), 0)
    return jnp.concatenate(
        [
            jnp.where(rows == turned[count - 1 - b : count - b, :], 1.0, 0.0).astype(LOW)
            for b in range(count)
        ],
        axis=1,
    )


def attend(length, count, q, k, v, tab, ctx, far_scratch, prob_out):
    rows = q.shape[1]
    window = rows + BLOCK
    scale = 1.0 / math.sqrt(3.0 * HEAD_DIM)
    key_ok = lax.broadcasted_iota(jnp.int32, (1, rows), 1) < length
    blocks = [slice(i * BLOCK, (i + 1) * BLOCK) for i in range(rows // BLOCK)]

    def head(h, carry):
        for here in blocks:
            w0 = rows - BLOCK - here.start
            far = mm(k[h, here, :], tab[0, h, :, w0 : w0 + window])
            far = pltpu.roll(far, window - BLOCK, 1, stride=1, stride_axis=0)[:, :rows]
            far_scratch[:, here] = far.T
        for here in blocks:
            w0 = rows - BLOCK - here.start
            near = mm(q[h, here, :], tab[1, h, :, w0 : w0 + window])
            near = pltpu.roll(near, window - BLOCK, 1, stride=1, stride_axis=0)[:, :rows]
            far_scratch[here, :] += near
        for here in blocks:
            score = (mm(q[h, here, :], k[h], NT) + far_scratch[here, :]) * scale
            score = jnp.where(key_ok, score, -1e30)
            top = jnp.max(score, axis=1, keepdims=True)
            weights = jnp.exp(score - top)
            row_ok = here.start + lax.broadcasted_iota(jnp.int32, (BLOCK, 1), 0) < length
            norm = jnp.where(row_ok, 1.0 / jnp.sum(weights, axis=1, keepdims=True), 0.0)
            prob = (weights * norm).astype(LOW)
            if prob_out is not None:
                prob_out[h, here, :] = prob
            ctx[h, here, :] = mm(prob, v[h]).astype(LOW)
        return carry

    lax.fori_loop(0, count, head, 0)


def attention_first(
    lengths, x, relative, table, wq, bq, wk, bk, wv, bv,
    q_out, k_out, v_out, tab_out, hot_out, prob_out, ctx_out, far_scratch,
):
    length = lengths[lax.axis_index("dp")]
    project(x[...], (wq, wk, wv), (bq, bk, bv), (q_out, k_out, v_out))
    send(q_out, k_out, v_out)
    rel = relative[...]
    hot = one_hot(table, relative.shape[0])
    hot_out[...] = hot
    for slot, (weight, bias) in enumerate(((wq, bq), (wk, bk))):
        low = (mm(rel, weight[...], NT) + bias[...].astype(WIDE)[None, :]).astype(LOW)
        spread = mm(low, hot, TN).astype(LOW)
        for h in range(q_out.shape[0]):
            tab_out[slot, h] = spread[h * HEAD_DIM : (h + 1) * HEAD_DIM]
    send(tab_out, hot_out)
    attend(length, ctx_out.shape[0], q_out, k_out, v_out, tab_out, ctx_out, far_scratch, prob_out)


def attention_rest(
    lengths, q, k, v, tab, wout, ctx_before, prob_out, ctx_out, attn_out, far_scratch
):
    length = lengths[lax.axis_index("dp")]
    ready(q, k, v, tab)
    attend(length, q.shape[0], q, k, v, tab, ctx_out, far_scratch, prob_out)
    send(prob_out)
    heads = [ctx_before[h] for h in range(ctx_before.shape[0])]
    heads += [ctx_out[h] for h in range(q.shape[0])]
    attn_out[...] = mm(jnp.concatenate(heads, axis=1), wout[...]).astype(LOW)


def attention_dealt(
    spots, piece, lengths, dealing, mine, theirs, tab, wq, bq, wk, bk, wv, bv, wout,
    x_out, attn_out, q, k, v, ctx, far_scratch,
):
    length = lengths[dealing[lax.axis_index("dp")]]
    assemble(mine, theirs, spots, piece, piece, x_out)
    send(x_out)
    project(x_out[...], (wq, wk, wv), (bq, bk, bv), (q, k, v))
    ready(tab)
    attend(length, q.shape[0], q, k, v, tab, ctx, far_scratch, None)
    heads = [ctx[h] for h in range(q.shape[0])]
    attn_out[...] = mm(jnp.concatenate(heads, axis=1), wout[...]).astype(LOW)


def row_norm(values):
    center = values - jnp.mean(values, axis=-1, keepdims=True)
    inverse = lax.rsqrt(jnp.mean(center * center, axis=-1, keepdims=True) + EPSILON)
    return center * inverse, inverse


def norm_back(scaled, normed, inverse):
    one = jnp.mean(scaled, axis=-1, keepdims=True)
    two = jnp.mean(scaled * normed, axis=-1, keepdims=True)
    return inverse * (scaled - one - normed * two)


def ffn_forward(
    keep, x, mine, theirs, bout, gain, shift, wup, bup, wdown, normed_out, down_out, *rest
):
    low_scratch, act_scratch = rest[-2:]
    if keep:
        inverse_out, hidden_out, act_out, slope_out = rest[:4]
    rows = x.shape[0]
    blocks = [slice(i * BLOCK, (i + 1) * BLOCK) for i in range(rows // BLOCK)]
    for here in blocks:
        attn = mine[here, :].astype(WIDE) + theirs[here, :].astype(WIDE) + wide_row(bout)
        normed, inverse = row_norm(x[here, :].astype(WIDE) + attn)
        normed_out[here, :] = normed
        low = (normed * wide_row(gain) + wide_row(shift)).astype(LOW)
        low_scratch[here, :] = low
        if keep:
            inverse_out[here, :] = inverse
            hidden_out[here, :] = low
    send(normed_out)
    for here in blocks:
        u = mm(low_scratch[here, :], wup[...]) + wide_row(bup)
        cdf = 0.5 * (1.0 + lax.erf(u * ROOT_HALF))
        act = (u * cdf).astype(LOW)
        act_scratch[here, :] = act
        if keep:
            act_out[here, :] = act
            density = jnp.exp(-0.5 * u * u) * INV_ROOT_TAU
            slope_out[here, :] = (cdf + u * density).astype(LOW)
    if keep:
        send(inverse_out, hidden_out, act_out, slope_out)
    for here in blocks:
        down_out[here, :] = mm(act_scratch[here, :], wdown[...]).astype(LOW)


def wide_row(vector):
    return vector[...].astype(WIDE)[None, :]


def second_norm(here, mine, theirs, bdown, normed, gain, shift):
    f = mine[here, :].astype(WIDE) + theirs[here, :].astype(WIDE) + wide_row(bdown)
    return row_norm(normed[here, :] * wide_row(gain) + wide_row(shift) + f)


def finish_dealt(mine, theirs, bdown, normed, gain, shift, fgain, fshift, y_out):
    for i in range(normed.shape[0] // BLOCK):
        here = slice(i * BLOCK, (i + 1) * BLOCK)
        n2, _ = second_norm(here, mine, theirs, bdown, normed, gain, shift)
        y_out[here, :] = (n2 * wide_row(fgain) + wide_row(fshift)).astype(LOW)


def put(buffer, chunk, first, value):
    near = position(buffer.shape[0])
    for place, offset, start, take in pieces(first, value.shape[0], chunk):
        buffer[place ^ near, offset : offset + take, :] = value[start : start + take]


def put_zeros(buffer, chunk, first):
    inner, _, width = buffer.shape
    left = inner * chunk - first
    if left > 0:
        put(buffer, chunk, first, jnp.zeros((left, width), buffer.dtype))


def ffn_backward(
    chunk, spots, piece, lengths,
    mine, theirs, bdown, normed, gain, shift, fgain, cot_mine, cot_theirs,
    hidden, act, slope, wup, wdown,
    part_out, gf_out, small_out, buffer_out, low_scratch, gu_scratch, cot_scratch,
):
    length = lengths[lax.axis_index("dp")]
    rows, width = normed.shape
    units = act.shape[1]
    assemble(cot_mine, cot_theirs, spots, 0, piece, cot_scratch)
    sums = [jnp.zeros((1, width), WIDE) for _ in range(3)]
    for i in range(rows // BLOCK):
        here = slice(i * BLOCK, (i + 1) * BLOCK)
        n2, r2 = second_norm(here, mine, theirs, bdown, normed, gain, shift)
        row_ok = i * BLOCK + lax.broadcasted_iota(jnp.int32, (BLOCK, 1), 0) < length
        gy = jnp.where(row_ok, cot_scratch[here, :].astype(WIDE), 0.0)
        gf = norm_back(gy * wide_row(fgain), n2, r2)
        gf_out[here, :] = gf
        low = gf.astype(LOW)
        low_scratch[here, :] = low
        sums[0] += jnp.sum(low.astype(WIDE), axis=0, keepdims=True)
        sums[1] += jnp.sum(gy * n2, axis=0, keepdims=True)
        sums[2] += jnp.sum(gy, axis=0, keepdims=True)
    send(gf_out)
    gu_sum = jnp.zeros((1, units), WIDE)
    for i in range(rows // BLOCK):
        here = slice(i * BLOCK, (i + 1) * BLOCK)
        gu = (mm(low_scratch[here, :], wdown[...], NT) * slope[here, :].astype(WIDE)).astype(LOW)
        gu_scratch[here, :] = gu
        gu_sum += jnp.sum(gu.astype(WIDE), axis=0, keepdims=True)
        part_out[here, :] = mm(gu, wup[...], NT).astype(LOW)
    send(part_out)
    small_out[...] = jnp.zeros(small_out.shape, WIDE)
    for k in range(units // width):
        small_out[k : k + 1, :] = gu_sum[:, k * width : (k + 1) * width]
    for k in range(3):
        small_out[units // width + k : units // width + k + 1, :] = sums[k]
    put(buffer_out, chunk, units, mm(act[...], low_scratch[...], TN).astype(LOW))
    for k in range(units // width):
        columns = slice(k * width, (k + 1) * width)
        put(
            buffer_out, chunk, k * width,
            mm(hidden[...], gu_scratch[:, columns], TN).astype(LOW),
        )
    put_zeros(buffer_out, chunk, 2 * units)


def head_backward(
    h, q, k, v, tab, prob, gctx, anti, g_out, gpq_out, gpk_out,
    gs_scratch, gp_scratch, turned_scratch, moved_scratch,
):
    rows = q.shape[1]
    span = tab.shape[3]
    window = rows + BLOCK
    scale = 1.0 / math.sqrt(3.0 * HEAD_DIM)
    blocks = [slice(i * BLOCK, (i + 1) * BLOCK) for i in range(rows // BLOCK)]
    pad = jnp.zeros((BLOCK, BLOCK), WIDE)
    for here in blocks:
        weights = prob[h, here, :].astype(WIDE)
        gprob = mm(gctx[h, here, :], v[h], NT)
        dots = jnp.sum(weights * gprob, axis=1, keepdims=True)
        gs_scratch[here, :] = (weights * (gprob - dots)).astype(LOW)
    g_out[2, h] = mm(prob[h], gctx[h], TN).astype(LOW)
    for slot, (source, other) in enumerate(((q, k), (k, q))):
        for here in blocks:
            if slot == 0:
                turned = mm(anti, gs_scratch[here, :])
            else:
                turned = mm(anti, gs_scratch[:, here], NT)
            turned_scratch[slot, here, :] = turned.astype(LOW)
            moved_scratch[slot, here, :] = pltpu.roll(
                jnp.concatenate([turned, pad], axis=1), 1, 1, stride=1, stride_axis=0
            ).astype(LOW)
    gp_scratch[...] = jnp.zeros((2, HEAD_DIM, span), WIDE)
    for slot, (source, other) in enumerate(((q, k), (k, q))):
        for here in blocks:
            w0 = rows - BLOCK - here.start
            moved = moved_scratch[slot, here, :]
            table_here = tab[1 - slot, h, :, w0 : w0 + window]
            grad = (mm(turned_scratch[slot, here, :], other[h]) + mm(moved, table_here, NT)) * scale
            g_out[slot, h, here, :] = mm(anti, grad.astype(LOW)).astype(LOW)
            turned = mm(anti, source[h, here, :]).astype(LOW)
            gp_scratch[1 - slot, :, w0 : w0 + window] += mm(turned, moved, TN)
    gpq_out[h] = gp_scratch[0].astype(LOW)
    gpk_out[h] = gp_scratch[1].astype(LOW)


def attention_backward(
    wout, mine, theirs, gf, normed, inverse, gain, ctx, ctx_last, q, k, v, tab, prob,
    gp_out, wout_out, small_out, gctx_out, g_out, gpq_out, gpk_out,
    gpb_scratch, gctx_scratch, *scratch,
):
    first, rows, _ = ctx.shape
    heads = first + 1
    width = gp_out.shape[1]
    blocks = rows // BLOCK
    sums = [jnp.zeros((1, width), WIDE) for _ in range(3)]
    for i in range(blocks):
        here = slice(i * BLOCK, (i + 1) * BLOCK)
        gh = gf[here, :] + (mine[here, :].astype(WIDE) + theirs[here, :].astype(WIDE))
        n1 = normed[here, :]
        gp = norm_back(gh * wide_row(gain), n1, inverse[here, :])
        gp_out[here, :] = gp
        low = gp.astype(LOW)
        gpb_scratch[here, :] = low
        sums[0] += jnp.sum(low.astype(WIDE), axis=0, keepdims=True)
        sums[1] += jnp.sum(gh * n1, axis=0, keepdims=True)
        sums[2] += jnp.sum(gh, axis=0, keepdims=True)
        grad = mm(low, wout[...], NT).astype(LOW)
        for h in range(heads):
            part = grad[:, h * HEAD_DIM : (h + 1) * HEAD_DIM]
            if h < first:
                gctx_scratch[h, here, :] = part
            else:
                gctx_out[0, here, :] = part
    small_out[...] = jnp.zeros(small_out.shape, WIDE)
    for n in range(3):
        small_out[2 + n : 3 + n, :] = sums[n]
    for h in range(heads):
        wout_out[h * HEAD_DIM : (h + 1) * HEAD_DIM, :] = mm(
            ctx[h] if h < first else ctx_last[0], gpb_scratch[...], TN
        ).astype(LOW)
    send(gp_out, small_out, wout_out, gctx_out)
    anti = anti_diagonal()
    ready(q, k, v, tab, prob)

    def head(h, carry):
        head_backward(
            h, q, k, v, tab, prob, gctx_scratch, anti, g_out, gpq_out, gpk_out, *scratch
        )
        return carry

    lax.fori_loop(0, first, head, 0)


def attention_backward_last(
    hot, wq, wk, wv, gctx, q, k, v, tab, prob, before, gpq_before, gpk_before,
    g_out, gpq_out, gpk_out, send_out, keep_out,
    gpq_scratch, gpk_scratch, rel_scratch, *scratch,
):
    side = lax.axis_index("tensor")
    buckets = rel_scratch.shape[0]
    half = buckets // 2
    scale = 1.0 / math.sqrt(3.0 * HEAD_DIM)
    anti = anti_diagonal()
    head_backward(
        0, q, k, v, tab, prob, gctx, anti, g_out, gpq_scratch, gpk_scratch, *scratch
    )
    send(g_out)
    for first, here, out in (
        (gpq_before, gpq_scratch, gpq_out), (gpk_before, gpk_scratch, gpk_out)
    ):
        parts = [first[h] for h in range(first.shape[0])] + [here[0]]
        out[...] = mm(hot[...], jnp.concatenate(parts, axis=0), NT) * scale
    rel_scratch[...] = mm(gpq_out[...].astype(LOW), wq[...]) + mm(gpk_out[...].astype(LOW), wk[...])
    send(gpq_out, gpk_out)
    rows = buckets
    send_out[rows:, :] = rel_scratch[
        pl.ds(pl.multiple_of((1 - side) * half, half), half), :
    ].astype(LOW)
    keep_out[...] = rel_scratch[pl.ds(pl.multiple_of(side * half, half), half), :].astype(LOW)
    send_out[:rows, :] = (
        mm(together(0, before, g_out), wq[...])
        + mm(together(1, before, g_out), wk[...])
        + mm(together(2, before, g_out), wv[...])
    ).astype(LOW)


def together(slot, before, last):
    parts = [before[slot, h] for h in range(before.shape[1])] + [last[slot, 0]]
    return jnp.concatenate(parts, axis=1)


def weight_gradients(
    chunk, x, relative, before, last, gpq, gpk, wout_grad, small_ffn, small_attn, keep, got,
    buffer_out,
):
    part = gpq.shape[1]
    xv = x[...]
    rel = relative[...]
    gq, gk, gv = (together(slot, before, last) for slot in range(3))
    put(
        buffer_out, chunk, 0,
        (mm(gq, xv, TN) + mm(gpq[...].astype(LOW), rel, TN)).astype(LOW),
    )
    put(
        buffer_out, chunk, part,
        (mm(gk, xv, TN) + mm(gpk[...].astype(LOW), rel, TN)).astype(LOW),
    )
    put(buffer_out, chunk, 2 * part, mm(gv, xv, TN).astype(LOW))
    put(buffer_out, chunk, 3 * part, wout_grad[...])
    half = keep.shape[0]
    both = (keep[...].astype(WIDE) + got[got.shape[0] - half :, :].astype(WIDE)).astype(LOW)
    put(buffer_out, chunk, 4 * part, both)
    count = 4 * part + keep.shape[0]
    bias = [
        jnp.sum(gq.astype(WIDE), axis=0, keepdims=True) + jnp.sum(gpq[...], axis=0, keepdims=True),
        jnp.sum(gk.astype(WIDE), axis=0, keepdims=True) + jnp.sum(gpk[...], axis=0, keepdims=True),
        jnp.sum(gv.astype(WIDE), axis=0, keepdims=True),
    ]
    second = jnp.concatenate([bias[2], jnp.zeros_like(bias[2])], axis=1)
    small = jnp.concatenate(
        [small_ffn[...], jnp.concatenate(bias[:2], axis=1), second, small_attn[2:, :]], axis=0
    ).astype(LOW)
    put(buffer_out, chunk, count, small)
    put_zeros(buffer_out, chunk, count + small.shape[0])


def finish_tokens(gp, mine, theirs, grad_out):
    for i in range(gp.shape[0] // BLOCK):
        here = slice(i * BLOCK, (i + 1) * BLOCK)
        both = mine[here, :].astype(WIDE) + theirs[here, :].astype(WIDE)
        grad_out[here, :] = (gp[here, :] + both).astype(LOW)


def chunks(gathered, first, count):
    for place, offset, start, take in pieces(first, count, gathered.shape[1]):
        yield start, take, gathered[place, offset : offset + take, :].astype(WIDE)


def unpack_ffn(gathered, wup_out, wdown_out):
    width, units = wup_out.shape
    for start, take, value in chunks(gathered, units, units):
        wdown_out[start : start + take, :] = value
    send(wdown_out)
    for k in range(units // width):
        for start, take, value in chunks(gathered, k * width, width):
            wup_out[start : start + take, k * width : (k + 1) * width] = value


def unpack_relative(first, gathered, rel_out):
    for start, take, value in chunks(gathered, first, rel_out.shape[0]):
        rel_out[start : start + take, :] = value.astype(LOW)


def unpack_attention(
    first, gathered, wq_out, wk_out, wv_out, wout_out, bup_out,
    bq_out, bk_out, bv_out, bout_out, again_out, ashift_out, bdown_out, fgain_out, fshift_out,
):
    part, width = wq_out.shape
    units = bup_out.shape[0]
    for k, out in enumerate((wq_out, wk_out, wv_out, wout_out)):
        for start, take, value in chunks(gathered, k * part, part):
            out[start : start + take, :] = value
        send(out)
    small = jnp.concatenate([value for _, _, value in chunks(gathered, first, 16)], axis=0)
    ups = units // width
    for k in range(ups):
        bup_out[k * width : (k + 1) * width] = small[k]
    bdown_out[...] = small[ups]
    fgain_out[...] = small[ups + 1]
    fshift_out[...] = small[ups + 2]
    bq_out[...] = small[8, :part]
    bk_out[...] = small[8, part:]
    bv_out[...] = small[9, :part]
    bout_out[...] = small[10]
    again_out[...] = small[11]
    ashift_out[...] = small[12]


def join_relative(mine, theirs, out):
    side = lax.axis_index("tensor")
    half = mine.shape[0]
    out[pl.ds(pl.multiple_of(side * half, half), half), :] = mine[...].astype(WIDE)
    out[pl.ds(pl.multiple_of((1 - side) * half, half), half), :] = theirs[...].astype(WIDE)


def with_statics(body, *statics):
    def wrapped(*refs):
        body(*statics, *refs)

    wrapped.__name__ = body.__name__
    return wrapped


def swap(array):
    return lax.ppermute(array, "tensor", [(0, 1), (1, 0)])


def exchange(array):
    return lax.all_to_all(array, "dp", split_axis=0, concat_axis=0, tiled=True)


def trade(arrays, groups):
    got = []
    for k, array in enumerate(arrays, 1):
        pairs = [(group[p], group[p ^ k]) for group in groups for p in range(len(group))]
        got.append(lax.ppermute(array, "dp", pairs))
    return got


def after(value, *others):
    return lax.optimization_barrier((value,) + others)[0]


class Sequence:
    def __init__(self):
        self.last = None

    def run(self, body, outs, args, scratch=(), smem=0, flops=1):
        args = list(args)
        if self.last is not None:
            free = [i for i in range(smem, len(args)) if not isinstance(args[i], (Here, Stack))]
            if free:
                arg = args[free[0]]
                if isinstance(arg, Part):
                    args[free[0]] = Part(after(arg.array, self.last), arg.axis, arg.start, arg.count)
                else:
                    args[free[0]] = after(arg, self.last)
            elif isinstance(args[smem], Stack):
                first = args[smem].arrays
                args[smem] = Stack((after(first[0], self.last),) + first[1:])
            else:
                args[smem] = Here(after(args[smem].what[0], self.last))
        got = call(body, outs, args, scratch, smem, flops)
        self.last = got[0][0] if isinstance(got[0], list) else got[0]
        return got


def on_device(
    tokens, lengths, dealing, bucket_table, relative,
    w_query, b_query, w_key, b_key, w_value, b_value, w_out, b_out,
    attn_gain, attn_shift, w_up, b_up, w_down, b_down, ffn_gain, ffn_shift, cotangent,
):
    _, rows, width = tokens.shape
    total = dealing.shape[0]
    part = w_query.shape[1]
    heads = part // HEAD_DIM
    before = heads - 1
    units = w_up.shape[1]
    half = rows // 2
    span = 2 * rows
    piece = max(16, half // total)
    spots = half // piece
    side = lax.axis_index("tensor")
    inner = 1 << ((total.bit_length()) // 2)
    outer = total // inner
    near_groups = [[o * inner + i for i in range(inner)] for o in range(outer)]
    chunk_one = chunk_rows(2 * units, inner, 16)
    chunk_two = chunk_rows(4 * part + half + 16, inner, 16)

    sequence = Sequence()
    run = sequence.run

    def cut(array):
        mine = lax.dynamic_slice_in_dim(array[0], side * half, half, 0)
        return mine.reshape(spots, piece, width)

    moving = jnp.concatenate([cut(cotangent), cut(tokens)], axis=1)
    if spots < total:
        moving = jnp.pad(moving, ((0, total - spots), (0, 0), (0, 0)))
    arrived = exchange(moving)
    x = tokens[0]
    table = jnp.pad(bucket_table, (0, span - bucket_table.shape[0]), constant_values=-1)
    table = table.reshape(span // BLOCK, BLOCK)
    projections = (w_query.T, b_query, w_key.T, b_key, w_value.T, b_value, w_out)
    head_shape = (heads, rows, HEAD_DIM)
    q, k, v, tab, hot, prob, ctx = run(
        attention_first,
        [(head_shape, LOW)] * 3
        + [((2, heads, HEAD_DIM, span), LOW), ((relative.shape[0], span), LOW), ((before, rows, rows), LOW),
           ((before, rows, HEAD_DIM), LOW)],
        (lengths, x, relative, table) + projections[:6],
        scratch=[pltpu.VMEM((rows, rows), WIDE)],
        smem=1,
    )
    arrived = after(arrived, sequence.last)
    (turned,) = call_here(
        with_statics(permute_body, piece), [(arrived.shape, LOW)], (dealing, arrived), smem=1
    )
    sequence.last = turned
    dealt_mine = exchange(turned)
    dealt_theirs = swap(dealt_mine)
    prob_last, ctx_last, attn_part = run(
        attention_rest,
        [((1, rows, rows), LOW), ((1, rows, HEAD_DIM), LOW), Here((rows, width), LOW)],
        (lengths,)
        + tuple(Part(array, 0, before, 1) for array in (q, k, v))
        + (Part(tab, 1, before, 1), w_out, ctx),
        scratch=[pltpu.VMEM((rows, rows), WIDE)],
        smem=1,
    )
    attn_got = swap(attn_part)
    ffn_weights = (b_out, attn_gain, attn_shift, w_up, b_up, w_down)
    normed, down_part, inverse, hidden, act, slope = run(
        with_statics(ffn_forward, True),
        [((rows, width), WIDE), Here((rows, width), LOW), ((rows, 1), WIDE), ((rows, width), LOW),
         ((rows, units), LOW), ((rows, units), LOW)],
        (x, Here(attn_part), Here(attn_got)) + ffn_weights,
        scratch=[pltpu.VMEM((rows, width), LOW), pltpu.VMEM((rows, units), LOW)],
    )
    down_got = swap(down_part)
    hidden_part, gf, small_ffn, near_one = run(
        with_statics(ffn_backward, chunk_one, spots, piece),
        [Here((rows, width), LOW), ((rows, width), WIDE), ((8, width), WIDE),
         Pieces(inner, (chunk_one, width), LOW)],
        (lengths, Here(down_part), Here(down_got), b_down, normed, attn_gain, attn_shift,
         ffn_gain, Here(dealt_mine), Here(dealt_theirs), hidden, act, slope, w_up, w_down),
        scratch=[
            pltpu.VMEM((rows, width), LOW),
            pltpu.VMEM((rows, units), LOW),
            pltpu.VMEM((rows, width), LOW),
        ],
        smem=1,
    )
    hidden_got = swap(hidden_part)
    near_one[1:] = trade(near_one[1:], near_groups)

    def total_of(own, got):
        acc = after(own, sequence.last).astype(WIDE)
        for other in got:
            acc += other.astype(WIDE)
        sequence.last = acc.astype(LOW)
        return sequence.last

    def far_step(array, step):
        reach = inner << step
        return lax.ppermute(array, "dp", [(p, p ^ reach) for p in range(total)])

    steps = outer.bit_length() - 1

    def gather_near(line):
        return Stack([line] + trade([line] * (inner - 1), near_groups))

    head_scratch = [
        pltpu.VMEM((rows, rows), LOW),
        pltpu.VMEM((2, HEAD_DIM, span), WIDE),
        pltpu.VMEM((2, rows, rows), LOW),
        pltpu.VMEM((2, rows, rows + BLOCK), LOW),
    ]
    gp, wout_grad, small_attn, gctx, g_before, gpq_before, gpk_before = run(
        attention_backward,
        [((rows, width), WIDE), ((part, width), LOW), ((8, width), WIDE),
         ((1, rows, HEAD_DIM), LOW), ((3, before, rows, HEAD_DIM), LOW),
         ((before, HEAD_DIM, span), LOW), ((before, HEAD_DIM, span), LOW)],
        (w_out, Here(hidden_part), Here(hidden_got), gf, normed, inverse, attn_gain, ctx, ctx_last)
        + tuple(Part(array, 0, 0, before) for array in (q, k, v))
        + (Part(tab, 1, 0, before), prob),
        scratch=[
            pltpu.VMEM((rows, width), LOW),
            pltpu.VMEM((before, rows, HEAD_DIM), LOW),
        ]
        + head_scratch,
    )
    line_one = total_of(near_one[0], near_one[1:])
    got_one = far_step(line_one, 0)
    g_last, gpq, gpk, send_part, rel_keep = run(
        attention_backward_last,
        [((3, 1, rows, HEAD_DIM), LOW), ((rows, part), WIDE), ((rows, part), WIDE),
         ((rows + half, width), LOW), ((half, width), LOW)],
        (hot, w_query.T, w_key.T, w_value.T, gctx)
        + tuple(Part(array, 0, before, 1) for array in (q, k, v))
        + (Part(tab, 1, before, 1), prob_last, g_before, gpq_before, gpk_before),
        scratch=[
            pltpu.VMEM((1, HEAD_DIM, span), LOW),
            pltpu.VMEM((1, HEAD_DIM, span), LOW),
            pltpu.VMEM((rows, width), WIDE),
        ]
        + head_scratch,
    )
    for step in range(1, steps):
        line_one = total_of(line_one, [got_one])
        got_one = far_step(line_one, step)
    send_got = swap(after(send_part, line_one))
    (near_two,) = run(
        with_statics(weight_gradients, chunk_two),
        [Pieces(inner, (chunk_two, width), LOW)],
        (x, relative, g_before, g_last, gpq, gpk, wout_grad, small_ffn, small_attn, rel_keep,
         Here(send_got)),
    )
    near_two[1:] = trade(near_two[1:], near_groups)

    x_dealt, attn_dealt = run(
        with_statics(attention_dealt, spots, piece),
        [((rows, width), LOW), Here((rows, width), LOW)],
        (lengths, dealing, dealt_mine, dealt_theirs, tab) + projections,
        scratch=[pltpu.VMEM(head_shape, LOW) for _ in range(4)] + [pltpu.VMEM((rows, rows), WIDE)],
        smem=2,
    )
    line_two = total_of(near_two[0], near_two[1:])
    got_two = far_step(line_two, 0)
    line_one = total_of(line_one, [got_one])
    all_one = gather_near(line_one)
    attn_dealt_got = swap(after(attn_dealt, line_one))
    normed_dealt, down_dealt = run(
        with_statics(ffn_forward, False),
        [((rows, width), WIDE), Here((rows, width), LOW)],
        (x_dealt, Here(attn_dealt), Here(attn_dealt_got)) + ffn_weights,
        scratch=[pltpu.VMEM((rows, width), LOW), pltpu.VMEM((rows, units), LOW)],
    )
    for step in range(1, steps):
        line_two = total_of(line_two, [got_two])
        got_two = far_step(line_two, step)
    down_dealt_got = swap(after(down_dealt, line_two))
    (grad_tokens,) = run(
        finish_tokens,
        [((rows, width), LOW)],
        (gp, Part(send_part, 0, 0, rows), Part(send_got, 0, 0, rows)),
        flops=6 * 10**9,
    )
    (y,) = run(
        finish_dealt,
        [((rows, width), LOW)],
        (Here(down_dealt), Here(down_dealt_got), b_down, normed_dealt, attn_gain, attn_shift,
         ffn_gain, ffn_shift),
        flops=6 * 10**9,
    )
    g_up, g_down = run(
        unpack_ffn, [((width, units), WIDE), ((units, width), WIDE)], (all_one,),
        flops=6 * 10**9,
    )
    line_two = total_of(line_two, [got_two])
    all_two = gather_near(line_two)
    first = 4 * part
    (rel_half,) = run(with_statics(unpack_relative, first), [Here((half, width), LOW)], (all_two,))
    rel_other = swap(rel_half)
    g_wq, g_wk, g_wv, g_wout, g_bup, g_bq, g_bk, g_bv, g_bout, g_again, g_ashift, g_bdown, g_fgain, g_fshift = run(
        with_statics(unpack_attention, first + half),
        [((part, width), WIDE)] * 4
        + [((units,), WIDE)]
        + [((part,), WIDE)] * 3
        + [((width,), WIDE)] * 6,
        (all_two,),
    )
    (g_rel,) = run(join_relative, [((rows, width), WIDE)], (Here(rel_half), Here(rel_other)))
    return (
        y[None], grad_tokens[None], g_rel, g_wq.T, g_bq, g_wk.T, g_bk, g_wv.T, g_bv, g_wout,
        g_bout, g_again, g_ashift, g_up, g_bup, g_down, g_bdown, g_fgain, g_fshift,
    )


def solution(mesh):
    return jax.shard_map(
        on_device,
        mesh=mesh,
        in_specs=(
            P("dp", None, None), P(), P(), P(), P(),
            P(None, "tensor"), P("tensor"), P(None, "tensor"), P("tensor"),
            P(None, "tensor"), P("tensor"), P("tensor", None), P(), P(), P(),
            P(None, "tensor"), P("tensor"), P("tensor", None), P(), P(), P(),
            P("dp", None, None),
        ),
        out_specs=(
            P("dp", None, None), P("dp", None, None), P(),
            P(None, "tensor"), P("tensor"), P(None, "tensor"), P("tensor"),
            P(None, "tensor"), P("tensor"), P("tensor", None), P(), P(), P(),
            P(None, "tensor"), P("tensor"), P("tensor", None), P(), P(), P(),
        ),
        check_vma=False,
    )
```

```python
import math

import jax
import jax.numpy as jnp
from jax import lax
from jax.experimental import pallas as pl
from jax.experimental.pallas import tpu as pltpu
from jax.sharding import PartitionSpec as P

HEAD_DIM = 64
EPSILON = 1e-07
ROOT_HALF = 0.7071067811865476
INV_ROOT_TAU = 0.3989422804014327
BLOCK = 128
LOW = jnp.bfloat16
WIDE = jnp.float32

NN = (((1,), (0,)), ((), ()))
NT = (((1,), (1,)), ((), ()))
TN = (((0,), (0,)), ((), ()))
TT = (((0,), (1,)), ((), ()))


def mm(left, right, dims=NN):
    return lax.dot_general(left, right, dims, preferred_element_type=WIDE)


def pieces(first, count, chunk):
    out = []
    done = 0
    while done < count:
        place, offset = divmod(first + done, chunk)
        take = min(chunk - offset, count - done)
        out.append((place, offset, done, take))
        done += take
    return out


def chunk_rows(rows, parts, unit):
    return -(-(-(-rows // parts)) // unit) * unit


class Part:
    def __init__(self, array, axis, start, count):
        self.array, self.axis, self.start, self.count = array, axis, start, count


class Stack:
    def __init__(self, arrays):
        self.arrays = tuple(arrays)


class Here:
    def __init__(self, *what):
        self.what = what


class Pieces:
    def __init__(self, count, shape, kind):
        self.count, self.shape, self.kind = count, shape, kind


class Fetched:
    def __init__(self, buffer, copies):
        self.buffer, self.copies = buffer, copies
        self.shape, self.dtype = buffer.shape, buffer.dtype
        for copy in copies:
            copy.start()

    def ready(self):
        for copy in self.copies:
            copy.wait()
        self.copies = ()

    def __getitem__(self, index):
        self.ready()
        return self.buffer[index]


class Shipped:
    def __init__(self, buffer, copies):
        self.buffer, self.copies, self.sent = buffer, copies, False
        self.shape, self.dtype = buffer.shape, buffer.dtype

    def send(self):
        if not self.sent:
            for copy in self.copies:
                copy.start()
        self.sent = True

    def wait(self):
        for copy in self.copies:
            copy.wait()

    def __getitem__(self, index):
        return self.buffer[index]

    def __setitem__(self, index, value):
        self.buffer[index] = value


def ready(*refs):
    for ref in refs:
        ref.ready()


def send(*refs):
    for ref in refs:
        ref.send()


def position(inner):
    index = lax.axis_index("dp")
    return index % inner


def call(body, outs, args, scratch=(), smem=0, flops=1):
    arrays, buffers, copies_in, here_in, here_out, loose = [], [], 0, set(), set(), set()
    for arg in args[smem:]:
        if isinstance(arg, Part):
            shape = list(arg.array.shape)
            shape[arg.axis] = arg.count
            arrays.append(arg.array)
            buffers.append(pltpu.VMEM(tuple(shape), arg.array.dtype))
            copies_in += 1
        elif isinstance(arg, Here):
            arrays.append(arg.what[0])
            here_in.add(len(arrays) - 1)
        elif isinstance(arg, Stack):
            first = arg.arrays[0]
            here_in.update(range(len(arrays), len(arrays) + len(arg.arrays)))
            loose.update(range(len(arrays), len(arrays) + len(arg.arrays)))
            arrays.extend(arg.arrays)
            buffers.append(pltpu.VMEM((len(arg.arrays),) + first.shape, first.dtype))
            copies_in += len(arg.arrays)
        else:
            arrays.append(arg)
            buffers.append(pltpu.VMEM(arg.shape, arg.dtype))
            copies_in += 1
    results, out_buffers, copies_out = [], [], 0
    for out in outs:
        if isinstance(out, Pieces):
            results += [pltpu.HBM(out.shape, out.kind)] * out.count
            out_buffers.append(pltpu.VMEM((out.count,) + out.shape, out.kind))
            copies_out += out.count
        elif isinstance(out, Here):
            here_out.add(len(results))
            results.append(jax.ShapeDtypeStruct(*out.what))
        else:
            results.append(pltpu.HBM(*out))
            out_buffers.append(pltpu.VMEM(*out))
            copies_out += 1

    def kernel(*refs):
        refs = list(refs)
        scalars = [refs.pop(0) for _ in range(smem)]
        sources = [refs.pop(0) for _ in arrays]
        targets = [refs.pop(0) for _ in results]
        in_sems, out_sems = refs.pop(0), refs.pop(0)
        fetched, shipped = [], []
        count = 0
        for arg in args[smem:]:
            if isinstance(arg, Here):
                fetched.append(Fetched(sources.pop(0), ()))
                continue
            buffer = refs.pop(0)
            if isinstance(arg, Stack):
                copies = []
                near = position(len(arg.arrays))
                for k in range(len(arg.arrays)):
                    copies.append(
                        pltpu.make_async_copy(
                            sources.pop(0), buffer.at[k ^ near], in_sems.at[count]
                        )
                    )
                    count += 1
            else:
                source = sources.pop(0)
                if isinstance(arg, Part):
                    window = (slice(None),) * arg.axis + (pl.ds(arg.start, arg.count),)
                    source = source.at[window]
                copies = [pltpu.make_async_copy(source, buffer, in_sems.at[count])]
                count += 1
            fetched.append(Fetched(buffer, copies))
        count = 0
        for out in outs:
            if isinstance(out, Here):
                shipped.append(Shipped(targets.pop(0), ()))
                continue
            buffer = refs.pop(0)
            if isinstance(out, Pieces):
                ends = [(buffer.at[k], targets.pop(0)) for k in range(out.count)]
            else:
                ends = [(buffer, targets.pop(0))]
            copies = []
            for source, target in ends:
                copies.append(pltpu.make_async_copy(source, target, out_sems.at[count]))
                count += 1
            shipped.append(Shipped(buffer, copies))
        body(*scalars, *fetched, *shipped, *refs)
        ready(*fetched)
        send(*shipped)
        for ship in shipped:
            ship.wait()

    kernel.__name__ = body.__name__
    space = pltpu.MemorySpace.HBM
    got = pl.pallas_call(
        kernel,
        out_shape=results,
        in_specs=[pl.BlockSpec(memory_space=pltpu.SMEM) for _ in range(smem)]
        + [
            pl.BlockSpec(memory_space=pltpu.VMEM if i in here_in - loose else pl.ANY if i in loose else space)
            for i in range(len(arrays))
        ],
        out_specs=[
            pl.BlockSpec(memory_space=pltpu.VMEM if i in here_out else space)
            for i in range(len(results))
        ],
        scratch_shapes=[
            pltpu.SemaphoreType.DMA((max(copies_in, 1),)),
            pltpu.SemaphoreType.DMA((max(copies_out, 1),)),
        ]
        + buffers
        + out_buffers
        + list(scratch),
        compiler_params=pltpu.CompilerParams(vmem_limit_bytes=40 * 1024 * 1024),
        cost_estimate=pl.CostEstimate(flops=flops, bytes_accessed=1, transcendentals=0),
    )(
        *args[:smem],
        *(
            array if i in here_in else pltpu.with_memory_space_constraint(array, space)
            for i, array in enumerate(arrays)
        ),
    )
    final = []
    for out in outs:
        if isinstance(out, Pieces):
            final.append(list(got[: out.count]))
            got = got[out.count :]
        else:
            final.append(got[0])
            got = got[1:]
    return final


def call_here(body, outs, args, smem=0):
    return pl.pallas_call(
        body,
        out_shape=[jax.ShapeDtypeStruct(shape, kind) for shape, kind in outs],
        in_specs=[
            pl.BlockSpec(memory_space=pltpu.SMEM if i < smem else pltpu.VMEM) for i in range(len(args))
        ],
        out_specs=[pl.BlockSpec(memory_space=pltpu.VMEM) for _ in outs],
        compiler_params=pltpu.CompilerParams(vmem_limit_bytes=4 * 1024 * 1024),
    )(*args)


def permute_body(piece, dealing, source, target):
    for k in range(source.shape[0]):
        there = dealing[k]
        target[there, :piece, :] = source[k, :piece, :]
        target[k, piece:, :] = source[there, piece:, :]


def assemble(mine, theirs, spots, first, piece, target):
    side = lax.axis_index("tensor")
    half = spots * piece
    for source, base in ((mine, side * half), (theirs, (1 - side) * half)):
        for p in range(spots):
            target[pl.ds(pl.multiple_of(base + p * piece, piece), piece), :] = source[
                p, first : first + piece, :
            ]


def project(x, weights, biases, outs):
    for weight, bias, out in zip(weights, biases, outs):
        full = (mm(x, weight[...], NT) + bias[...].astype(WIDE)[None, :]).astype(LOW)
        for h in range(out.shape[0]):
            out[h] = full[:, h * HEAD_DIM : (h + 1) * HEAD_DIM]


def anti_diagonal():
    return jnp.where(
        lax.broadcasted_iota(jnp.int32, (BLOCK, BLOCK), 0)
        + lax.broadcasted_iota(jnp.int32, (BLOCK, BLOCK), 1)
        == BLOCK - 1,
        1.0,
        0.0,
    ).astype(LOW)


def one_hot(table, buckets):
    anti = anti_diagonal()
    entries = table[...]
    high = entries // 256
    turned = mm(high.astype(WIDE).astype(LOW), anti) * 256.0 + mm(
        (entries - high * 256).astype(WIDE).astype(LOW), anti
    )
    turned = turned.astype(jnp.int32)
    count = table.shape[0]
    rows = lax.broadcasted_iota(jnp.int32, (buckets, BLOCK), 0)
    return jnp.concatenate(
        [
            jnp.where(rows == turned[count - 1 - b : count - b, :], 1.0, 0.0).astype(LOW)
            for b in range(count)
        ],
        axis=1,
    )


def attend(length, count, q, k, v, tab, ctx, far_scratch, prob_out):
    rows = q.shape[1]
    window = rows + BLOCK
    scale = 1.0 / math.sqrt(3.0 * HEAD_DIM)
    key_ok = lax.broadcasted_iota(jnp.int32, (1, rows), 1) < length
    blocks = [slice(i * BLOCK, (i + 1) * BLOCK) for i in range(rows // BLOCK)]

    def head(h, carry):
        for here in blocks:
            w0 = rows - BLOCK - here.start
            far = mm(k[h, here, :], tab[0, h, :, w0 : w0 + window])
            far = pltpu.roll(far, window - BLOCK, 1, stride=1, stride_axis=0)[:, :rows]
            far_scratch[:, here] = far.T
        for here in blocks:
            w0 = rows - BLOCK - here.start
            near = mm(q[h, here, :], tab[1, h, :, w0 : w0 + window])
            near = pltpu.roll(near, window - BLOCK, 1, stride=1, stride_axis=0)[:, :rows]
            far_scratch[here, :] += near
        for here in blocks:
            score = (mm(q[h, here, :], k[h], NT) + far_scratch[here, :]) * scale
            score = jnp.where(key_ok, score, -1e30)
            top = jnp.max(score, axis=1, keepdims=True)
            weights = jnp.exp(score - top)
            row_ok = here.start + lax.broadcasted_iota(jnp.int32, (BLOCK, 1), 0) < length
            norm = jnp.where(row_ok, 1.0 / jnp.sum(weights, axis=1, keepdims=True), 0.0)
            prob = (weights * norm).astype(LOW)
            if prob_out is not None:
                prob_out[h, here, :] = prob
            ctx[h, here, :] = mm(prob, v[h]).astype(LOW)
        return carry

    lax.fori_loop(0, count, head, 0)


def attention_first(
    lengths, x, relative, table, wq, bq, wk, bk, wv, bv,
    q_out, k_out, v_out, tab_out, hot_out, prob_out, ctx_out, far_scratch,
):
    length = lengths[lax.axis_index("dp")]
    project(x[...], (wq, wk, wv), (bq, bk, bv), (q_out, k_out, v_out))
    send(q_out, k_out, v_out)
    rel = relative[...]
    hot = one_hot(table, relative.shape[0])
    hot_out[...] = hot
    for slot, (weight, bias) in enumerate(((wq, bq), (wk, bk))):
        low = (mm(rel, weight[...], NT) + bias[...].astype(WIDE)[None, :]).astype(LOW)
        spread = mm(low, hot, TN).astype(LOW)
        for h in range(q_out.shape[0]):
            tab_out[slot, h] = spread[h * HEAD_DIM : (h + 1) * HEAD_DIM]
    send(tab_out, hot_out)
    attend(length, ctx_out.shape[0], q_out, k_out, v_out, tab_out, ctx_out, far_scratch, prob_out)


def attention_rest(
    lengths, q, k, v, tab, wout, ctx_before, prob_out, ctx_out, attn_out, far_scratch
):
    length = lengths[lax.axis_index("dp")]
    ready(q, k, v, tab)
    attend(length, q.shape[0], q, k, v, tab, ctx_out, far_scratch, prob_out)
    send(prob_out)
    heads = [ctx_before[h] for h in range(ctx_before.shape[0])]
    heads += [ctx_out[h] for h in range(q.shape[0])]
    attn_out[...] = mm(jnp.concatenate(heads, axis=1), wout[...]).astype(LOW)


def attention_dealt(
    spots, piece, lengths, dealing, mine, theirs, tab, wq, bq, wk, bk, wv, bv, wout,
    x_out, attn_out, q, k, v, ctx, far_scratch,
):
    length = lengths[dealing[lax.axis_index("dp")]]
    assemble(mine, theirs, spots, piece, piece, x_out)
    send(x_out)
    project(x_out[...], (wq, wk, wv), (bq, bk, bv), (q, k, v))
    ready(tab)
    attend(length, q.shape[0], q, k, v, tab, ctx, far_scratch, None)
    heads = [ctx[h] for h in range(q.shape[0])]
    attn_out[...] = mm(jnp.concatenate(heads, axis=1), wout[...]).astype(LOW)


def row_norm(values):
    center = values - jnp.mean(values, axis=-1, keepdims=True)
    inverse = lax.rsqrt(jnp.mean(center * center, axis=-1, keepdims=True) + EPSILON)
    return center * inverse, inverse


def norm_back(scaled, normed, inverse):
    one = jnp.mean(scaled, axis=-1, keepdims=True)
    two = jnp.mean(scaled * normed, axis=-1, keepdims=True)
    return inverse * (scaled - one - normed * two)


def ffn_forward(
    keep, x, mine, theirs, bout, gain, shift, wup, bup, wdown, normed_out, down_out, *rest
):
    low_scratch, act_scratch = rest[-2:]
    if keep:
        inverse_out, hidden_out, act_out, slope_out = rest[:4]
    rows = x.shape[0]
    blocks = [slice(i * BLOCK, (i + 1) * BLOCK) for i in range(rows // BLOCK)]
    for here in blocks:
        attn = mine[here, :].astype(WIDE) + theirs[here, :].astype(WIDE) + wide_row(bout)
        normed, inverse = row_norm(x[here, :].astype(WIDE) + attn)
        normed_out[here, :] = normed
        low = (normed * wide_row(gain) + wide_row(shift)).astype(LOW)
        low_scratch[here, :] = low
        if keep:
            inverse_out[here, :] = inverse
            hidden_out[here, :] = low
    send(normed_out)
    for here in blocks:
        u = mm(low_scratch[here, :], wup[...]) + wide_row(bup)
        cdf = 0.5 * (1.0 + lax.erf(u * ROOT_HALF))
        act = (u * cdf).astype(LOW)
        act_scratch[here, :] = act
        if keep:
            act_out[here, :] = act
            density = jnp.exp(-0.5 * u * u) * INV_ROOT_TAU
            slope_out[here, :] = (cdf + u * density).astype(LOW)
    if keep:
        send(inverse_out, hidden_out, act_out, slope_out)
    for here in blocks:
        down_out[here, :] = mm(act_scratch[here, :], wdown[...]).astype(LOW)


def wide_row(vector):
    return vector[...].astype(WIDE)[None, :]


def second_norm(here, mine, theirs, bdown, normed, gain, shift):
    f = mine[here, :].astype(WIDE) + theirs[here, :].astype(WIDE) + wide_row(bdown)
    return row_norm(normed[here, :] * wide_row(gain) + wide_row(shift) + f)


def finish_dealt(mine, theirs, bdown, normed, gain, shift, fgain, fshift, y_out):
    for i in range(normed.shape[0] // BLOCK):
        here = slice(i * BLOCK, (i + 1) * BLOCK)
        n2, _ = second_norm(here, mine, theirs, bdown, normed, gain, shift)
        y_out[here, :] = (n2 * wide_row(fgain) + wide_row(fshift)).astype(LOW)


def put(buffer, chunk, first, value):
    near = position(buffer.shape[0])
    for place, offset, start, take in pieces(first, value.shape[0], chunk):
        buffer[place ^ near, offset : offset + take, :] = value[start : start + take]


def put_zeros(buffer, chunk, first):
    inner, _, width = buffer.shape
    left = inner * chunk - first
    if left > 0:
        put(buffer, chunk, first, jnp.zeros((left, width), buffer.dtype))


def ffn_backward(
    chunk, spots, piece, lengths,
    mine, theirs, bdown, normed, gain, shift, fgain, cot_mine, cot_theirs,
    hidden, act, slope, wup, wdown,
    part_out, gf_out, small_out, buffer_out, low_scratch, gu_scratch, cot_scratch,
):
    length = lengths[lax.axis_index("dp")]
    rows, width = normed.shape
    units = act.shape[1]
    assemble(cot_mine, cot_theirs, spots, 0, piece, cot_scratch)
    sums = [jnp.zeros((1, width), WIDE) for _ in range(3)]
    for i in range(rows // BLOCK):
        here = slice(i * BLOCK, (i + 1) * BLOCK)
        n2, r2 = second_norm(here, mine, theirs, bdown, normed, gain, shift)
        row_ok = i * BLOCK + lax.broadcasted_iota(jnp.int32, (BLOCK, 1), 0) < length
        gy = jnp.where(row_ok, cot_scratch[here, :].astype(WIDE), 0.0)
        gf = norm_back(gy * wide_row(fgain), n2, r2)
        gf_out[here, :] = gf
        low = gf.astype(LOW)
        low_scratch[here, :] = low
        sums[0] += jnp.sum(low.astype(WIDE), axis=0, keepdims=True)
        sums[1] += jnp.sum(gy * n2, axis=0, keepdims=True)
        sums[2] += jnp.sum(gy, axis=0, keepdims=True)
    send(gf_out)
    gu_sum = jnp.zeros((1, units), WIDE)
    for i in range(rows // BLOCK):
        here = slice(i * BLOCK, (i + 1) * BLOCK)
        gu = (mm(low_scratch[here, :], wdown[...], NT) * slope[here, :].astype(WIDE)).astype(LOW)
        gu_scratch[here, :] = gu
        gu_sum += jnp.sum(gu.astype(WIDE), axis=0, keepdims=True)
        part_out[here, :] = mm(gu, wup[...], NT).astype(LOW)
    send(part_out)
    small_out[...] = jnp.zeros(small_out.shape, WIDE)
    for k in range(units // width):
        small_out[k : k + 1, :] = gu_sum[:, k * width : (k + 1) * width]
    for k in range(3):
        small_out[units // width + k : units // width + k + 1, :] = sums[k]
    put(buffer_out, chunk, units, mm(act[...], low_scratch[...], TN).astype(LOW))
    for k in range(units // width):
        columns = slice(k * width, (k + 1) * width)
        put(
            buffer_out, chunk, k * width,
            mm(hidden[...], gu_scratch[:, columns], TN).astype(LOW),
        )
    put_zeros(buffer_out, chunk, 2 * units)


def head_backward(
    h, q, k, v, tab, prob, gctx, anti, g_out, gpq_out, gpk_out,
    gs_scratch, gp_scratch, turned_scratch, moved_scratch,
):
    rows = q.shape[1]
    span = tab.shape[3]
    window = rows + BLOCK
    scale = 1.0 / math.sqrt(3.0 * HEAD_DIM)
    blocks = [slice(i * BLOCK, (i + 1) * BLOCK) for i in range(rows // BLOCK)]
    pad = jnp.zeros((BLOCK, BLOCK), WIDE)
    for here in blocks:
        weights = prob[h, here, :].astype(WIDE)
        gprob = mm(gctx[h, here, :], v[h], NT)
        dots = jnp.sum(weights * gprob, axis=1, keepdims=True)
        gs_scratch[here, :] = (weights * (gprob - dots)).astype(LOW)
    g_out[2, h] = mm(prob[h], gctx[h], TN).astype(LOW)
    for slot, (source, other) in enumerate(((q, k), (k, q))):
        for here in blocks:
            if slot == 0:
                turned = mm(anti, gs_scratch[here, :])
            else:
                turned = mm(anti, gs_scratch[:, here], NT)
            turned_scratch[slot, here, :] = turned.astype(LOW)
            moved_scratch[slot, here, :] = pltpu.roll(
                jnp.concatenate([turned, pad], axis=1), 1, 1, stride=1, stride_axis=0
            ).astype(LOW)
    gp_scratch[...] = jnp.zeros((2, HEAD_DIM, span), WIDE)
    for slot, (source, other) in enumerate(((q, k), (k, q))):
        for here in blocks:
            w0 = rows - BLOCK - here.start
            moved = moved_scratch[slot, here, :]
            table_here = tab[1 - slot, h, :, w0 : w0 + window]
            grad = (mm(turned_scratch[slot, here, :], other[h]) + mm(moved, table_here, NT)) * scale
            g_out[slot, h, here, :] = mm(anti, grad.astype(LOW)).astype(LOW)
            turned = mm(anti, source[h, here, :]).astype(LOW)
            gp_scratch[1 - slot, :, w0 : w0 + window] += mm(turned, moved, TN)
    gpq_out[h] = gp_scratch[0].astype(LOW)
    gpk_out[h] = gp_scratch[1].astype(LOW)


def attention_backward(
    wout, mine, theirs, gf, normed, inverse, gain, ctx, ctx_last, q, k, v, tab, prob,
    gp_out, wout_out, small_out, gctx_out, g_out, gpq_out, gpk_out,
    gpb_scratch, gctx_scratch, *scratch,
):
    first, rows, _ = ctx.shape
    heads = first + 1
    width = gp_out.shape[1]
    blocks = rows // BLOCK
    sums = [jnp.zeros((1, width), WIDE) for _ in range(3)]
    for i in range(blocks):
        here = slice(i * BLOCK, (i + 1) * BLOCK)
        gh = gf[here, :] + (mine[here, :].astype(WIDE) + theirs[here, :].astype(WIDE))
        n1 = normed[here, :]
        gp = norm_back(gh * wide_row(gain), n1, inverse[here, :])
        gp_out[here, :] = gp
        low = gp.astype(LOW)
        gpb_scratch[here, :] = low
        sums[0] += jnp.sum(low.astype(WIDE), axis=0, keepdims=True)
        sums[1] += jnp.sum(gh * n1, axis=0, keepdims=True)
        sums[2] += jnp.sum(gh, axis=0, keepdims=True)
        grad = mm(low, wout[...], NT).astype(LOW)
        for h in range(heads):
            part = grad[:, h * HEAD_DIM : (h + 1) * HEAD_DIM]
            if h < first:
                gctx_scratch[h, here, :] = part
            else:
                gctx_out[0, here, :] = part
    small_out[...] = jnp.zeros(small_out.shape, WIDE)
    for n in range(3):
        small_out[2 + n : 3 + n, :] = sums[n]
    for h in range(heads):
        wout_out[h * HEAD_DIM : (h + 1) * HEAD_DIM, :] = mm(
            ctx[h] if h < first else ctx_last[0], gpb_scratch[...], TN
        ).astype(LOW)
    send(gp_out, small_out, wout_out, gctx_out)
    anti = anti_diagonal()
    ready(q, k, v, tab, prob)

    def head(h, carry):
        head_backward(
            h, q, k, v, tab, prob, gctx_scratch, anti, g_out, gpq_out, gpk_out, *scratch
        )
        return carry

    lax.fori_loop(0, first, head, 0)


def attention_backward_last(
    hot, wq, wk, wv, gctx, q, k, v, tab, prob, before, gpq_before, gpk_before,
    g_out, gpq_out, gpk_out, send_out, keep_out,
    gpq_scratch, gpk_scratch, rel_scratch, *scratch,
):
    side = lax.axis_index("tensor")
    buckets = rel_scratch.shape[0]
    half = buckets // 2
    scale = 1.0 / math.sqrt(3.0 * HEAD_DIM)
    anti = anti_diagonal()
    head_backward(
        0, q, k, v, tab, prob, gctx, anti, g_out, gpq_scratch, gpk_scratch, *scratch
    )
    send(g_out)
    for first, here, out in (
        (gpq_before, gpq_scratch, gpq_out), (gpk_before, gpk_scratch, gpk_out)
    ):
        parts = [first[h] for h in range(first.shape[0])] + [here[0]]
        out[...] = mm(hot[...], jnp.concatenate(parts, axis=0), NT) * scale
    rel_scratch[...] = mm(gpq_out[...].astype(LOW), wq[...]) + mm(gpk_out[...].astype(LOW), wk[...])
    send(gpq_out, gpk_out)
    rows = buckets
    send_out[rows:, :] = rel_scratch[
        pl.ds(pl.multiple_of((1 - side) * half, half), half), :
    ].astype(LOW)
    keep_out[...] = rel_scratch[pl.ds(pl.multiple_of(side * half, half), half), :].astype(LOW)
    send_out[:rows, :] = (
        mm(together(0, before, g_out), wq[...])
        + mm(together(1, before, g_out), wk[...])
        + mm(together(2, before, g_out), wv[...])
    ).astype(LOW)


def together(slot, before, last):
    parts = [before[slot, h] for h in range(before.shape[1])] + [last[slot, 0]]
    return jnp.concatenate(parts, axis=1)


def weight_gradients(
    chunk, x, relative, before, last, gpq, gpk, wout_grad, small_ffn, small_attn, keep, got,
    buffer_out,
):
    part = gpq.shape[1]
    xv = x[...]
    rel = relative[...]
    gq, gk, gv = (together(slot, before, last) for slot in range(3))
    put(
        buffer_out, chunk, 0,
        (mm(gq, xv, TN) + mm(gpq[...].astype(LOW), rel, TN)).astype(LOW),
    )
    put(
        buffer_out, chunk, part,
        (mm(gk, xv, TN) + mm(gpk[...].astype(LOW), rel, TN)).astype(LOW),
    )
    put(buffer_out, chunk, 2 * part, mm(gv, xv, TN).astype(LOW))
    put(buffer_out, chunk, 3 * part, wout_grad[...])
    half = keep.shape[0]
    both = (keep[...].astype(WIDE) + got[got.shape[0] - half :, :].astype(WIDE)).astype(LOW)
    put(buffer_out, chunk, 4 * part, both)
    count = 4 * part + keep.shape[0]
    bias = [
        jnp.sum(gq.astype(WIDE), axis=0, keepdims=True) + jnp.sum(gpq[...], axis=0, keepdims=True),
        jnp.sum(gk.astype(WIDE), axis=0, keepdims=True) + jnp.sum(gpk[...], axis=0, keepdims=True),
        jnp.sum(gv.astype(WIDE), axis=0, keepdims=True),
    ]
    second = jnp.concatenate([bias[2], jnp.zeros_like(bias[2])], axis=1)
    small = jnp.concatenate(
        [small_ffn[...], jnp.concatenate(bias[:2], axis=1), second, small_attn[2:, :]], axis=0
    ).astype(LOW)
    put(buffer_out, chunk, count, small)
    put_zeros(buffer_out, chunk, count + small.shape[0])


def finish_tokens(gp, mine, theirs, grad_out):
    for i in range(gp.shape[0] // BLOCK):
        here = slice(i * BLOCK, (i + 1) * BLOCK)
        both = mine[here, :].astype(WIDE) + theirs[here, :].astype(WIDE)
        grad_out[here, :] = (gp[here, :] + both).astype(LOW)


def chunks(gathered, first, count):
    for place, offset, start, take in pieces(first, count, gathered.shape[1]):
        yield start, take, gathered[place, offset : offset + take, :].astype(WIDE)


def unpack_ffn(gathered, wup_out, wdown_out):
    width, units = wup_out.shape
    for start, take, value in chunks(gathered, units, units):
        wdown_out[start : start + take, :] = value
    send(wdown_out)
    for k in range(units // width):
        for start, take, value in chunks(gathered, k * width, width):
            wup_out[start : start + take, k * width : (k + 1) * width] = value


def unpack_relative(first, gathered, rel_out):
    for start, take, value in chunks(gathered, first, rel_out.shape[0]):
        rel_out[start : start + take, :] = value.astype(LOW)


def unpack_attention(
    first, gathered, wq_out, wk_out, wv_out, wout_out, bup_out,
    bq_out, bk_out, bv_out, bout_out, again_out, ashift_out, bdown_out, fgain_out, fshift_out,
):
    part, width = wq_out.shape
    units = bup_out.shape[0]
    for k, out in enumerate((wq_out, wk_out, wv_out, wout_out)):
        for start, take, value in chunks(gathered, k * part, part):
            out[start : start + take, :] = value
        send(out)
    small = jnp.concatenate([value for _, _, value in chunks(gathered, first, 16)], axis=0)
    ups = units // width
    for k in range(ups):
        bup_out[k * width : (k + 1) * width] = small[k]
    bdown_out[...] = small[ups]
    fgain_out[...] = small[ups + 1]
    fshift_out[...] = small[ups + 2]
    bq_out[...] = small[8, :part]
    bk_out[...] = small[8, part:]
    bv_out[...] = small[9, :part]
    bout_out[...] = small[10]
    again_out[...] = small[11]
    ashift_out[...] = small[12]


def join_relative(mine, theirs, out):
    side = lax.axis_index("tensor")
    half = mine.shape[0]
    out[pl.ds(pl.multiple_of(side * half, half), half), :] = mine[...].astype(WIDE)
    out[pl.ds(pl.multiple_of((1 - side) * half, half), half), :] = theirs[...].astype(WIDE)


def with_statics(body, *statics):
    def wrapped(*refs):
        body(*statics, *refs)

    wrapped.__name__ = body.__name__
    return wrapped


def swap(array):
    return lax.ppermute(array, "tensor", [(0, 1), (1, 0)])


def exchange(array):
    return lax.all_to_all(array, "dp", split_axis=0, concat_axis=0, tiled=True)


def trade(arrays, groups):
    got = []
    for k, array in enumerate(arrays, 1):
        pairs = [(group[p], group[p ^ k]) for group in groups for p in range(len(group))]
        got.append(lax.ppermute(array, "dp", pairs))
    return got


def after(value, *others):
    return lax.optimization_barrier((value,) + others)[0]


class Sequence:
    def __init__(self):
        self.last = None

    def run(self, body, outs, args, scratch=(), smem=0, flops=1):
        args = list(args)
        if self.last is not None:
            free = [i for i in range(smem, len(args)) if not isinstance(args[i], (Here, Stack))]
            if free:
                arg = args[free[0]]
                if isinstance(arg, Part):
                    args[free[0]] = Part(after(arg.array, self.last), arg.axis, arg.start, arg.count)
                else:
                    args[free[0]] = after(arg, self.last)
            elif isinstance(args[smem], Stack):
                first = args[smem].arrays
                args[smem] = Stack((after(first[0], self.last),) + first[1:])
            else:
                args[smem] = Here(after(args[smem].what[0], self.last))
        got = call(body, outs, args, scratch, smem, flops)
        self.last = got[0][0] if isinstance(got[0], list) else got[0]
        return got


def on_device(
    tokens, lengths, dealing, bucket_table, relative,
    w_query, b_query, w_key, b_key, w_value, b_value, w_out, b_out,
    attn_gain, attn_shift, w_up, b_up, w_down, b_down, ffn_gain, ffn_shift, cotangent,
):
    _, rows, width = tokens.shape
    total = dealing.shape[0]
    part = w_query.shape[1]
    heads = part // HEAD_DIM
    before = heads - 1
    units = w_up.shape[1]
    half = rows // 2
    span = 2 * rows
    piece = max(16, half // total)
    spots = half // piece
    side = lax.axis_index("tensor")
    inner = 1 << ((total.bit_length()) // 2)
    outer = total // inner
    near_groups = [[o * inner + i for i in range(inner)] for o in range(outer)]
    chunk_one = chunk_rows(2 * units, inner, 16)
    chunk_two = chunk_rows(4 * part + half + 16, inner, 16)

    sequence = Sequence()
    run = sequence.run

    def cut(array):
        mine = lax.dynamic_slice_in_dim(array[0], side * half, half, 0)
        return mine.reshape(spots, piece, width)

    moving = jnp.concatenate([cut(cotangent), cut(tokens)], axis=1)
    if spots < total:
        moving = jnp.pad(moving, ((0, total - spots), (0, 0), (0, 0)))
    arrived = exchange(moving)
    x = tokens[0]
    table = jnp.pad(bucket_table, (0, span - bucket_table.shape[0]), constant_values=-1)
    table = table.reshape(span // BLOCK, BLOCK)
    projections = (w_query.T, b_query, w_key.T, b_key, w_value.T, b_value, w_out)
    head_shape = (heads, rows, HEAD_DIM)
    q, k, v, tab, hot, prob, ctx = run(
        attention_first,
        [(head_shape, LOW)] * 3
        + [((2, heads, HEAD_DIM, span), LOW), ((relative.shape[0], span), LOW), ((before, rows, rows), LOW),
           ((before, rows, HEAD_DIM), LOW)],
        (lengths, x, relative, table) + projections[:6],
        scratch=[pltpu.VMEM((rows, rows), WIDE)],
        smem=1,
    )
    arrived = after(arrived, sequence.last)
    (turned,) = call_here(
        with_statics(permute_body, piece), [(arrived.shape, LOW)], (dealing, arrived), smem=1
    )
    sequence.last = turned
    dealt_mine = exchange(turned)
    dealt_theirs = swap(dealt_mine)
    prob_last, ctx_last, attn_part = run(
        attention_rest,
        [((1, rows, rows), LOW), ((1, rows, HEAD_DIM), LOW), Here((rows, width), LOW)],
        (lengths,)
        + tuple(Part(array, 0, before, 1) for array in (q, k, v))
        + (Part(tab, 1, before, 1), w_out, ctx),
        scratch=[pltpu.VMEM((rows, rows), WIDE)],
        smem=1,
    )
    attn_got = swap(attn_part)
    ffn_weights = (b_out, attn_gain, attn_shift, w_up, b_up, w_down)
    normed, down_part, inverse, hidden, act, slope = run(
        with_statics(ffn_forward, True),
        [((rows, width), WIDE), Here((rows, width), LOW), ((rows, 1), WIDE), ((rows, width), LOW),
         ((rows, units), LOW), ((rows, units), LOW)],
        (x, Here(attn_part), Here(attn_got)) + ffn_weights,
        scratch=[pltpu.VMEM((rows, width), LOW), pltpu.VMEM((rows, units), LOW)],
    )
    down_got = swap(down_part)
    hidden_part, gf, small_ffn, near_one = run(
        with_statics(ffn_backward, chunk_one, spots, piece),
        [Here((rows, width), LOW), ((rows, width), WIDE), ((8, width), WIDE),
         Pieces(inner, (chunk_one, width), LOW)],
        (lengths, Here(down_part), Here(down_got), b_down, normed, attn_gain, attn_shift,
         ffn_gain, Here(dealt_mine), Here(dealt_theirs), hidden, act, slope, w_up, w_down),
        scratch=[
            pltpu.VMEM((rows, width), LOW),
            pltpu.VMEM((rows, units), LOW),
            pltpu.VMEM((rows, width), LOW),
        ],
        smem=1,
    )
    hidden_got = swap(hidden_part)
    near_one[1:] = trade(near_one[1:], near_groups)

    def total_of(own, got):
        acc = after(own, sequence.last).astype(WIDE)
        for other in got:
            acc += other.astype(WIDE)
        sequence.last = acc.astype(LOW)
        return sequence.last

    def far_step(array, step):
        reach = inner << step
        return lax.ppermute(array, "dp", [(p, p ^ reach) for p in range(total)])

    steps = outer.bit_length() - 1

    def gather_near(line):
        return Stack([line] + trade([line] * (inner - 1), near_groups))

    head_scratch = [
        pltpu.VMEM((rows, rows), LOW),
        pltpu.VMEM((2, HEAD_DIM, span), WIDE),
        pltpu.VMEM((2, rows, rows), LOW),
        pltpu.VMEM((2, rows, rows + BLOCK), LOW),
    ]
    gp, wout_grad, small_attn, gctx, g_before, gpq_before, gpk_before = run(
        attention_backward,
        [((rows, width), WIDE), ((part, width), LOW), ((8, width), WIDE),
         ((1, rows, HEAD_DIM), LOW), ((3, before, rows, HEAD_DIM), LOW),
         ((before, HEAD_DIM, span), LOW), ((before, HEAD_DIM, span), LOW)],
        (w_out, Here(hidden_part), Here(hidden_got), gf, normed, inverse, attn_gain, ctx, ctx_last)
        + tuple(Part(array, 0, 0, before) for array in (q, k, v))
        + (Part(tab, 1, 0, before), prob),
        scratch=[
            pltpu.VMEM((rows, width), LOW),
            pltpu.VMEM((before, rows, HEAD_DIM), LOW),
        ]
        + head_scratch,
    )
    line_one = total_of(near_one[0], near_one[1:])
    got_one = far_step(line_one, 0)
    g_last, gpq, gpk, send_part, rel_keep = run(
        attention_backward_last,
        [((3, 1, rows, HEAD_DIM), LOW), ((rows, part), WIDE), ((rows, part), WIDE),
         ((rows + half, width), LOW), ((half, width), LOW)],
        (hot, w_query.T, w_key.T, w_value.T, gctx)
        + tuple(Part(array, 0, before, 1) for array in (q, k, v))
        + (Part(tab, 1, before, 1), prob_last, g_before, gpq_before, gpk_before),
        scratch=[
            pltpu.VMEM((1, HEAD_DIM, span), LOW),
            pltpu.VMEM((1, HEAD_DIM, span), LOW),
            pltpu.VMEM((rows, width), WIDE),
        ]
        + head_scratch,
    )
    for step in range(1, steps):
        line_one = total_of(line_one, [got_one])
        got_one = far_step(line_one, step)
    send_got = swap(after(send_part, line_one))
    (near_two,) = run(
        with_statics(weight_gradients, chunk_two),
        [Pieces(inner, (chunk_two, width), LOW)],
        (x, relative, g_before, g_last, gpq, gpk, wout_grad, small_ffn, small_attn, rel_keep,
         Here(send_got)),
    )
    near_two[1:] = trade(near_two[1:], near_groups)

    x_dealt, attn_dealt = run(
        with_statics(attention_dealt, spots, piece),
        [((rows, width), LOW), Here((rows, width), LOW)],
        (lengths, dealing, dealt_mine, dealt_theirs, tab) + projections,
        scratch=[pltpu.VMEM(head_shape, LOW) for _ in range(4)] + [pltpu.VMEM((rows, rows), WIDE)],
        smem=2,
    )
    line_one, *near_two[1:] = lax.optimization_barrier((line_one, *near_two[1:]))
    line_one = total_of(line_one, [got_one])
    line_two = total_of(near_two[0], near_two[1:])
    got_two = far_step(line_two, 0)
    all_one = gather_near(line_one)
    attn_dealt_got = swap(after(attn_dealt, line_two))
    normed_dealt, down_dealt = run(
        with_statics(ffn_forward, False),
        [((rows, width), WIDE), Here((rows, width), LOW)],
        (x_dealt, Here(attn_dealt), Here(attn_dealt_got)) + ffn_weights,
        scratch=[pltpu.VMEM((rows, width), LOW), pltpu.VMEM((rows, units), LOW)],
    )
    for step in range(1, steps):
        line_two = total_of(line_two, [got_two])
        got_two = far_step(line_two, step)
    down_dealt_got = swap(after(down_dealt, line_two))
    (grad_tokens,) = run(
        finish_tokens,
        [((rows, width), LOW)],
        (gp, Part(send_part, 0, 0, rows), Part(send_got, 0, 0, rows)),
        flops=6 * 10**9,
    )
    (y,) = run(
        finish_dealt,
        [((rows, width), LOW)],
        (Here(down_dealt), Here(down_dealt_got), b_down, normed_dealt, attn_gain, attn_shift,
         ffn_gain, ffn_shift),
        flops=6 * 10**9,
    )
    g_up, g_down = run(
        unpack_ffn, [((width, units), WIDE), ((units, width), WIDE)], (all_one,),
        flops=6 * 10**9,
    )
    line_two = total_of(line_two, [got_two])
    all_two = gather_near(line_two)
    first = 4 * part
    (rel_half,) = run(with_statics(unpack_relative, first), [Here((half, width), LOW)], (all_two,))
    rel_other = swap(rel_half)
    g_wq, g_wk, g_wv, g_wout, g_bup, g_bq, g_bk, g_bv, g_bout, g_again, g_ashift, g_bdown, g_fgain, g_fshift = run(
        with_statics(unpack_attention, first + half),
        [((part, width), WIDE)] * 4
        + [((units,), WIDE)]
        + [((part,), WIDE)] * 3
        + [((width,), WIDE)] * 6,
        (all_two,),
    )
    (g_rel,) = run(join_relative, [((rows, width), WIDE)], (Here(rel_half), Here(rel_other)))
    return (
        y[None], grad_tokens[None], g_rel, g_wq.T, g_bq, g_wk.T, g_bk, g_wv.T, g_bv, g_wout,
        g_bout, g_again, g_ashift, g_up, g_bup, g_down, g_bdown, g_fgain, g_fshift,
    )


def solution(mesh):
    return jax.shard_map(
        on_device,
        mesh=mesh,
        in_specs=(
            P("dp", None, None), P(), P(), P(), P(),
            P(None, "tensor"), P("tensor"), P(None, "tensor"), P("tensor"),
            P(None, "tensor"), P("tensor"), P("tensor", None), P(), P(), P(),
            P(None, "tensor"), P("tensor"), P("tensor", None), P(), P(), P(),
            P("dp", None, None),
        ),
        out_specs=(
            P("dp", None, None), P("dp", None, None), P(),
            P(None, "tensor"), P("tensor"), P(None, "tensor"), P("tensor"),
            P(None, "tensor"), P("tensor"), P("tensor", None), P(), P(), P(),
            P(None, "tensor"), P("tensor"), P("tensor", None), P(), P(), P(),
        ),
        check_vma=False,
    )
```

```python
import math

import jax
import jax.numpy as jnp
from jax import lax
from jax.experimental import pallas as pl
from jax.experimental.pallas import tpu as pltpu
from jax.sharding import PartitionSpec as P

HEAD_DIM = 64
EPSILON = 1e-07
ROOT_HALF = 0.7071067811865476
INV_ROOT_TAU = 0.3989422804014327
BLOCK = 128
LOW = jnp.bfloat16
WIDE = jnp.float32

NN = (((1,), (0,)), ((), ()))
NT = (((1,), (1,)), ((), ()))
TN = (((0,), (0,)), ((), ()))
TT = (((0,), (1,)), ((), ()))


def mm(left, right, dims=NN):
    return lax.dot_general(left, right, dims, preferred_element_type=WIDE)


def pieces(first, count, chunk):
    out = []
    done = 0
    while done < count:
        place, offset = divmod(first + done, chunk)
        take = min(chunk - offset, count - done)
        out.append((place, offset, done, take))
        done += take
    return out


def chunk_rows(rows, parts, unit):
    return -(-(-(-rows // parts)) // unit) * unit


class Part:
    def __init__(self, array, axis, start, count):
        self.array, self.axis, self.start, self.count = array, axis, start, count


class Stack:
    def __init__(self, arrays):
        self.arrays = tuple(arrays)


class Here:
    def __init__(self, *what):
        self.what = what


class Pieces:
    def __init__(self, count, shape, kind):
        self.count, self.shape, self.kind = count, shape, kind


class Fetched:
    def __init__(self, buffer, copies):
        self.buffer, self.copies = buffer, copies
        self.shape, self.dtype = buffer.shape, buffer.dtype
        for copy in copies:
            copy.start()

    def ready(self):
        for copy in self.copies:
            copy.wait()
        self.copies = ()

    def __getitem__(self, index):
        self.ready()
        return self.buffer[index]


class Shipped:
    def __init__(self, buffer, copies):
        self.buffer, self.copies, self.sent = buffer, copies, False
        self.shape, self.dtype = buffer.shape, buffer.dtype

    def send(self):
        if not self.sent:
            for copy in self.copies:
                copy.start()
        self.sent = True

    def wait(self):
        for copy in self.copies:
            copy.wait()

    def __getitem__(self, index):
        return self.buffer[index]

    def __setitem__(self, index, value):
        self.buffer[index] = value


def ready(*refs):
    for ref in refs:
        ref.ready()


def send(*refs):
    for ref in refs:
        ref.send()


def position(inner):
    index = lax.axis_index("dp")
    return index % inner


def call(body, outs, args, scratch=(), smem=0, flops=1):
    arrays, buffers, copies_in, here_in, here_out, loose = [], [], 0, set(), set(), set()
    for arg in args[smem:]:
        if isinstance(arg, Part):
            shape = list(arg.array.shape)
            shape[arg.axis] = arg.count
            arrays.append(arg.array)
            buffers.append(pltpu.VMEM(tuple(shape), arg.array.dtype))
            copies_in += 1
        elif isinstance(arg, Here):
            arrays.append(arg.what[0])
            here_in.add(len(arrays) - 1)
        elif isinstance(arg, Stack):
            first = arg.arrays[0]
            here_in.update(range(len(arrays), len(arrays) + len(arg.arrays)))
            loose.update(range(len(arrays), len(arrays) + len(arg.arrays)))
            arrays.extend(arg.arrays)
            buffers.append(pltpu.VMEM((len(arg.arrays),) + first.shape, first.dtype))
            copies_in += len(arg.arrays)
        else:
            arrays.append(arg)
            buffers.append(pltpu.VMEM(arg.shape, arg.dtype))
            copies_in += 1
    results, out_buffers, copies_out = [], [], 0
    for out in outs:
        if isinstance(out, Pieces):
            here_out.update(range(len(results), len(results) + out.count))
            results += [jax.ShapeDtypeStruct(out.shape, out.kind)] * out.count
            out_buffers.append(pltpu.VMEM((out.count,) + out.shape, out.kind))
            copies_out += out.count
        elif isinstance(out, Here):
            here_out.add(len(results))
            results.append(jax.ShapeDtypeStruct(*out.what))
        else:
            results.append(pltpu.HBM(*out))
            out_buffers.append(pltpu.VMEM(*out))
            copies_out += 1

    def kernel(*refs):
        refs = list(refs)
        scalars = [refs.pop(0) for _ in range(smem)]
        sources = [refs.pop(0) for _ in arrays]
        targets = [refs.pop(0) for _ in results]
        in_sems, out_sems = refs.pop(0), refs.pop(0)
        fetched, shipped = [], []
        count = 0
        for arg in args[smem:]:
            if isinstance(arg, Here):
                fetched.append(Fetched(sources.pop(0), ()))
                continue
            buffer = refs.pop(0)
            if isinstance(arg, Stack):
                copies = []
                near = position(len(arg.arrays))
                for k in range(len(arg.arrays)):
                    copies.append(
                        pltpu.make_async_copy(
                            sources.pop(0), buffer.at[k ^ near], in_sems.at[count]
                        )
                    )
                    count += 1
            else:
                source = sources.pop(0)
                if isinstance(arg, Part):
                    window = (slice(None),) * arg.axis + (pl.ds(arg.start, arg.count),)
                    source = source.at[window]
                copies = [pltpu.make_async_copy(source, buffer, in_sems.at[count])]
                count += 1
            fetched.append(Fetched(buffer, copies))
        count = 0
        for out in outs:
            if isinstance(out, Here):
                shipped.append(Shipped(targets.pop(0), ()))
                continue
            buffer = refs.pop(0)
            if isinstance(out, Pieces):
                ends = [(buffer.at[k], targets.pop(0)) for k in range(out.count)]
            else:
                ends = [(buffer, targets.pop(0))]
            copies = []
            for source, target in ends:
                copies.append(pltpu.make_async_copy(source, target, out_sems.at[count]))
                count += 1
            shipped.append(Shipped(buffer, copies))
        body(*scalars, *fetched, *shipped, *refs)
        ready(*fetched)
        send(*shipped)
        for ship in shipped:
            ship.wait()

    kernel.__name__ = body.__name__
    space = pltpu.MemorySpace.HBM
    got = pl.pallas_call(
        kernel,
        out_shape=results,
        in_specs=[pl.BlockSpec(memory_space=pltpu.SMEM) for _ in range(smem)]
        + [
            pl.BlockSpec(memory_space=pltpu.VMEM if i in here_in - loose else pl.ANY if i in loose else space)
            for i in range(len(arrays))
        ],
        out_specs=[
            pl.BlockSpec(memory_space=pltpu.VMEM if i in here_out else space)
            for i in range(len(results))
        ],
        scratch_shapes=[
            pltpu.SemaphoreType.DMA((max(copies_in, 1),)),
            pltpu.SemaphoreType.DMA((max(copies_out, 1),)),
        ]
        + buffers
        + out_buffers
        + list(scratch),
        compiler_params=pltpu.CompilerParams(vmem_limit_bytes=40 * 1024 * 1024),
        cost_estimate=pl.CostEstimate(flops=flops, bytes_accessed=1, transcendentals=0),
    )(
        *args[:smem],
        *(
            array if i in here_in else pltpu.with_memory_space_constraint(array, space)
            for i, array in enumerate(arrays)
        ),
    )
    final = []
    for out in outs:
        if isinstance(out, Pieces):
            final.append(list(got[: out.count]))
            got = got[out.count :]
        else:
            final.append(got[0])
            got = got[1:]
    return final


def call_here(body, outs, args, smem=0):
    return pl.pallas_call(
        body,
        out_shape=[jax.ShapeDtypeStruct(shape, kind) for shape, kind in outs],
        in_specs=[
            pl.BlockSpec(memory_space=pltpu.SMEM if i < smem else pltpu.VMEM) for i in range(len(args))
        ],
        out_specs=[pl.BlockSpec(memory_space=pltpu.VMEM) for _ in outs],
        compiler_params=pltpu.CompilerParams(vmem_limit_bytes=4 * 1024 * 1024),
    )(*args)


def permute_body(piece, dealing, source, target):
    for k in range(source.shape[0]):
        there = dealing[k]
        target[there, :piece, :] = source[k, :piece, :]
        target[k, piece:, :] = source[there, piece:, :]


def assemble(mine, theirs, spots, first, piece, target):
    side = lax.axis_index("tensor")
    half = spots * piece
    for source, base in ((mine, side * half), (theirs, (1 - side) * half)):
        for p in range(spots):
            target[pl.ds(pl.multiple_of(base + p * piece, piece), piece), :] = source[
                p, first : first + piece, :
            ]


def project(x, weights, biases, outs):
    for weight, bias, out in zip(weights, biases, outs):
        full = (mm(x, weight[...], NT) + bias[...].astype(WIDE)[None, :]).astype(LOW)
        for h in range(out.shape[0]):
            out[h] = full[:, h * HEAD_DIM : (h + 1) * HEAD_DIM]


def anti_diagonal():
    return jnp.where(
        lax.broadcasted_iota(jnp.int32, (BLOCK, BLOCK), 0)
        + lax.broadcasted_iota(jnp.int32, (BLOCK, BLOCK), 1)
        == BLOCK - 1,
        1.0,
        0.0,
    ).astype(LOW)


def one_hot(table, buckets):
    anti = anti_diagonal()
    entries = table[...]
    high = entries // 256
    turned = mm(high.astype(WIDE).astype(LOW), anti) * 256.0 + mm(
        (entries - high * 256).astype(WIDE).astype(LOW), anti
    )
    turned = turned.astype(jnp.int32)
    count = table.shape[0]
    rows = lax.broadcasted_iota(jnp.int32, (buckets, BLOCK), 0)
    return jnp.concatenate(
        [
            jnp.where(rows == turned[count - 1 - b : count - b, :], 1.0, 0.0).astype(LOW)
            for b in range(count)
        ],
        axis=1,
    )


def attend(length, count, q, k, v, tab, ctx, far_scratch, prob_out):
    rows = q.shape[1]
    window = rows + BLOCK
    scale = 1.0 / math.sqrt(3.0 * HEAD_DIM)
    key_ok = lax.broadcasted_iota(jnp.int32, (1, rows), 1) < length
    blocks = [slice(i * BLOCK, (i + 1) * BLOCK) for i in range(rows // BLOCK)]

    def head(h, carry):
        for here in blocks:
            w0 = rows - BLOCK - here.start
            far = mm(k[h, here, :], tab[0, h, :, w0 : w0 + window])
            far = pltpu.roll(far, window - BLOCK, 1, stride=1, stride_axis=0)[:, :rows]
            far_scratch[:, here] = far.T
        for here in blocks:
            w0 = rows - BLOCK - here.start
            near = mm(q[h, here, :], tab[1, h, :, w0 : w0 + window])
            near = pltpu.roll(near, window - BLOCK, 1, stride=1, stride_axis=0)[:, :rows]
            far_scratch[here, :] += near
        for here in blocks:
            score = (mm(q[h, here, :], k[h], NT) + far_scratch[here, :]) * scale
            score = jnp.where(key_ok, score, -1e30)
            top = jnp.max(score, axis=1, keepdims=True)
            weights = jnp.exp(score - top)
            row_ok = here.start + lax.broadcasted_iota(jnp.int32, (BLOCK, 1), 0) < length
            norm = jnp.where(row_ok, 1.0 / jnp.sum(weights, axis=1, keepdims=True), 0.0)
            prob = (weights * norm).astype(LOW)
            if prob_out is not None:
                prob_out[h, here, :] = prob
            ctx[h, here, :] = mm(prob, v[h]).astype(LOW)
        return carry

    lax.fori_loop(0, count, head, 0)


def attention_first(
    lengths, x, relative, table, wq, bq, wk, bk, wv, bv,
    q_out, k_out, v_out, tab_out, hot_out, prob_out, ctx_out, far_scratch,
):
    length = lengths[lax.axis_index("dp")]
    project(x[...], (wq, wk, wv), (bq, bk, bv), (q_out, k_out, v_out))
    send(q_out, k_out, v_out)
    rel = relative[...]
    hot = one_hot(table, relative.shape[0])
    hot_out[...] = hot
    for slot, (weight, bias) in enumerate(((wq, bq), (wk, bk))):
        low = (mm(rel, weight[...], NT) + bias[...].astype(WIDE)[None, :]).astype(LOW)
        spread = mm(low, hot, TN).astype(LOW)
        for h in range(q_out.shape[0]):
            tab_out[slot, h] = spread[h * HEAD_DIM : (h + 1) * HEAD_DIM]
    send(tab_out, hot_out)
    attend(length, ctx_out.shape[0], q_out, k_out, v_out, tab_out, ctx_out, far_scratch, prob_out)


def attention_rest(
    lengths, q, k, v, tab, wout, ctx_before, prob_out, ctx_out, attn_out, far_scratch
):
    length = lengths[lax.axis_index("dp")]
    ready(q, k, v, tab)
    attend(length, q.shape[0], q, k, v, tab, ctx_out, far_scratch, prob_out)
    send(prob_out)
    heads = [ctx_before[h] for h in range(ctx_before.shape[0])]
    heads += [ctx_out[h] for h in range(q.shape[0])]
    attn_out[...] = mm(jnp.concatenate(heads, axis=1), wout[...]).astype(LOW)


def attention_dealt(
    spots, piece, lengths, dealing, mine, theirs, tab, wq, bq, wk, bk, wv, bv, wout,
    x_out, attn_out, q, k, v, ctx, far_scratch,
):
    length = lengths[dealing[lax.axis_index("dp")]]
    assemble(mine, theirs, spots, piece, piece, x_out)
    send(x_out)
    project(x_out[...], (wq, wk, wv), (bq, bk, bv), (q, k, v))
    ready(tab)
    attend(length, q.shape[0], q, k, v, tab, ctx, far_scratch, None)
    heads = [ctx[h] for h in range(q.shape[0])]
    attn_out[...] = mm(jnp.concatenate(heads, axis=1), wout[...]).astype(LOW)


def row_norm(values):
    center = values - jnp.mean(values, axis=-1, keepdims=True)
    inverse = lax.rsqrt(jnp.mean(center * center, axis=-1, keepdims=True) + EPSILON)
    return center * inverse, inverse


def norm_back(scaled, normed, inverse):
    one = jnp.mean(scaled, axis=-1, keepdims=True)
    two = jnp.mean(scaled * normed, axis=-1, keepdims=True)
    return inverse * (scaled - one - normed * two)


def ffn_forward(
    keep, x, mine, theirs, bout, gain, shift, wup, bup, wdown, normed_out, down_out, *rest
):
    low_scratch, act_scratch = rest[-2:]
    if keep:
        inverse_out, hidden_out, act_out, slope_out = rest[:4]
    rows = x.shape[0]
    blocks = [slice(i * BLOCK, (i + 1) * BLOCK) for i in range(rows // BLOCK)]
    for here in blocks:
        attn = mine[here, :].astype(WIDE) + theirs[here, :].astype(WIDE) + wide_row(bout)
        normed, inverse = row_norm(x[here, :].astype(WIDE) + attn)
        normed_out[here, :] = normed
        low = (normed * wide_row(gain) + wide_row(shift)).astype(LOW)
        low_scratch[here, :] = low
        if keep:
            inverse_out[here, :] = inverse
            hidden_out[here, :] = low
    send(normed_out)
    for here in blocks:
        u = mm(low_scratch[here, :], wup[...]) + wide_row(bup)
        cdf = 0.5 * (1.0 + lax.erf(u * ROOT_HALF))
        act = (u * cdf).astype(LOW)
        act_scratch[here, :] = act
        if keep:
            act_out[here, :] = act
            density = jnp.exp(-0.5 * u * u) * INV_ROOT_TAU
            slope_out[here, :] = (cdf + u * density).astype(LOW)
    if keep:
        send(inverse_out, hidden_out, act_out, slope_out)
    for here in blocks:
        down_out[here, :] = mm(act_scratch[here, :], wdown[...]).astype(LOW)


def wide_row(vector):
    return vector[...].astype(WIDE)[None, :]


def second_norm(here, mine, theirs, bdown, normed, gain, shift):
    f = mine[here, :].astype(WIDE) + theirs[here, :].astype(WIDE) + wide_row(bdown)
    return row_norm(normed[here, :] * wide_row(gain) + wide_row(shift) + f)


def finish_dealt(mine, theirs, bdown, normed, gain, shift, fgain, fshift, y_out):
    for i in range(normed.shape[0] // BLOCK):
        here = slice(i * BLOCK, (i + 1) * BLOCK)
        n2, _ = second_norm(here, mine, theirs, bdown, normed, gain, shift)
        y_out[here, :] = (n2 * wide_row(fgain) + wide_row(fshift)).astype(LOW)


def put(buffer, chunk, first, value):
    near = position(buffer.shape[0])
    for place, offset, start, take in pieces(first, value.shape[0], chunk):
        buffer[place ^ near, offset : offset + take, :] = value[start : start + take]


def put_zeros(buffer, chunk, first):
    inner, _, width = buffer.shape
    left = inner * chunk - first
    if left > 0:
        put(buffer, chunk, first, jnp.zeros((left, width), buffer.dtype))


def ffn_backward(
    chunk, spots, piece, lengths,
    mine, theirs, bdown, normed, gain, shift, fgain, cot_mine, cot_theirs,
    hidden, act, slope, wup, wdown,
    part_out, gf_out, small_out, buffer_out, low_scratch, gu_scratch, cot_scratch,
):
    length = lengths[lax.axis_index("dp")]
    rows, width = normed.shape
    units = act.shape[1]
    assemble(cot_mine, cot_theirs, spots, 0, piece, cot_scratch)
    sums = [jnp.zeros((1, width), WIDE) for _ in range(3)]
    for i in range(rows // BLOCK):
        here = slice(i * BLOCK, (i + 1) * BLOCK)
        n2, r2 = second_norm(here, mine, theirs, bdown, normed, gain, shift)
        row_ok = i * BLOCK + lax.broadcasted_iota(jnp.int32, (BLOCK, 1), 0) < length
        gy = jnp.where(row_ok, cot_scratch[here, :].astype(WIDE), 0.0)
        gf = norm_back(gy * wide_row(fgain), n2, r2)
        gf_out[here, :] = gf
        low = gf.astype(LOW)
        low_scratch[here, :] = low
        sums[0] += jnp.sum(low.astype(WIDE), axis=0, keepdims=True)
        sums[1] += jnp.sum(gy * n2, axis=0, keepdims=True)
        sums[2] += jnp.sum(gy, axis=0, keepdims=True)
    send(gf_out)
    gu_sum = jnp.zeros((1, units), WIDE)
    for i in range(rows // BLOCK):
        here = slice(i * BLOCK, (i + 1) * BLOCK)
        gu = (mm(low_scratch[here, :], wdown[...], NT) * slope[here, :].astype(WIDE)).astype(LOW)
        gu_scratch[here, :] = gu
        gu_sum += jnp.sum(gu.astype(WIDE), axis=0, keepdims=True)
        part_out[here, :] = mm(gu, wup[...], NT).astype(LOW)
    send(part_out)
    small_out[...] = jnp.zeros(small_out.shape, WIDE)
    for k in range(units // width):
        small_out[k : k + 1, :] = gu_sum[:, k * width : (k + 1) * width]
    for k in range(3):
        small_out[units // width + k : units // width + k + 1, :] = sums[k]
    put(buffer_out, chunk, units, mm(act[...], low_scratch[...], TN).astype(LOW))
    for k in range(units // width):
        columns = slice(k * width, (k + 1) * width)
        put(
            buffer_out, chunk, k * width,
            mm(hidden[...], gu_scratch[:, columns], TN).astype(LOW),
        )
    put_zeros(buffer_out, chunk, 2 * units)


def head_backward(
    h, q, k, v, tab, prob, gctx, anti, g_out, gpq_out, gpk_out,
    gs_scratch, gp_scratch, turned_scratch, moved_scratch,
):
    rows = q.shape[1]
    span = tab.shape[3]
    window = rows + BLOCK
    scale = 1.0 / math.sqrt(3.0 * HEAD_DIM)
    blocks = [slice(i * BLOCK, (i + 1) * BLOCK) for i in range(rows // BLOCK)]
    pad = jnp.zeros((BLOCK, BLOCK), WIDE)
    for here in blocks:
        weights = prob[h, here, :].astype(WIDE)
        gprob = mm(gctx[h, here, :], v[h], NT)
        dots = jnp.sum(weights * gprob, axis=1, keepdims=True)
        gs_scratch[here, :] = (weights * (gprob - dots)).astype(LOW)
    g_out[2, h] = mm(prob[h], gctx[h], TN).astype(LOW)
    for slot, (source, other) in enumerate(((q, k), (k, q))):
        for here in blocks:
            if slot == 0:
                turned = mm(anti, gs_scratch[here, :])
            else:
                turned = mm(anti, gs_scratch[:, here], NT)
            turned_scratch[slot, here, :] = turned.astype(LOW)
            moved_scratch[slot, here, :] = pltpu.roll(
                jnp.concatenate([turned, pad], axis=1), 1, 1, stride=1, stride_axis=0
            ).astype(LOW)
    gp_scratch[...] = jnp.zeros((2, HEAD_DIM, span), WIDE)
    for slot, (source, other) in enumerate(((q, k), (k, q))):
        for here in blocks:
            w0 = rows - BLOCK - here.start
            moved = moved_scratch[slot, here, :]
            table_here = tab[1 - slot, h, :, w0 : w0 + window]
            grad = (mm(turned_scratch[slot, here, :], other[h]) + mm(moved, table_here, NT)) * scale
            g_out[slot, h, here, :] = mm(anti, grad.astype(LOW)).astype(LOW)
            turned = mm(anti, source[h, here, :]).astype(LOW)
            gp_scratch[1 - slot, :, w0 : w0 + window] += mm(turned, moved, TN)
    gpq_out[h] = gp_scratch[0].astype(LOW)
    gpk_out[h] = gp_scratch[1].astype(LOW)


def attention_backward(
    wout, mine, theirs, gf, normed, inverse, gain, ctx, ctx_last, q, k, v, tab, prob,
    gp_out, wout_out, small_out, gctx_out, g_out, gpq_out, gpk_out,
    gpb_scratch, gctx_scratch, *scratch,
):
    first, rows, _ = ctx.shape
    heads = first + 1
    width = gp_out.shape[1]
    blocks = rows // BLOCK
    sums = [jnp.zeros((1, width), WIDE) for _ in range(3)]
    for i in range(blocks):
        here = slice(i * BLOCK, (i + 1) * BLOCK)
        gh = gf[here, :] + (mine[here, :].astype(WIDE) + theirs[here, :].astype(WIDE))
        n1 = normed[here, :]
        gp = norm_back(gh * wide_row(gain), n1, inverse[here, :])
        gp_out[here, :] = gp
        low = gp.astype(LOW)
        gpb_scratch[here, :] = low
        sums[0] += jnp.sum(low.astype(WIDE), axis=0, keepdims=True)
        sums[1] += jnp.sum(gh * n1, axis=0, keepdims=True)
        sums[2] += jnp.sum(gh, axis=0, keepdims=True)
        grad = mm(low, wout[...], NT).astype(LOW)
        for h in range(heads):
            part = grad[:, h * HEAD_DIM : (h + 1) * HEAD_DIM]
            if h < first:
                gctx_scratch[h, here, :] = part
            else:
                gctx_out[0, here, :] = part
    small_out[...] = jnp.zeros(small_out.shape, WIDE)
    for n in range(3):
        small_out[2 + n : 3 + n, :] = sums[n]
    for h in range(heads):
        wout_out[h * HEAD_DIM : (h + 1) * HEAD_DIM, :] = mm(
            ctx[h] if h < first else ctx_last[0], gpb_scratch[...], TN
        ).astype(LOW)
    send(gp_out, small_out, wout_out, gctx_out)
    anti = anti_diagonal()
    ready(q, k, v, tab, prob)

    def head(h, carry):
        head_backward(
            h, q, k, v, tab, prob, gctx_scratch, anti, g_out, gpq_out, gpk_out, *scratch
        )
        return carry

    lax.fori_loop(0, first, head, 0)


def attention_backward_last(
    hot, wq, wk, wv, gctx, q, k, v, tab, prob, before, gpq_before, gpk_before,
    g_out, gpq_out, gpk_out, send_out, keep_out,
    gpq_scratch, gpk_scratch, rel_scratch, *scratch,
):
    side = lax.axis_index("tensor")
    buckets = rel_scratch.shape[0]
    half = buckets // 2
    scale = 1.0 / math.sqrt(3.0 * HEAD_DIM)
    anti = anti_diagonal()
    head_backward(
        0, q, k, v, tab, prob, gctx, anti, g_out, gpq_scratch, gpk_scratch, *scratch
    )
    send(g_out)
    for first, here, out in (
        (gpq_before, gpq_scratch, gpq_out), (gpk_before, gpk_scratch, gpk_out)
    ):
        parts = [first[h] for h in range(first.shape[0])] + [here[0]]
        out[...] = mm(hot[...], jnp.concatenate(parts, axis=0), NT) * scale
    rel_scratch[...] = mm(gpq_out[...].astype(LOW), wq[...]) + mm(gpk_out[...].astype(LOW), wk[...])
    send(gpq_out, gpk_out)
    rows = buckets
    send_out[rows:, :] = rel_scratch[
        pl.ds(pl.multiple_of((1 - side) * half, half), half), :
    ].astype(LOW)
    keep_out[...] = rel_scratch[pl.ds(pl.multiple_of(side * half, half), half), :].astype(LOW)
    send_out[:rows, :] = (
        mm(together(0, before, g_out), wq[...])
        + mm(together(1, before, g_out), wk[...])
        + mm(together(2, before, g_out), wv[...])
    ).astype(LOW)


def together(slot, before, last):
    parts = [before[slot, h] for h in range(before.shape[1])] + [last[slot, 0]]
    return jnp.concatenate(parts, axis=1)


def weight_gradients(
    chunk, x, relative, before, last, gpq, gpk, wout_grad, small_ffn, small_attn, keep, got,
    buffer_out,
):
    part = gpq.shape[1]
    xv = x[...]
    rel = relative[...]
    gq, gk, gv = (together(slot, before, last) for slot in range(3))
    put(
        buffer_out, chunk, 0,
        (mm(gq, xv, TN) + mm(gpq[...].astype(LOW), rel, TN)).astype(LOW),
    )
    put(
        buffer_out, chunk, part,
        (mm(gk, xv, TN) + mm(gpk[...].astype(LOW), rel, TN)).astype(LOW),
    )
    put(buffer_out, chunk, 2 * part, mm(gv, xv, TN).astype(LOW))
    put(buffer_out, chunk, 3 * part, wout_grad[...])
    half = keep.shape[0]
    both = (keep[...].astype(WIDE) + got[got.shape[0] - half :, :].astype(WIDE)).astype(LOW)
    put(buffer_out, chunk, 4 * part, both)
    count = 4 * part + keep.shape[0]
    bias = [
        jnp.sum(gq.astype(WIDE), axis=0, keepdims=True) + jnp.sum(gpq[...], axis=0, keepdims=True),
        jnp.sum(gk.astype(WIDE), axis=0, keepdims=True) + jnp.sum(gpk[...], axis=0, keepdims=True),
        jnp.sum(gv.astype(WIDE), axis=0, keepdims=True),
    ]
    second = jnp.concatenate([bias[2], jnp.zeros_like(bias[2])], axis=1)
    small = jnp.concatenate(
        [small_ffn[...], jnp.concatenate(bias[:2], axis=1), second, small_attn[2:, :]], axis=0
    ).astype(LOW)
    put(buffer_out, chunk, count, small)
    put_zeros(buffer_out, chunk, count + small.shape[0])


def finish_tokens(gp, mine, theirs, grad_out):
    for i in range(gp.shape[0] // BLOCK):
        here = slice(i * BLOCK, (i + 1) * BLOCK)
        both = mine[here, :].astype(WIDE) + theirs[here, :].astype(WIDE)
        grad_out[here, :] = (gp[here, :] + both).astype(LOW)


def chunks(gathered, first, count):
    for place, offset, start, take in pieces(first, count, gathered.shape[1]):
        yield start, take, gathered[place, offset : offset + take, :].astype(WIDE)


def unpack_ffn(gathered, wup_out, wdown_out):
    width, units = wup_out.shape
    for start, take, value in chunks(gathered, units, units):
        wdown_out[start : start + take, :] = value
    send(wdown_out)
    for k in range(units // width):
        for start, take, value in chunks(gathered, k * width, width):
            wup_out[start : start + take, k * width : (k + 1) * width] = value


def unpack_relative(first, gathered, rel_out):
    for start, take, value in chunks(gathered, first, rel_out.shape[0]):
        rel_out[start : start + take, :] = value.astype(LOW)


def unpack_attention(
    first, gathered, wq_out, wk_out, wv_out, wout_out, bup_out,
    bq_out, bk_out, bv_out, bout_out, again_out, ashift_out, bdown_out, fgain_out, fshift_out,
):
    part, width = wq_out.shape
    units = bup_out.shape[0]
    for k, out in enumerate((wq_out, wk_out, wv_out, wout_out)):
        for start, take, value in chunks(gathered, k * part, part):
            out[start : start + take, :] = value
        send(out)
    small = jnp.concatenate([value for _, _, value in chunks(gathered, first, 16)], axis=0)
    ups = units // width
    for k in range(ups):
        bup_out[k * width : (k + 1) * width] = small[k]
    bdown_out[...] = small[ups]
    fgain_out[...] = small[ups + 1]
    fshift_out[...] = small[ups + 2]
    bq_out[...] = small[8, :part]
    bk_out[...] = small[8, part:]
    bv_out[...] = small[9, :part]
    bout_out[...] = small[10]
    again_out[...] = small[11]
    ashift_out[...] = small[12]


def join_relative(mine, theirs, out):
    side = lax.axis_index("tensor")
    half = mine.shape[0]
    out[pl.ds(pl.multiple_of(side * half, half), half), :] = mine[...].astype(WIDE)
    out[pl.ds(pl.multiple_of((1 - side) * half, half), half), :] = theirs[...].astype(WIDE)


def with_statics(body, *statics):
    def wrapped(*refs):
        body(*statics, *refs)

    wrapped.__name__ = body.__name__
    return wrapped


def swap(array):
    return lax.ppermute(array, "tensor", [(0, 1), (1, 0)])


def exchange(array):
    return lax.all_to_all(array, "dp", split_axis=0, concat_axis=0, tiled=True)


def trade(arrays, groups):
    got = []
    for k, array in enumerate(arrays, 1):
        pairs = [(group[p], group[p ^ k]) for group in groups for p in range(len(group))]
        got.append(lax.ppermute(array, "dp", pairs))
    return got


def after(value, *others):
    return lax.optimization_barrier((value,) + others)[0]


class Sequence:
    def __init__(self):
        self.last = None

    def run(self, body, outs, args, scratch=(), smem=0, flops=1):
        args = list(args)
        if self.last is not None:
            free = [i for i in range(smem, len(args)) if not isinstance(args[i], (Here, Stack))]
            if free:
                arg = args[free[0]]
                if isinstance(arg, Part):
                    args[free[0]] = Part(after(arg.array, self.last), arg.axis, arg.start, arg.count)
                else:
                    args[free[0]] = after(arg, self.last)
            elif isinstance(args[smem], Stack):
                first = args[smem].arrays
                args[smem] = Stack((after(first[0], self.last),) + first[1:])
            else:
                args[smem] = Here(after(args[smem].what[0], self.last))
        got = call(body, outs, args, scratch, smem, flops)
        self.last = got[0][0] if isinstance(got[0], list) else got[0]
        return got


def on_device(
    tokens, lengths, dealing, bucket_table, relative,
    w_query, b_query, w_key, b_key, w_value, b_value, w_out, b_out,
    attn_gain, attn_shift, w_up, b_up, w_down, b_down, ffn_gain, ffn_shift, cotangent,
):
    _, rows, width = tokens.shape
    total = dealing.shape[0]
    part = w_query.shape[1]
    heads = part // HEAD_DIM
    before = heads - 1
    units = w_up.shape[1]
    half = rows // 2
    span = 2 * rows
    piece = max(16, half // total)
    spots = half // piece
    side = lax.axis_index("tensor")
    inner = 1 << ((total.bit_length()) // 2)
    outer = total // inner
    near_groups = [[o * inner + i for i in range(inner)] for o in range(outer)]
    chunk_one = chunk_rows(2 * units, inner, 16)
    chunk_two = chunk_rows(4 * part + half + 16, inner, 16)

    sequence = Sequence()
    run = sequence.run

    def cut(array):
        mine = lax.dynamic_slice_in_dim(array[0], side * half, half, 0)
        return mine.reshape(spots, piece, width)

    moving = jnp.concatenate([cut(cotangent), cut(tokens)], axis=1)
    if spots < total:
        moving = jnp.pad(moving, ((0, total - spots), (0, 0), (0, 0)))
    arrived = exchange(moving)
    x = tokens[0]
    table = jnp.pad(bucket_table, (0, span - bucket_table.shape[0]), constant_values=-1)
    table = table.reshape(span // BLOCK, BLOCK)
    projections = (w_query.T, b_query, w_key.T, b_key, w_value.T, b_value, w_out)
    head_shape = (heads, rows, HEAD_DIM)
    q, k, v, tab, hot, prob, ctx = run(
        attention_first,
        [(head_shape, LOW)] * 3
        + [((2, heads, HEAD_DIM, span), LOW), ((relative.shape[0], span), LOW), ((before, rows, rows), LOW),
           ((before, rows, HEAD_DIM), LOW)],
        (lengths, x, relative, table) + projections[:6],
        scratch=[pltpu.VMEM((rows, rows), WIDE)],
        smem=1,
    )
    arrived = after(arrived, sequence.last)
    (turned,) = call_here(
        with_statics(permute_body, piece), [(arrived.shape, LOW)], (dealing, arrived), smem=1
    )
    sequence.last = turned
    dealt_mine = exchange(turned)
    dealt_theirs = swap(dealt_mine)
    prob_last, ctx_last, attn_part = run(
        attention_rest,
        [((1, rows, rows), LOW), ((1, rows, HEAD_DIM), LOW), Here((rows, width), LOW)],
        (lengths,)
        + tuple(Part(array, 0, before, 1) for array in (q, k, v))
        + (Part(tab, 1, before, 1), w_out, ctx),
        scratch=[pltpu.VMEM((rows, rows), WIDE)],
        smem=1,
    )
    attn_got = swap(attn_part)
    ffn_weights = (b_out, attn_gain, attn_shift, w_up, b_up, w_down)
    normed, down_part, inverse, hidden, act, slope = run(
        with_statics(ffn_forward, True),
        [((rows, width), WIDE), Here((rows, width), LOW), ((rows, 1), WIDE), ((rows, width), LOW),
         ((rows, units), LOW), ((rows, units), LOW)],
        (x, Here(attn_part), Here(attn_got)) + ffn_weights,
        scratch=[pltpu.VMEM((rows, width), LOW), pltpu.VMEM((rows, units), LOW)],
    )
    down_got = swap(down_part)
    hidden_part, gf, small_ffn, near_one = run(
        with_statics(ffn_backward, chunk_one, spots, piece),
        [Here((rows, width), LOW), ((rows, width), WIDE), ((8, width), WIDE),
         Pieces(inner, (chunk_one, width), LOW)],
        (lengths, Here(down_part), Here(down_got), b_down, normed, attn_gain, attn_shift,
         ffn_gain, Here(dealt_mine), Here(dealt_theirs), hidden, act, slope, w_up, w_down),
        scratch=[
            pltpu.VMEM((rows, width), LOW),
            pltpu.VMEM((rows, units), LOW),
            pltpu.VMEM((rows, width), LOW),
        ],
        smem=1,
    )
    hidden_got = swap(hidden_part)
    near_one[1:] = trade(near_one[1:], near_groups)

    def total_of(own, got):
        acc = after(own, sequence.last).astype(WIDE)
        for other in got:
            acc += other.astype(WIDE)
        sequence.last = acc.astype(LOW)
        return sequence.last

    def far_step(array, step):
        reach = inner << step
        return lax.ppermute(array, "dp", [(p, p ^ reach) for p in range(total)])

    steps = outer.bit_length() - 1

    def gather_near(line):
        return Stack([line] + trade([line] * (inner - 1), near_groups))

    head_scratch = [
        pltpu.VMEM((rows, rows), LOW),
        pltpu.VMEM((2, HEAD_DIM, span), WIDE),
        pltpu.VMEM((2, rows, rows), LOW),
        pltpu.VMEM((2, rows, rows + BLOCK), LOW),
    ]
    gp, wout_grad, small_attn, gctx, g_before, gpq_before, gpk_before = run(
        attention_backward,
        [((rows, width), WIDE), ((part, width), LOW), ((8, width), WIDE),
         ((1, rows, HEAD_DIM), LOW), ((3, before, rows, HEAD_DIM), LOW),
         ((before, HEAD_DIM, span), LOW), ((before, HEAD_DIM, span), LOW)],
        (w_out, Here(hidden_part), Here(hidden_got), gf, normed, inverse, attn_gain, ctx, ctx_last)
        + tuple(Part(array, 0, 0, before) for array in (q, k, v))
        + (Part(tab, 1, 0, before), prob),
        scratch=[
            pltpu.VMEM((rows, width), LOW),
            pltpu.VMEM((before, rows, HEAD_DIM), LOW),
        ]
        + head_scratch,
    )
    line_one = total_of(near_one[0], near_one[1:])
    got_one = far_step(line_one, 0)
    g_last, gpq, gpk, send_part, rel_keep = run(
        attention_backward_last,
        [((3, 1, rows, HEAD_DIM), LOW), ((rows, part), WIDE), ((rows, part), WIDE),
         ((rows + half, width), LOW), ((half, width), LOW)],
        (hot, w_query.T, w_key.T, w_value.T, gctx)
        + tuple(Part(array, 0, before, 1) for array in (q, k, v))
        + (Part(tab, 1, before, 1), prob_last, g_before, gpq_before, gpk_before),
        scratch=[
            pltpu.VMEM((1, HEAD_DIM, span), LOW),
            pltpu.VMEM((1, HEAD_DIM, span), LOW),
            pltpu.VMEM((rows, width), WIDE),
        ]
        + head_scratch,
    )
    for step in range(1, steps):
        line_one = total_of(line_one, [got_one])
        got_one = far_step(line_one, step)
    send_got = swap(after(send_part, line_one))
    (near_two,) = run(
        with_statics(weight_gradients, chunk_two),
        [Pieces(inner, (chunk_two, width), LOW)],
        (x, relative, g_before, g_last, gpq, gpk, wout_grad, small_ffn, small_attn, rel_keep,
         Here(send_got)),
    )
    near_two[1:] = trade(near_two[1:], near_groups)

    x_dealt, attn_dealt = run(
        with_statics(attention_dealt, spots, piece),
        [((rows, width), LOW), Here((rows, width), LOW)],
        (lengths, dealing, dealt_mine, dealt_theirs, tab) + projections,
        scratch=[pltpu.VMEM(head_shape, LOW) for _ in range(4)] + [pltpu.VMEM((rows, rows), WIDE)],
        smem=2,
    )
    line_one, *near_two[1:] = lax.optimization_barrier((line_one, *near_two[1:]))
    line_one = total_of(line_one, [got_one])
    line_two = total_of(near_two[0], near_two[1:])
    got_two = far_step(line_two, 0)
    all_one = gather_near(line_one)
    attn_dealt_got = swap(after(attn_dealt, line_two))
    normed_dealt, down_dealt = run(
        with_statics(ffn_forward, False),
        [((rows, width), WIDE), Here((rows, width), LOW)],
        (x_dealt, Here(attn_dealt), Here(attn_dealt_got)) + ffn_weights,
        scratch=[pltpu.VMEM((rows, width), LOW), pltpu.VMEM((rows, units), LOW)],
    )
    for step in range(1, steps):
        line_two = total_of(line_two, [got_two])
        got_two = far_step(line_two, step)
    down_dealt_got = swap(after(down_dealt, line_two))
    (grad_tokens,) = run(
        finish_tokens,
        [((rows, width), LOW)],
        (gp, Part(send_part, 0, 0, rows), Part(send_got, 0, 0, rows)),
        flops=6 * 10**9,
    )
    (y,) = run(
        finish_dealt,
        [((rows, width), LOW)],
        (Here(down_dealt), Here(down_dealt_got), b_down, normed_dealt, attn_gain, attn_shift,
         ffn_gain, ffn_shift),
        flops=6 * 10**9,
    )
    g_up, g_down = run(
        unpack_ffn, [((width, units), WIDE), ((units, width), WIDE)], (all_one,),
        flops=6 * 10**9,
    )
    line_two = total_of(line_two, [got_two])
    all_two = gather_near(line_two)
    first = 4 * part
    (rel_half,) = run(with_statics(unpack_relative, first), [Here((half, width), LOW)], (all_two,))
    rel_other = swap(rel_half)
    g_wq, g_wk, g_wv, g_wout, g_bup, g_bq, g_bk, g_bv, g_bout, g_again, g_ashift, g_bdown, g_fgain, g_fshift = run(
        with_statics(unpack_attention, first + half),
        [((part, width), WIDE)] * 4
        + [((units,), WIDE)]
        + [((part,), WIDE)] * 3
        + [((width,), WIDE)] * 6,
        (all_two,),
    )
    (g_rel,) = run(join_relative, [((rows, width), WIDE)], (Here(rel_half), Here(rel_other)))
    return (
        y[None], grad_tokens[None], g_rel, g_wq.T, g_bq, g_wk.T, g_bk, g_wv.T, g_bv, g_wout,
        g_bout, g_again, g_ashift, g_up, g_bup, g_down, g_bdown, g_fgain, g_fshift,
    )


def solution(mesh):
    return jax.shard_map(
        on_device,
        mesh=mesh,
        in_specs=(
            P("dp", None, None), P(), P(), P(), P(),
            P(None, "tensor"), P("tensor"), P(None, "tensor"), P("tensor"),
            P(None, "tensor"), P("tensor"), P("tensor", None), P(), P(), P(),
            P(None, "tensor"), P("tensor"), P("tensor", None), P(), P(), P(),
            P("dp", None, None),
        ),
        out_specs=(
            P("dp", None, None), P("dp", None, None), P(),
            P(None, "tensor"), P("tensor"), P(None, "tensor"), P("tensor"),
            P(None, "tensor"), P("tensor"), P("tensor", None), P(), P(), P(),
            P(None, "tensor"), P("tensor"), P("tensor", None), P(), P(), P(),
        ),
        check_vma=False,
    )
```

```python
import math

import jax
import jax.numpy as jnp
from jax import lax
from jax.experimental import pallas as pl
from jax.experimental.pallas import tpu as pltpu
from jax.sharding import PartitionSpec as P

HEAD_DIM = 64
EPSILON = 1e-07
ROOT_HALF = 0.7071067811865476
INV_ROOT_TAU = 0.3989422804014327
BLOCK = 128
LOW = jnp.bfloat16
WIDE = jnp.float32

NN = (((1,), (0,)), ((), ()))
NT = (((1,), (1,)), ((), ()))
TN = (((0,), (0,)), ((), ()))
TT = (((0,), (1,)), ((), ()))


def mm(left, right, dims=NN):
    return lax.dot_general(left, right, dims, preferred_element_type=WIDE)


def pieces(first, count, chunk):
    out = []
    done = 0
    while done < count:
        place, offset = divmod(first + done, chunk)
        take = min(chunk - offset, count - done)
        out.append((place, offset, done, take))
        done += take
    return out


def chunk_rows(rows, parts, unit):
    return -(-(-(-rows // parts)) // unit) * unit


class Part:
    def __init__(self, array, axis, start, count):
        self.array, self.axis, self.start, self.count = array, axis, start, count


class Stack:
    def __init__(self, arrays):
        self.arrays = tuple(arrays)


class Here:
    def __init__(self, *what):
        self.what = what


class Pieces:
    def __init__(self, count, shape, kind):
        self.count, self.shape, self.kind = count, shape, kind


class Fetched:
    def __init__(self, buffer, copies):
        self.buffer, self.copies = buffer, copies
        self.shape, self.dtype = buffer.shape, buffer.dtype
        for copy in copies:
            copy.start()

    def ready(self):
        for copy in self.copies:
            copy.wait()
        self.copies = ()

    def __getitem__(self, index):
        self.ready()
        return self.buffer[index]


class Shipped:
    def __init__(self, buffer, copies):
        self.buffer, self.copies, self.sent = buffer, copies, False
        self.shape, self.dtype = buffer.shape, buffer.dtype

    def send(self):
        if not self.sent:
            for copy in self.copies:
                copy.start()
        self.sent = True

    def wait(self):
        for copy in self.copies:
            copy.wait()

    def __getitem__(self, index):
        return self.buffer[index]

    def __setitem__(self, index, value):
        self.buffer[index] = value


def ready(*refs):
    for ref in refs:
        ref.ready()


def send(*refs):
    for ref in refs:
        ref.send()


def position(inner):
    index = lax.axis_index("dp")
    return index % inner


def call(body, outs, args, scratch=(), smem=0, flops=1):
    arrays, buffers, copies_in, here_in, here_out, loose = [], [], 0, set(), set(), set()
    for arg in args[smem:]:
        if isinstance(arg, Part):
            shape = list(arg.array.shape)
            shape[arg.axis] = arg.count
            arrays.append(arg.array)
            buffers.append(pltpu.VMEM(tuple(shape), arg.array.dtype))
            copies_in += 1
        elif isinstance(arg, Here):
            arrays.append(arg.what[0])
            here_in.add(len(arrays) - 1)
        elif isinstance(arg, Stack):
            first = arg.arrays[0]
            here_in.update(range(len(arrays), len(arrays) + len(arg.arrays)))
            loose.update(range(len(arrays), len(arrays) + len(arg.arrays)))
            arrays.extend(arg.arrays)
            buffers.append(pltpu.VMEM((len(arg.arrays),) + first.shape, first.dtype))
            copies_in += len(arg.arrays)
        else:
            arrays.append(arg)
            buffers.append(pltpu.VMEM(arg.shape, arg.dtype))
            copies_in += 1
    results, out_buffers, copies_out = [], [], 0
    for out in outs:
        if isinstance(out, Pieces):
            here_out.update(range(len(results), len(results) + out.count))
            results += [jax.ShapeDtypeStruct(out.shape, out.kind)] * out.count
            out_buffers.append(pltpu.VMEM((out.count,) + out.shape, out.kind))
            copies_out += out.count
        elif isinstance(out, Here):
            here_out.add(len(results))
            results.append(jax.ShapeDtypeStruct(*out.what))
        else:
            results.append(pltpu.HBM(*out))
            out_buffers.append(pltpu.VMEM(*out))
            copies_out += 1

    def kernel(*refs):
        refs = list(refs)
        scalars = [refs.pop(0) for _ in range(smem)]
        sources = [refs.pop(0) for _ in arrays]
        targets = [refs.pop(0) for _ in results]
        in_sems, out_sems = refs.pop(0), refs.pop(0)
        fetched, shipped = [], []
        count = 0
        for arg in args[smem:]:
            if isinstance(arg, Here):
                fetched.append(Fetched(sources.pop(0), ()))
                continue
            buffer = refs.pop(0)
            if isinstance(arg, Stack):
                copies = []
                near = position(len(arg.arrays))
                for k in range(len(arg.arrays)):
                    copies.append(
                        pltpu.make_async_copy(
                            sources.pop(0), buffer.at[k ^ near], in_sems.at[count]
                        )
                    )
                    count += 1
            else:
                source = sources.pop(0)
                if isinstance(arg, Part):
                    window = (slice(None),) * arg.axis + (pl.ds(arg.start, arg.count),)
                    source = source.at[window]
                copies = [pltpu.make_async_copy(source, buffer, in_sems.at[count])]
                count += 1
            fetched.append(Fetched(buffer, copies))
        count = 0
        for out in outs:
            if isinstance(out, Here):
                shipped.append(Shipped(targets.pop(0), ()))
                continue
            buffer = refs.pop(0)
            if isinstance(out, Pieces):
                ends = [(buffer.at[k], targets.pop(0)) for k in range(out.count)]
            else:
                ends = [(buffer, targets.pop(0))]
            copies = []
            for source, target in ends:
                copies.append(pltpu.make_async_copy(source, target, out_sems.at[count]))
                count += 1
            shipped.append(Shipped(buffer, copies))
        body(*scalars, *fetched, *shipped, *refs)
        ready(*fetched)
        send(*shipped)
        for ship in shipped:
            ship.wait()

    kernel.__name__ = body.__name__
    space = pltpu.MemorySpace.HBM
    got = pl.pallas_call(
        kernel,
        out_shape=results,
        in_specs=[pl.BlockSpec(memory_space=pltpu.SMEM) for _ in range(smem)]
        + [
            pl.BlockSpec(memory_space=pltpu.VMEM if i in here_in - loose else pl.ANY if i in loose else space)
            for i in range(len(arrays))
        ],
        out_specs=[
            pl.BlockSpec(memory_space=pltpu.VMEM if i in here_out else space)
            for i in range(len(results))
        ],
        scratch_shapes=[
            pltpu.SemaphoreType.DMA((max(copies_in, 1),)),
            pltpu.SemaphoreType.DMA((max(copies_out, 1),)),
        ]
        + buffers
        + out_buffers
        + list(scratch),
        compiler_params=pltpu.CompilerParams(vmem_limit_bytes=40 * 1024 * 1024),
        cost_estimate=pl.CostEstimate(flops=flops, bytes_accessed=1, transcendentals=0),
    )(
        *args[:smem],
        *(
            array if i in here_in else pltpu.with_memory_space_constraint(array, space)
            for i, array in enumerate(arrays)
        ),
    )
    final = []
    for out in outs:
        if isinstance(out, Pieces):
            final.append(list(got[: out.count]))
            got = got[out.count :]
        else:
            final.append(got[0])
            got = got[1:]
    return final


def call_here(body, outs, args, smem=0):
    return pl.pallas_call(
        body,
        out_shape=[jax.ShapeDtypeStruct(shape, kind) for shape, kind in outs],
        in_specs=[
            pl.BlockSpec(memory_space=pltpu.SMEM if i < smem else pltpu.VMEM) for i in range(len(args))
        ],
        out_specs=[pl.BlockSpec(memory_space=pltpu.VMEM) for _ in outs],
        compiler_params=pltpu.CompilerParams(vmem_limit_bytes=4 * 1024 * 1024),
    )(*args)


def permute_body(piece, dealing, source, target):
    for k in range(source.shape[0]):
        there = dealing[k]
        target[there, :piece, :] = source[k, :piece, :]
        target[k, piece:, :] = source[there, piece:, :]


def assemble(mine, theirs, spots, first, piece, target):
    side = lax.axis_index("tensor")
    half = spots * piece
    for source, base in ((mine, side * half), (theirs, (1 - side) * half)):
        for p in range(spots):
            target[pl.ds(pl.multiple_of(base + p * piece, piece), piece), :] = source[
                p, first : first + piece, :
            ]


def project(x, weights, biases, outs):
    for weight, bias, out in zip(weights, biases, outs):
        full = (mm(x, weight[...], NT) + bias[...].astype(WIDE)[None, :]).astype(LOW)
        for h in range(out.shape[0]):
            out[h] = full[:, h * HEAD_DIM : (h + 1) * HEAD_DIM]


def anti_diagonal():
    return jnp.where(
        lax.broadcasted_iota(jnp.int32, (BLOCK, BLOCK), 0)
        + lax.broadcasted_iota(jnp.int32, (BLOCK, BLOCK), 1)
        == BLOCK - 1,
        1.0,
        0.0,
    ).astype(LOW)


def one_hot(table, buckets):
    anti = anti_diagonal()
    entries = table[...]
    high = entries // 256
    turned = mm(high.astype(WIDE).astype(LOW), anti) * 256.0 + mm(
        (entries - high * 256).astype(WIDE).astype(LOW), anti
    )
    turned = turned.astype(jnp.int32)
    count = table.shape[0]
    rows = lax.broadcasted_iota(jnp.int32, (buckets, BLOCK), 0)
    return jnp.concatenate(
        [
            jnp.where(rows == turned[count - 1 - b : count - b, :], 1.0, 0.0).astype(LOW)
            for b in range(count)
        ],
        axis=1,
    )


def attend(length, count, q, k, v, tab, ctx, far_scratch, prob_out):
    rows = q.shape[1]
    window = rows + BLOCK
    scale = 1.0 / math.sqrt(3.0 * HEAD_DIM)
    key_ok = lax.broadcasted_iota(jnp.int32, (1, rows), 1) < length
    blocks = [slice(i * BLOCK, (i + 1) * BLOCK) for i in range(rows // BLOCK)]

    def head(h, carry):
        for here in blocks:
            w0 = rows - BLOCK - here.start
            far = mm(k[h, here, :], tab[0, h, :, w0 : w0 + window])
            far = pltpu.roll(far, window - BLOCK, 1, stride=1, stride_axis=0)[:, :rows]
            far_scratch[:, here] = far.T
        for here in blocks:
            w0 = rows - BLOCK - here.start
            near = mm(q[h, here, :], tab[1, h, :, w0 : w0 + window])
            near = pltpu.roll(near, window - BLOCK, 1, stride=1, stride_axis=0)[:, :rows]
            far_scratch[here, :] += near
        for here in blocks:
            score = (mm(q[h, here, :], k[h], NT) + far_scratch[here, :]) * scale
            score = jnp.where(key_ok, score, -1e30)
            top = jnp.max(score, axis=1, keepdims=True)
            weights = jnp.exp(score - top)
            row_ok = here.start + lax.broadcasted_iota(jnp.int32, (BLOCK, 1), 0) < length
            norm = jnp.where(row_ok, 1.0 / jnp.sum(weights, axis=1, keepdims=True), 0.0)
            prob = (weights * norm).astype(LOW)
            if prob_out is not None:
                prob_out[h, here, :] = prob
            ctx[h, here, :] = mm(prob, v[h]).astype(LOW)
        return carry

    lax.fori_loop(0, count, head, 0)


def attention_first(
    lengths, x, relative, table, wq, bq, wk, bk, wv, bv,
    q_out, k_out, v_out, tab_out, hot_out, prob_out, ctx_out, far_scratch,
):
    length = lengths[lax.axis_index("dp")]
    project(x[...], (wq, wk, wv), (bq, bk, bv), (q_out, k_out, v_out))
    send(q_out, k_out, v_out)
    rel = relative[...]
    hot = one_hot(table, relative.shape[0])
    hot_out[...] = hot
    for slot, (weight, bias) in enumerate(((wq, bq), (wk, bk))):
        low = (mm(rel, weight[...], NT) + bias[...].astype(WIDE)[None, :]).astype(LOW)
        spread = mm(low, hot, TN).astype(LOW)
        for h in range(q_out.shape[0]):
            tab_out[slot, h] = spread[h * HEAD_DIM : (h + 1) * HEAD_DIM]
    send(tab_out, hot_out)
    attend(length, ctx_out.shape[0], q_out, k_out, v_out, tab_out, ctx_out, far_scratch, prob_out)


def attention_rest(
    lengths, q, k, v, tab, wout, ctx_before, prob_out, ctx_out, attn_out, far_scratch
):
    length = lengths[lax.axis_index("dp")]
    ready(q, k, v, tab)
    attend(length, q.shape[0], q, k, v, tab, ctx_out, far_scratch, prob_out)
    send(prob_out)
    heads = [ctx_before[h] for h in range(ctx_before.shape[0])]
    heads += [ctx_out[h] for h in range(q.shape[0])]
    attn_out[...] = mm(jnp.concatenate(heads, axis=1), wout[...]).astype(LOW)


def attention_dealt(
    spots, piece, lengths, dealing, mine, theirs, tab, wq, bq, wk, bk, wv, bv, wout,
    x_out, attn_out, q, k, v, ctx, far_scratch,
):
    length = lengths[dealing[lax.axis_index("dp")]]
    assemble(mine, theirs, spots, piece, piece, x_out)
    send(x_out)
    project(x_out[...], (wq, wk, wv), (bq, bk, bv), (q, k, v))
    ready(tab)
    attend(length, q.shape[0], q, k, v, tab, ctx, far_scratch, None)
    heads = [ctx[h] for h in range(q.shape[0])]
    attn_out[...] = mm(jnp.concatenate(heads, axis=1), wout[...]).astype(LOW)


def row_norm(values):
    center = values - jnp.mean(values, axis=-1, keepdims=True)
    inverse = lax.rsqrt(jnp.mean(center * center, axis=-1, keepdims=True) + EPSILON)
    return center * inverse, inverse


def norm_back(scaled, normed, inverse):
    one = jnp.mean(scaled, axis=-1, keepdims=True)
    two = jnp.mean(scaled * normed, axis=-1, keepdims=True)
    return inverse * (scaled - one - normed * two)


def ffn_forward(
    keep, x, mine, theirs, bout, gain, shift, wup, bup, wdown, normed_out, down_out, *rest
):
    low_scratch, act_scratch = rest[-2:]
    if keep:
        inverse_out, hidden_out, act_out, slope_out = rest[:4]
    rows = x.shape[0]
    blocks = [slice(i * BLOCK, (i + 1) * BLOCK) for i in range(rows // BLOCK)]
    for here in blocks:
        attn = mine[here, :].astype(WIDE) + theirs[here, :].astype(WIDE) + wide_row(bout)
        normed, inverse = row_norm(x[here, :].astype(WIDE) + attn)
        normed_out[here, :] = normed
        low = (normed * wide_row(gain) + wide_row(shift)).astype(LOW)
        low_scratch[here, :] = low
        if keep:
            inverse_out[here, :] = inverse
            hidden_out[here, :] = low
    send(normed_out)
    for here in blocks:
        u = mm(low_scratch[here, :], wup[...]) + wide_row(bup)
        cdf = 0.5 * (1.0 + lax.erf(u * ROOT_HALF))
        act = (u * cdf).astype(LOW)
        act_scratch[here, :] = act
        if keep:
            act_out[here, :] = act
            density = jnp.exp(-0.5 * u * u) * INV_ROOT_TAU
            slope_out[here, :] = (cdf + u * density).astype(LOW)
    if keep:
        send(inverse_out, hidden_out, act_out, slope_out)
    for here in blocks:
        down_out[here, :] = mm(act_scratch[here, :], wdown[...]).astype(LOW)


def wide_row(vector):
    return vector[...].astype(WIDE)[None, :]


def second_norm(here, mine, theirs, bdown, normed, gain, shift):
    f = mine[here, :].astype(WIDE) + theirs[here, :].astype(WIDE) + wide_row(bdown)
    return row_norm(normed[here, :] * wide_row(gain) + wide_row(shift) + f)


def finish_dealt(mine, theirs, bdown, normed, gain, shift, fgain, fshift, y_out):
    for i in range(normed.shape[0] // BLOCK):
        here = slice(i * BLOCK, (i + 1) * BLOCK)
        n2, _ = second_norm(here, mine, theirs, bdown, normed, gain, shift)
        y_out[here, :] = (n2 * wide_row(fgain) + wide_row(fshift)).astype(LOW)


def put(buffer, chunk, first, value):
    near = position(buffer.shape[0])
    for place, offset, start, take in pieces(first, value.shape[0], chunk):
        buffer[place ^ near, offset : offset + take, :] = value[start : start + take]


def put_zeros(buffer, chunk, first):
    inner, _, width = buffer.shape
    left = inner * chunk - first
    if left > 0:
        put(buffer, chunk, first, jnp.zeros((left, width), buffer.dtype))


def ffn_backward(
    chunk, spots, piece, lengths,
    mine, theirs, bdown, normed, gain, shift, fgain, cot_mine, cot_theirs,
    hidden, act, slope, wup, wdown,
    part_out, gf_out, small_out, buffer_out, low_scratch, gu_scratch, cot_scratch,
):
    length = lengths[lax.axis_index("dp")]
    rows, width = normed.shape
    units = act.shape[1]
    assemble(cot_mine, cot_theirs, spots, 0, piece, cot_scratch)
    sums = [jnp.zeros((1, width), WIDE) for _ in range(3)]
    for i in range(rows // BLOCK):
        here = slice(i * BLOCK, (i + 1) * BLOCK)
        n2, r2 = second_norm(here, mine, theirs, bdown, normed, gain, shift)
        row_ok = i * BLOCK + lax.broadcasted_iota(jnp.int32, (BLOCK, 1), 0) < length
        gy = jnp.where(row_ok, cot_scratch[here, :].astype(WIDE), 0.0)
        gf = norm_back(gy * wide_row(fgain), n2, r2)
        gf_out[here, :] = gf
        low = gf.astype(LOW)
        low_scratch[here, :] = low
        sums[0] += jnp.sum(low.astype(WIDE), axis=0, keepdims=True)
        sums[1] += jnp.sum(gy * n2, axis=0, keepdims=True)
        sums[2] += jnp.sum(gy, axis=0, keepdims=True)
    send(gf_out)
    gu_sum = jnp.zeros((1, units), WIDE)
    for i in range(rows // BLOCK):
        here = slice(i * BLOCK, (i + 1) * BLOCK)
        gu = (mm(low_scratch[here, :], wdown[...], NT) * slope[here, :].astype(WIDE)).astype(LOW)
        gu_scratch[here, :] = gu
        gu_sum += jnp.sum(gu.astype(WIDE), axis=0, keepdims=True)
        part_out[here, :] = mm(gu, wup[...], NT).astype(LOW)
    send(part_out)
    small_out[...] = jnp.zeros(small_out.shape, WIDE)
    for k in range(units // width):
        small_out[k : k + 1, :] = gu_sum[:, k * width : (k + 1) * width]
    for k in range(3):
        small_out[units // width + k : units // width + k + 1, :] = sums[k]
    put(buffer_out, chunk, units, mm(act[...], low_scratch[...], TN).astype(LOW))
    for k in range(units // width):
        columns = slice(k * width, (k + 1) * width)
        put(
            buffer_out, chunk, k * width,
            mm(hidden[...], gu_scratch[:, columns], TN).astype(LOW),
        )
    put_zeros(buffer_out, chunk, 2 * units)


def head_backward(
    h, q, k, v, tab, prob, gctx, anti, g_out, gpq_out, gpk_out,
    gs_scratch, gp_scratch, turned_scratch, moved_scratch,
):
    rows = q.shape[1]
    span = tab.shape[3]
    window = rows + BLOCK
    scale = 1.0 / math.sqrt(3.0 * HEAD_DIM)
    blocks = [slice(i * BLOCK, (i + 1) * BLOCK) for i in range(rows // BLOCK)]
    pad = jnp.zeros((BLOCK, BLOCK), WIDE)
    for here in blocks:
        weights = prob[h, here, :].astype(WIDE)
        gprob = mm(gctx[h, here, :], v[h], NT)
        dots = jnp.sum(weights * gprob, axis=1, keepdims=True)
        gs_scratch[here, :] = (weights * (gprob - dots)).astype(LOW)
    g_out[2, h] = mm(prob[h], gctx[h], TN).astype(LOW)
    for slot, (source, other) in enumerate(((q, k), (k, q))):
        for here in blocks:
            if slot == 0:
                turned = mm(anti, gs_scratch[here, :])
            else:
                turned = mm(anti, gs_scratch[:, here], NT)
            turned_scratch[slot, here, :] = turned.astype(LOW)
            moved_scratch[slot, here, :] = pltpu.roll(
                jnp.concatenate([turned, pad], axis=1), 1, 1, stride=1, stride_axis=0
            ).astype(LOW)
    gp_scratch[...] = jnp.zeros((2, HEAD_DIM, span), WIDE)
    for slot, (source, other) in enumerate(((q, k), (k, q))):
        for here in blocks:
            w0 = rows - BLOCK - here.start
            moved = moved_scratch[slot, here, :]
            table_here = tab[1 - slot, h, :, w0 : w0 + window]
            grad = (mm(turned_scratch[slot, here, :], other[h]) + mm(moved, table_here, NT)) * scale
            g_out[slot, h, here, :] = mm(anti, grad.astype(LOW)).astype(LOW)
            turned = mm(anti, source[h, here, :]).astype(LOW)
            gp_scratch[1 - slot, :, w0 : w0 + window] += mm(turned, moved, TN)
    gpq_out[h] = gp_scratch[0].astype(LOW)
    gpk_out[h] = gp_scratch[1].astype(LOW)


def attention_backward(
    wout, mine, theirs, gf, normed, inverse, gain, ctx, ctx_last, q, k, v, tab, prob,
    gp_out, wout_out, small_out, gctx_out, g_out, gpq_out, gpk_out,
    gpb_scratch, gctx_scratch, *scratch,
):
    first, rows, _ = ctx.shape
    heads = first + 1
    width = gp_out.shape[1]
    blocks = rows // BLOCK
    sums = [jnp.zeros((1, width), WIDE) for _ in range(3)]
    for i in range(blocks):
        here = slice(i * BLOCK, (i + 1) * BLOCK)
        gh = gf[here, :] + (mine[here, :].astype(WIDE) + theirs[here, :].astype(WIDE))
        n1 = normed[here, :]
        gp = norm_back(gh * wide_row(gain), n1, inverse[here, :])
        gp_out[here, :] = gp
        low = gp.astype(LOW)
        gpb_scratch[here, :] = low
        sums[0] += jnp.sum(low.astype(WIDE), axis=0, keepdims=True)
        sums[1] += jnp.sum(gh * n1, axis=0, keepdims=True)
        sums[2] += jnp.sum(gh, axis=0, keepdims=True)
        grad = mm(low, wout[...], NT).astype(LOW)
        for h in range(heads):
            part = grad[:, h * HEAD_DIM : (h + 1) * HEAD_DIM]
            if h < first:
                gctx_scratch[h, here, :] = part
            else:
                gctx_out[0, here, :] = part
    small_out[...] = jnp.zeros(small_out.shape, WIDE)
    for n in range(3):
        small_out[2 + n : 3 + n, :] = sums[n]
    for h in range(heads):
        wout_out[h * HEAD_DIM : (h + 1) * HEAD_DIM, :] = mm(
            ctx[h] if h < first else ctx_last[0], gpb_scratch[...], TN
        ).astype(LOW)
    send(gp_out, small_out, wout_out, gctx_out)
    anti = anti_diagonal()
    ready(q, k, v, tab, prob)

    def head(h, carry):
        head_backward(
            h, q, k, v, tab, prob, gctx_scratch, anti, g_out, gpq_out, gpk_out, *scratch
        )
        return carry

    lax.fori_loop(0, first, head, 0)


def attention_backward_last(
    hot, wq, wk, wv, gctx, q, k, v, tab, prob, before, gpq_before, gpk_before,
    g_out, gpq_out, gpk_out, sums_out, send_out, keep_out,
    gpq_scratch, gpk_scratch, rel_scratch, *scratch,
):
    side = lax.axis_index("tensor")
    buckets = rel_scratch.shape[0]
    half = buckets // 2
    scale = 1.0 / math.sqrt(3.0 * HEAD_DIM)
    anti = anti_diagonal()
    head_backward(
        0, q, k, v, tab, prob, gctx, anti, g_out, gpq_scratch, gpk_scratch, *scratch
    )
    send(g_out)
    for slot, (first, here, out) in enumerate(
        ((gpq_before, gpq_scratch, gpq_out), (gpk_before, gpk_scratch, gpk_out))
    ):
        parts = [first[h] for h in range(first.shape[0])] + [here[0]]
        value = mm(hot[...], jnp.concatenate(parts, axis=0), NT) * scale
        out[...] = value.astype(LOW)
        sums_out[slot : slot + 1, :] = jnp.sum(value, axis=0, keepdims=True)
    rel_scratch[...] = mm(gpq_out[...], wq[...]) + mm(gpk_out[...], wk[...])
    send(gpq_out, gpk_out, sums_out)
    rows = buckets
    send_out[rows:, :] = rel_scratch[
        pl.ds(pl.multiple_of((1 - side) * half, half), half), :
    ].astype(LOW)
    keep_out[...] = rel_scratch[pl.ds(pl.multiple_of(side * half, half), half), :].astype(LOW)
    send_out[:rows, :] = (
        mm(together(0, before, g_out), wq[...])
        + mm(together(1, before, g_out), wk[...])
        + mm(together(2, before, g_out), wv[...])
    ).astype(LOW)


def together(slot, before, last):
    parts = [before[slot, h] for h in range(before.shape[1])] + [last[slot, 0]]
    return jnp.concatenate(parts, axis=1)


def weight_gradients(
    chunk, x, relative, before, last, gpq, gpk, sums, wout_grad, small_ffn, small_attn, keep, got,
    buffer_out,
):
    part = gpq.shape[1]
    xv = x[...]
    rel = relative[...]
    gq, gk, gv = (together(slot, before, last) for slot in range(3))
    put(
        buffer_out, chunk, 0,
        (mm(gq, xv, TN) + mm(gpq[...], rel, TN)).astype(LOW),
    )
    put(
        buffer_out, chunk, part,
        (mm(gk, xv, TN) + mm(gpk[...], rel, TN)).astype(LOW),
    )
    put(buffer_out, chunk, 2 * part, mm(gv, xv, TN).astype(LOW))
    put(buffer_out, chunk, 3 * part, wout_grad[...])
    half = keep.shape[0]
    both = (keep[...].astype(WIDE) + got[got.shape[0] - half :, :].astype(WIDE)).astype(LOW)
    put(buffer_out, chunk, 4 * part, both)
    count = 4 * part + keep.shape[0]
    bias = [
        jnp.sum(gq.astype(WIDE), axis=0, keepdims=True) + sums[0:1, :],
        jnp.sum(gk.astype(WIDE), axis=0, keepdims=True) + sums[1:2, :],
        jnp.sum(gv.astype(WIDE), axis=0, keepdims=True),
    ]
    second = jnp.concatenate([bias[2], jnp.zeros_like(bias[2])], axis=1)
    small = jnp.concatenate(
        [small_ffn[...], jnp.concatenate(bias[:2], axis=1), second, small_attn[2:, :]], axis=0
    ).astype(LOW)
    put(buffer_out, chunk, count, small)
    put_zeros(buffer_out, chunk, count + small.shape[0])


def finish_tokens(gp, mine, theirs, grad_out):
    for i in range(gp.shape[0] // BLOCK):
        here = slice(i * BLOCK, (i + 1) * BLOCK)
        both = mine[here, :].astype(WIDE) + theirs[here, :].astype(WIDE)
        grad_out[here, :] = (gp[here, :] + both).astype(LOW)


def chunks(gathered, first, count):
    for place, offset, start, take in pieces(first, count, gathered.shape[1]):
        yield start, take, gathered[place, offset : offset + take, :].astype(WIDE)


def unpack_ffn(gathered, wup_out, wdown_out):
    width, units = wup_out.shape
    for start, take, value in chunks(gathered, units, units):
        wdown_out[start : start + take, :] = value
    send(wdown_out)
    for k in range(units // width):
        for start, take, value in chunks(gathered, k * width, width):
            wup_out[start : start + take, k * width : (k + 1) * width] = value


def unpack_relative(first, gathered, rel_out):
    for start, take, value in chunks(gathered, first, rel_out.shape[0]):
        rel_out[start : start + take, :] = value.astype(LOW)


def unpack_attention(
    first, gathered, wq_out, wk_out, wv_out, wout_out, bup_out,
    bq_out, bk_out, bv_out, bout_out, again_out, ashift_out, bdown_out, fgain_out, fshift_out,
):
    part, width = wq_out.shape
    units = bup_out.shape[0]
    for k, out in enumerate((wq_out, wk_out, wv_out, wout_out)):
        for start, take, value in chunks(gathered, k * part, part):
            out[start : start + take, :] = value
        send(out)
    small = jnp.concatenate([value for _, _, value in chunks(gathered, first, 16)], axis=0)
    ups = units // width
    for k in range(ups):
        bup_out[k * width : (k + 1) * width] = small[k]
    bdown_out[...] = small[ups]
    fgain_out[...] = small[ups + 1]
    fshift_out[...] = small[ups + 2]
    bq_out[...] = small[8, :part]
    bk_out[...] = small[8, part:]
    bv_out[...] = small[9, :part]
    bout_out[...] = small[10]
    again_out[...] = small[11]
    ashift_out[...] = small[12]


def join_relative(mine, theirs, out):
    side = lax.axis_index("tensor")
    half = mine.shape[0]
    out[pl.ds(pl.multiple_of(side * half, half), half), :] = mine[...].astype(WIDE)
    out[pl.ds(pl.multiple_of((1 - side) * half, half), half), :] = theirs[...].astype(WIDE)


def with_statics(body, *statics):
    def wrapped(*refs):
        body(*statics, *refs)

    wrapped.__name__ = body.__name__
    return wrapped


def swap(array):
    return lax.ppermute(array, "tensor", [(0, 1), (1, 0)])


def exchange(array):
    return lax.all_to_all(array, "dp", split_axis=0, concat_axis=0, tiled=True)


def trade(arrays, groups):
    got = []
    for k, array in enumerate(arrays, 1):
        pairs = [(group[p], group[p ^ k]) for group in groups for p in range(len(group))]
        got.append(lax.ppermute(array, "dp", pairs))
    return got


def after(value, *others):
    return lax.optimization_barrier((value,) + others)[0]


class Sequence:
    def __init__(self):
        self.last = None

    def run(self, body, outs, args, scratch=(), smem=0, flops=1):
        args = list(args)
        if self.last is not None:
            free = [i for i in range(smem, len(args)) if not isinstance(args[i], (Here, Stack))]
            if free:
                arg = args[free[0]]
                if isinstance(arg, Part):
                    args[free[0]] = Part(after(arg.array, self.last), arg.axis, arg.start, arg.count)
                else:
                    args[free[0]] = after(arg, self.last)
            elif isinstance(args[smem], Stack):
                first = args[smem].arrays
                args[smem] = Stack((after(first[0], self.last),) + first[1:])
            else:
                args[smem] = Here(after(args[smem].what[0], self.last))
        got = call(body, outs, args, scratch, smem, flops)
        self.last = got[0][0] if isinstance(got[0], list) else got[0]
        return got


def on_device(
    tokens, lengths, dealing, bucket_table, relative,
    w_query, b_query, w_key, b_key, w_value, b_value, w_out, b_out,
    attn_gain, attn_shift, w_up, b_up, w_down, b_down, ffn_gain, ffn_shift, cotangent,
):
    _, rows, width = tokens.shape
    total = dealing.shape[0]
    part = w_query.shape[1]
    heads = part // HEAD_DIM
    before = heads - 1
    units = w_up.shape[1]
    half = rows // 2
    span = 2 * rows
    piece = max(16, half // total)
    spots = half // piece
    side = lax.axis_index("tensor")
    inner = 1 << ((total.bit_length()) // 2)
    outer = total // inner
    near_groups = [[o * inner + i for i in range(inner)] for o in range(outer)]
    chunk_one = chunk_rows(2 * units, inner, 16)
    chunk_two = chunk_rows(4 * part + half + 16, inner, 16)

    sequence = Sequence()
    run = sequence.run

    def cut(array):
        mine = lax.dynamic_slice_in_dim(array[0], side * half, half, 0)
        return mine.reshape(spots, piece, width)

    moving = jnp.concatenate([cut(cotangent), cut(tokens)], axis=1)
    if spots < total:
        moving = jnp.pad(moving, ((0, total - spots), (0, 0), (0, 0)))
    arrived = exchange(moving)
    x = tokens[0]
    table = jnp.pad(bucket_table, (0, span - bucket_table.shape[0]), constant_values=-1)
    table = table.reshape(span // BLOCK, BLOCK)
    projections = (w_query.T, b_query, w_key.T, b_key, w_value.T, b_value, w_out)
    head_shape = (heads, rows, HEAD_DIM)
    q, k, v, tab, hot, prob, ctx = run(
        attention_first,
        [(head_shape, LOW)] * 3
        + [((2, heads, HEAD_DIM, span), LOW), ((relative.shape[0], span), LOW), ((before, rows, rows), LOW),
           ((before, rows, HEAD_DIM), LOW)],
        (lengths, x, relative, table) + projections[:6],
        scratch=[pltpu.VMEM((rows, rows), WIDE)],
        smem=1,
    )
    arrived = after(arrived, sequence.last)
    (turned,) = call_here(
        with_statics(permute_body, piece), [(arrived.shape, LOW)], (dealing, arrived), smem=1
    )
    sequence.last = turned
    dealt_mine = exchange(turned)
    dealt_theirs = swap(dealt_mine)
    prob_last, ctx_last, attn_part = run(
        attention_rest,
        [((1, rows, rows), LOW), ((1, rows, HEAD_DIM), LOW), Here((rows, width), LOW)],
        (lengths,)
        + tuple(Part(array, 0, before, 1) for array in (q, k, v))
        + (Part(tab, 1, before, 1), w_out, ctx),
        scratch=[pltpu.VMEM((rows, rows), WIDE)],
        smem=1,
    )
    attn_got = swap(attn_part)
    ffn_weights = (b_out, attn_gain, attn_shift, w_up, b_up, w_down)
    normed, down_part, inverse, hidden, act, slope = run(
        with_statics(ffn_forward, True),
        [((rows, width), WIDE), Here((rows, width), LOW), ((rows, 1), WIDE), ((rows, width), LOW),
         ((rows, units), LOW), ((rows, units), LOW)],
        (x, Here(attn_part), Here(attn_got)) + ffn_weights,
        scratch=[pltpu.VMEM((rows, width), LOW), pltpu.VMEM((rows, units), LOW)],
    )
    down_got = swap(down_part)
    hidden_part, gf, small_ffn, near_one = run(
        with_statics(ffn_backward, chunk_one, spots, piece),
        [Here((rows, width), LOW), ((rows, width), WIDE), ((8, width), WIDE),
         Pieces(inner, (chunk_one, width), LOW)],
        (lengths, Here(down_part), Here(down_got), b_down, normed, attn_gain, attn_shift,
         ffn_gain, Here(dealt_mine), Here(dealt_theirs), hidden, act, slope, w_up, w_down),
        scratch=[
            pltpu.VMEM((rows, width), LOW),
            pltpu.VMEM((rows, units), LOW),
            pltpu.VMEM((rows, width), LOW),
        ],
        smem=1,
    )
    hidden_got = swap(hidden_part)
    near_one[1:] = trade(near_one[1:], near_groups)

    def total_of(own, got):
        acc = after(own, sequence.last).astype(WIDE)
        for other in got:
            acc += other.astype(WIDE)
        sequence.last = acc.astype(LOW)
        return sequence.last

    def far_step(array, step):
        reach = inner << step
        return lax.ppermute(array, "dp", [(p, p ^ reach) for p in range(total)])

    steps = outer.bit_length() - 1

    def gather_near(line):
        return Stack([line] + trade([line] * (inner - 1), near_groups))

    head_scratch = [
        pltpu.VMEM((rows, rows), LOW),
        pltpu.VMEM((2, HEAD_DIM, span), WIDE),
        pltpu.VMEM((2, rows, rows), LOW),
        pltpu.VMEM((2, rows, rows + BLOCK), LOW),
    ]
    gp, wout_grad, small_attn, gctx, g_before, gpq_before, gpk_before = run(
        attention_backward,
        [((rows, width), WIDE), ((part, width), LOW), ((8, width), WIDE),
         ((1, rows, HEAD_DIM), LOW), ((3, before, rows, HEAD_DIM), LOW),
         ((before, HEAD_DIM, span), LOW), ((before, HEAD_DIM, span), LOW)],
        (w_out, Here(hidden_part), Here(hidden_got), gf, normed, inverse, attn_gain, ctx, ctx_last)
        + tuple(Part(array, 0, 0, before) for array in (q, k, v))
        + (Part(tab, 1, 0, before), prob),
        scratch=[
            pltpu.VMEM((rows, width), LOW),
            pltpu.VMEM((before, rows, HEAD_DIM), LOW),
        ]
        + head_scratch,
    )
    line_one = total_of(near_one[0], near_one[1:])
    got_one = far_step(line_one, 0)
    g_last, gpq, gpk, sums, send_part, rel_keep = run(
        attention_backward_last,
        [((3, 1, rows, HEAD_DIM), LOW), ((rows, part), LOW), ((rows, part), LOW),
         ((2, part), WIDE),
         ((rows + half, width), LOW), ((half, width), LOW)],
        (hot, w_query.T, w_key.T, w_value.T, gctx)
        + tuple(Part(array, 0, before, 1) for array in (q, k, v))
        + (Part(tab, 1, before, 1), prob_last, g_before, gpq_before, gpk_before),
        scratch=[
            pltpu.VMEM((1, HEAD_DIM, span), LOW),
            pltpu.VMEM((1, HEAD_DIM, span), LOW),
            pltpu.VMEM((rows, width), WIDE),
        ]
        + head_scratch,
    )
    for step in range(1, steps):
        line_one = total_of(line_one, [got_one])
        got_one = far_step(line_one, step)
    send_got = swap(after(send_part, line_one))
    (near_two,) = run(
        with_statics(weight_gradients, chunk_two),
        [Pieces(inner, (chunk_two, width), LOW)],
        (x, relative, g_before, g_last, gpq, gpk, sums, wout_grad, small_ffn, small_attn, rel_keep,
         Here(send_got)),
    )
    near_two[1:] = trade(near_two[1:], near_groups)

    x_dealt, attn_dealt = run(
        with_statics(attention_dealt, spots, piece),
        [((rows, width), LOW), Here((rows, width), LOW)],
        (lengths, dealing, dealt_mine, dealt_theirs, tab) + projections,
        scratch=[pltpu.VMEM(head_shape, LOW) for _ in range(4)] + [pltpu.VMEM((rows, rows), WIDE)],
        smem=2,
    )
    line_one, *near_two[1:] = lax.optimization_barrier((line_one, *near_two[1:]))
    line_one = total_of(line_one, [got_one])
    line_two = total_of(near_two[0], near_two[1:])
    got_two = far_step(line_two, 0)
    all_one = gather_near(line_one)
    attn_dealt_got = swap(after(attn_dealt, line_two))
    normed_dealt, down_dealt = run(
        with_statics(ffn_forward, False),
        [((rows, width), WIDE), Here((rows, width), LOW)],
        (x_dealt, Here(attn_dealt), Here(attn_dealt_got)) + ffn_weights,
        scratch=[pltpu.VMEM((rows, width), LOW), pltpu.VMEM((rows, units), LOW)],
    )
    for step in range(1, steps):
        line_two = total_of(line_two, [got_two])
        got_two = far_step(line_two, step)
    down_dealt_got = swap(after(down_dealt, line_two))
    (grad_tokens,) = run(
        finish_tokens,
        [((rows, width), LOW)],
        (gp, Part(send_part, 0, 0, rows), Part(send_got, 0, 0, rows)),
        flops=6 * 10**9,
    )
    (y,) = run(
        finish_dealt,
        [((rows, width), LOW)],
        (Here(down_dealt), Here(down_dealt_got), b_down, normed_dealt, attn_gain, attn_shift,
         ffn_gain, ffn_shift),
        flops=6 * 10**9,
    )
    g_up, g_down = run(
        unpack_ffn, [((width, units), WIDE), ((units, width), WIDE)], (all_one,),
        flops=6 * 10**9,
    )
    line_two = total_of(line_two, [got_two])
    all_two = gather_near(line_two)
    first = 4 * part
    (rel_half,) = run(with_statics(unpack_relative, first), [Here((half, width), LOW)], (all_two,))
    rel_other = swap(rel_half)
    g_wq, g_wk, g_wv, g_wout, g_bup, g_bq, g_bk, g_bv, g_bout, g_again, g_ashift, g_bdown, g_fgain, g_fshift = run(
        with_statics(unpack_attention, first + half),
        [((part, width), WIDE)] * 4
        + [((units,), WIDE)]
        + [((part,), WIDE)] * 3
        + [((width,), WIDE)] * 6,
        (all_two,),
    )
    (g_rel,) = run(join_relative, [((rows, width), WIDE)], (Here(rel_half), Here(rel_other)))
    return (
        y[None], grad_tokens[None], g_rel, g_wq.T, g_bq, g_wk.T, g_bk, g_wv.T, g_bv, g_wout,
        g_bout, g_again, g_ashift, g_up, g_bup, g_down, g_bdown, g_fgain, g_fshift,
    )


def solution(mesh):
    return jax.shard_map(
        on_device,
        mesh=mesh,
        in_specs=(
            P("dp", None, None), P(), P(), P(), P(),
            P(None, "tensor"), P("tensor"), P(None, "tensor"), P("tensor"),
            P(None, "tensor"), P("tensor"), P("tensor", None), P(), P(), P(),
            P(None, "tensor"), P("tensor"), P("tensor", None), P(), P(), P(),
            P("dp", None, None),
        ),
        out_specs=(
            P("dp", None, None), P("dp", None, None), P(),
            P(None, "tensor"), P("tensor"), P(None, "tensor"), P("tensor"),
            P(None, "tensor"), P("tensor"), P("tensor", None), P(), P(), P(),
            P(None, "tensor"), P("tensor"), P("tensor", None), P(), P(), P(),
        ),
        check_vma=False,
    )
```
